128 devices in a mesh: sub: 32 (over y, z, core), rep: 4 (over x).
Axes of the slice: x: 4, y: 4, z: 4, core: 2. Of those that a mesh axis runs over, the one named last changes fastest.
Arguments:
- regions: bfloat16 [512, 512, 256], P('rep', 'sub'), may hold values from -6 to 6
- leaf_map: int32 [512], P('sub'), may hold values from 0 to 15, as said below
- leaf_bond_weight: bfloat16 [128, 4, 256, 1024], P(('sub', 'rep')), may hold values from -0.375 to 0.375
- mid_weight: bfloat16 [32, 4, 1024, 1024], P('sub', 'rep'), may hold values from -0.1875 to 0.1875
- upper_weight: bfloat16 [32, 1024, 2, 1024], P('sub'), may hold values from -0.1875 to 0.1875
- head_cotangent: float32 [512, 1024], P('rep', 'sub'), may hold values from -0.75 to 0.75
Outputs:
- leaf_grad: bfloat16 [128, 4, 256, 1024], P(('sub', 'rep'))
- middle_weight_gradient: bfloat16 [32, 4, 1024, 1024], P('sub', 'rep')
- upper_grad: bfloat16 [32, 1024, 2, 1024], P('sub', 'rep')
The draws below stay inside these ranges and needn't reach their ends.
Inputs may be any that keep to these rules, and one draw needn't show every extreme that they name: `leaf_map`: each aligned block of 16 entries is a permutation of 0 .. 15.
All inputs are finite; a program needn't handle non-finite values.
Results may differ from the reference program's by a relative error of at most 0.04.
Values may be sent and summed in bfloat16 or wider, within the bound.
A program may use at most 128 MiB of HBM per device.

```python
import jax
import jax.numpy as jnp
from jax import lax

D = 1024
F = 256
REG_DEV = 16
BATCH = 512
REGIONS = 512
LEAF_NODES = 128
LEVELS = 5
N_SUB = 32


def draw_leaf_map(key, part):
    streams = jax.random.split(key, N_SUB)
    shuffles = jax.vmap(lambda stream: jax.random.permutation(stream, REG_DEV))(streams)
    return shuffles.reshape(N_SUB * REG_DEV).astype(jnp.int32)


def steps_of(rng, shape, pieces, least, largest):
    def one(dim, shards_of):
        steps = jax.random.uniform(jax.random.fold_in(jax.random.fold_in(rng, 6), dim), (shards_of,), jnp.float32, least / len(pieces), largest / len(pieces))
        return jnp.repeat(jnp.exp(steps), shape[dim] // shards_of).reshape((-1,) + (1,) * (len(shape) - dim - 1))

    level = one(*pieces[0])
    for cut in pieces[1:]:
        level = level * one(*cut)
    return level


def normal_values(stream_key, extent, deviation, bound, pieces=(), kind=jnp.bfloat16):
    values = jax.random.normal(stream_key, extent, jnp.float32) * deviation
    if len(pieces) > 0:
        values = steps_of(stream_key, extent, pieces, -0.22, 0.18) * values
    return jnp.clip(values, min=-bound, max=bound).astype(kind)


def setup_inputs(seed: int = 0) -> dict:
    splits = jax.random.split(jax.random.key(seed), 7)
    return {
        "regions": normal_values(splits[0], (BATCH, REGIONS, F), 1.0, 6.0, ((0, 4), (1, 32))),
        "leaf_map": draw_leaf_map(jax.random.fold_in(splits[6], 71), 0),
        "leaf_bond_weight": normal_values(splits[2], (LEAF_NODES, 4, F, D), F ** -0.5, 0.375, ((0, 128),)),
        "mid_weight": normal_values(splits[3], (N_SUB, 4, D, D), D ** -0.5, 0.1875, ((0, 32), (1, 4))),
        "upper_weight": normal_values(splits[4], (N_SUB, D, 2, D), D ** -0.5, 0.1875, ((0, 32),)),
        "head_cotangent": normal_values(splits[5], (BATCH, D), 0.05, 0.75, ((0, 4), (1, 32)), jnp.float32),
    }


EPSILON = 1e-06

def widen(array):
    return array.astype(jnp.float32)

def tensor_contraction(formula, left_arr, right_arr):
    return jnp.einsum(formula, widen(left_arr), widen(right_arr), precision=lax.Precision.HIGHEST)

def rms_factor(values):
    return lax.rsqrt(lax.optimization_barrier(jnp.mean(values * values, axis=-1, keepdims=True)) + EPSILON)

def norm_back(gradient, normed, factor):
    return factor * (gradient - normed * lax.optimization_barrier(jnp.mean(gradient * normed, axis=-1, keepdims=True)))

def product_of(factors):
    running = factors[..., 0, :]
    for position in range(1, factors.shape[-2]):
        running = running * factors[..., position, :]
    return running

def leave_one(factors):
    how_many = factors.shape[-2]
    results = []
    for position in range(how_many):
        remaining = [factors[..., partner_idx, :] for partner_idx in range(how_many) if partner_idx != position]
        running = remaining[0]
        for factor in remaining[1:]:
            running = running * factor
        results.append(running)
    return jnp.stack(results, axis=-2)

def subtree_parts(region_x, slot_map, leaf_w, middle_weight):
    batch_rows = region_x.shape[0]
    placed = jnp.take(region_x, slot_map, axis=1).reshape(batch_rows, 4, 4, F)
    leaf_terms = tensor_contraction('bnkf,nkfd->bnkd', placed, leaf_w)
    leaf_prod = product_of(1.0 + leaf_terms)
    leaf_scale = rms_factor(leaf_prod)
    leaf_norm = leaf_prod * leaf_scale
    leaf_message_rows = leaf_norm.astype(jnp.bfloat16)
    middle_node_terms = tensor_contraction('zpc,pci->zpi', leaf_message_rows, middle_weight).astype(jnp.bfloat16)
    mid_factors = 1.0 + widen(middle_node_terms)
    mid_prod = product_of(mid_factors)
    mid_scale = rms_factor(mid_prod)
    mid_norm = mid_prod * mid_scale
    sub_msg = mid_norm.astype(jnp.bfloat16)
    return (placed, leaf_terms, leaf_scale, leaf_norm, leaf_message_rows, mid_factors, mid_scale, mid_norm, sub_msg)

def subtree_grads(region_x, slot_map, leaf_w, middle_weight, sub_grad_in):
    placed, leaf_terms, leaf_scale, leaf_norm, leaf_message_rows, mid_factors, mid_scale, mid_norm, sub_msg = subtree_parts(region_x, slot_map, leaf_w, middle_weight)
    mid_back = norm_back(sub_grad_in, mid_norm, mid_scale)
    middle_gradient_list = (mid_back[:, None, :] * leave_one(mid_factors)).astype(jnp.bfloat16)
    middle_weight_gradient = tensor_contraction('sax,sav->axv', leaf_message_rows, middle_gradient_list).astype(jnp.bfloat16)
    leaf_backward_pass = tensor_contraction('xym,yam->xya', middle_gradient_list, middle_weight)
    node_back = norm_back(leaf_backward_pass, leaf_norm, leaf_scale)
    leaf_weight_gradients = (node_back[:, :, None, :] * leave_one(1.0 + leaf_terms)).astype(jnp.bfloat16)
    leaf_grad = tensor_contraction('bnkf,bnkd->nkfd', placed, leaf_weight_gradients).astype(jnp.bfloat16)
    return (leaf_grad, middle_weight_gradient)

def reference(regions, leaf_map, leaf_bond_weight, mid_weight, upper_weight, head_cotangent):
    batch_rows = regions.shape[0]
    region_sets = jnp.transpose(regions.reshape(batch_rows, N_SUB, REG_DEV, F), (1, 0, 2, 3))
    slot_maps = leaf_map.reshape(N_SUB, REG_DEV).astype(jnp.int32)
    leaf_sets = leaf_bond_weight.reshape(N_SUB, 4, 4, F, D)
    messages = lax.map(lambda packed: subtree_parts(*packed)[-1], (region_sets, slot_maps, leaf_sets, mid_weight))
    records = []
    for tier_level in range(LEVELS):
        group_size = 2 ** (tier_level + 1)
        block_width = D // group_size
        first_col = D - 2 * block_width
        groups = N_SUB // group_size
        block = upper_weight[:, :, :, first_col:first_col + block_width].reshape(groups, group_size, D, 2, block_width)
        weights = jnp.transpose(block, (0, 2, 3, 1, 4)).reshape(groups, D, 2, D)
        left_msg = messages[0::2]
        right_msg = messages[1::2]
        up_left = tensor_contraction('gbi,gio->gbo', left_msg, weights[:, :, 0, :])
        up_right = tensor_contraction('gbi,gio->gbo', right_msg, weights[:, :, 1, :])
        joined = (1.0 + up_left) * (1.0 + up_right)
        scaling = rms_factor(joined)
        messages = (joined * scaling).astype(jnp.bfloat16)
        records.append((group_size, block_width, groups, weights, left_msg, right_msg, up_left, up_right, scaling))
    root_msg = messages[0]
    head_width = D // N_SUB
    head_maps = jnp.transpose(upper_weight[:, :, :, D - head_width:], (1, 2, 0, 3)).reshape(D, 2, D)
    head_left = head_maps[:, 0, :]
    head_right = head_maps[:, 1, :]
    head_value = tensor_contraction('bi,io->bo', root_msg, head_left)
    head_gate = tensor_contraction('bi,io->bo', root_msg, head_right)
    gating = jax.nn.sigmoid(head_gate)
    grad_value = (head_cotangent * gating).astype(jnp.bfloat16)
    grad_gate = (head_cotangent * head_value * gating * (1.0 - gating)).astype(jnp.bfloat16)
    root_grad_msg = tensor_contraction('bo,io->bi', grad_value, head_left) + tensor_contraction('bo,io->bi', grad_gate, head_right)
    head_full = jnp.stack([tensor_contraction('bi,bo->io', root_msg, grad_value), tensor_contraction('bi,bo->io', root_msg, grad_gate)], axis=1)
    head_piece = jnp.transpose(head_full.reshape(D, 2, N_SUB, head_width), (2, 0, 1, 3))
    level_pieces = [None] * LEVELS
    grad_msgs = root_grad_msg[None]
    for tier_level in reversed(range(LEVELS)):
        group_size, block_width, groups, weights, left_msg, right_msg, up_left, up_right, scaling = records[tier_level]
        normed = (1.0 + up_left) * (1.0 + up_right) * scaling
        joined_grad = norm_back(grad_msgs, normed, scaling)
        grad_left = (joined_grad * (1.0 + up_right)).astype(jnp.bfloat16)
        grad_right = (joined_grad * (1.0 + up_left)).astype(jnp.bfloat16)
        node_grad = jnp.stack([tensor_contraction('gbi,gbo->gio', left_msg, grad_left), tensor_contraction('gbi,gbo->gio', right_msg, grad_right)], axis=2)
        node_piece = jnp.transpose(node_grad.reshape(groups, D, 2, group_size, block_width), (0, 3, 1, 2, 4)).reshape(N_SUB, D, 2, block_width)
        level_pieces[tier_level] = node_piece
        to_left = tensor_contraction('gbo,gio->gbi', grad_left, weights[:, :, 0, :])
        to_right = tensor_contraction('gbo,gio->gbi', grad_right, weights[:, :, 1, :])
        grad_msgs = jnp.stack([to_left, to_right], axis=1).reshape(2 * groups, batch_rows, D)
    upper_sum = jnp.concatenate(level_pieces + [head_piece], axis=-1)
    leaf_weight_gradients, middle_gradient_list = lax.map(lambda packed: subtree_grads(*packed), (region_sets, slot_maps, leaf_sets, mid_weight, grad_msgs))
    leaf_grad = leaf_weight_gradients.reshape(N_SUB * 4, 4, F, D)
    return (leaf_grad, middle_gradient_list, upper_sum.astype(jnp.bfloat16))
```

```python
import jax
import jax.numpy as jnp
from jax import lax
from jax.experimental import pallas as pl
from jax.experimental.pallas import tpu as pltpu
from jax.sharding import PartitionSpec as P

F32 = jnp.float32
BF = jnp.bfloat16
MESH = pl.DeviceIdType.MESH
EPSILON = 1e-06
D = 1024
F = 256
B = 128
REPS = 4
SUBS = 32
LEVELS = 5
ALL = REPS * B
WIDTH = [D // 2 ** (j + 1) for j in range(LEVELS)] + [D // SUBS]
COLUMN = [D - 2 * WIDTH[j] for j in range(LEVELS)] + [D - D // SUBS]
CHUNK = [2 * WIDTH[j] for j in range(LEVELS)] + [WIDTH[5]]
GROUP = [2 ** (j + 1) for j in range(LEVELS)] + [SUBS]


def nn(a, b):
    return jnp.dot(a, b, preferred_element_type=F32)


def nt(a, b):
    return lax.dot_general(a, b, (((1,), (1,)), ((), ())), preferred_element_type=F32)


def fold(values):
    return jnp.sum(values.reshape(values.shape[0] // 8, 8, values.shape[1]), axis=0)


def column_sum(values):
    return jnp.sum(values, axis=0, keepdims=True)


def factor_of(squares):
    return lax.rsqrt(column_sum(squares) * (1.0 / D) + EPSILON)


def at(index, size):
    return pl.ds(pl.multiple_of(index * size, size), size)


def others(f):
    p01 = f[0] * f[1]
    p23 = f[2] * f[3]
    return [f[1] * p23, f[0] * p23, p01 * f[3], p01 * f[2]]


def split_tile(row):
    high = row.astype(BF).astype(F32)
    index = lax.broadcasted_iota(jnp.int32, (16, B), 0)
    tile = jnp.where(index == 0, high, jnp.where(index == 1, row - high, 0.0))
    return tile.astype(BF)


def kernel(
    map_ref, reg_hbm, lw_hbm, mw_hbm, uw_hbm, cot_hbm,
    lg_hbm, mg_hbm, ug_hbm,
    R, Q, XS, XR, LW, LWT, MW, MWT, UW, WN, WT, COT, FK, LP, RL, LM, MS, MR, MP,
    A0, A1, A2, A3, A4, A5, UL, UR, JJ, GP, GB,
    BS0, BS1, BS2, BS3, BS4, BS5, BR0, BR1, BR2, BR3, BR4, BR5,
    GX, AX, CS, CR, LB, CT, XT, OU, OI,
    load_sem, local_sem, x1s, x1r, x2s, x2r, x3s, x3r, fs, fr, bs, br, axs, axr, gxs, gxr, out_sem,
):
    A = [A0, A1, A2, A3, A4, A5]
    BS = [BS0, BS1, BS2, BS3, BS4, BS5]
    BR = [BR0, BR1, BR2, BR3, BR4, BR5]
    s = lax.axis_index("sub")
    p = lax.axis_index("rep")

    def to_rep(src, dst, send, recv, peer):
        pltpu.make_async_remote_copy(
            src_ref=src, dst_ref=dst, send_sem=send, recv_sem=recv,
            device_id={"rep": peer}, device_id_type=MESH,
        ).start()

    def to_sub(src, dst, send, recv, peer):
        pltpu.make_async_remote_copy(
            src_ref=src, dst_ref=dst, send_sem=send, recv_sem=recv,
            device_id={"sub": peer}, device_id_type=MESH,
        ).start()

    def await_bytes(ref, sem):
        pltpu.make_async_copy(ref, ref, sem).wait()

    loads = [
        pltpu.make_async_copy(src, dst, load_sem.at[i])
        for i, (src, dst) in enumerate(
            [(reg_hbm, R), (lw_hbm, LW), (mw_hbm, MW), (uw_hbm, UW), (cot_hbm, COT)]
        )
    ]
    for load in loads:
        load.start()

    barrier = pltpu.get_barrier_semaphore()

    def greet_sub(i, carry):
        pl.semaphore_signal(
            barrier, inc=1, device_id={"sub": lax.rem(s + i, SUBS)}, device_id_type=MESH
        )
        return carry

    def greet_rep(i, carry):
        pl.semaphore_signal(
            barrier, inc=1, device_id={"rep": lax.rem(p + i, REPS)}, device_id_type=MESH
        )
        return carry

    lax.fori_loop(1, SUBS, greet_sub, 0)
    lax.fori_loop(1, REPS, greet_rep, 0)

    column = lax.broadcasted_iota(jnp.int32, (16, 256), 1)
    sample = lax.broadcasted_iota(jnp.int32, (16, 256), 0)
    for l in range(16):
        wanted = sample * 16 + map_ref[l]
        Q[16 * l : 16 * l + 16, :] = jnp.where(column == wanted, 1.0, 0.0).astype(BF)
    loads[0].wait()

    def place(q, carry):
        got = nn(Q[...], R[at(q, 256), :]).astype(BF)
        for l in range(16):
            XS[l // 4, l % 4, at(q, 16), :] = got[16 * l : 16 * l + 16, :]
        return carry

    lax.fori_loop(0, 8, place, 0)
    pl.semaphore_wait(barrier, SUBS - 1 + REPS - 1)

    def send_slots(i, carry):
        peer = lax.rem(p + i, REPS)
        to_rep(XS.at[peer], XR.at[:, at(p, B), :], x1s, x1r.at[p], peer)
        return carry

    lax.fori_loop(1, REPS, send_slots, 0)
    own_slots = pltpu.make_async_copy(XS.at[p], XR.at[:, at(p, B), :], local_sem.at[0])
    own_slots.start()

    GP[...] = jnp.zeros(GP.shape, BF)
    loads[1].wait()

    def turn_leaf(i, carry):
        k, t = i // 4, lax.rem(i, 4)
        LWT[k, at(t, 256), :] = LW[k, :, at(t, 256)].T
        return carry

    lax.fori_loop(0, 16, turn_leaf, 0)
    loads[2].wait()

    def turn_mid(i, carry):
        a, b = i // 4, lax.rem(i, 4)
        MWT[at(b, 256), at(a, 256)] = MW[at(a, 256), at(b, 256)].T
        return carry

    lax.fori_loop(0, 16, turn_mid, 0)

    def source(i):
        return lax.rem(p + i + i // 2 - 2 * (i // 3), REPS)

    def leaf_chunk(i):
        src = source(i)
        lanes = at(src, B)

        def terms(t, squares):
            rows = at(t, 256)
            product = None
            for k in range(4):
                factor = 1.0 + nt(LWT[k, rows, :], XR[k, lanes, :])
                FK[k, rows, lanes] = factor
                product = factor if product is None else product * factor
            LP[rows, lanes] = product
            return squares + fold(product * product)

        r = factor_of(lax.fori_loop(0, 4, terms, jnp.zeros((8, B), F32)))
        RL[:, lanes] = jnp.broadcast_to(r, (8, B))

        def scale(t, carry):
            rows = at(t, 256)
            h = LP[rows, lanes] * r
            LP[rows, lanes] = h
            LM[rows, lanes] = h.astype(BF)
            return carry

        lax.fori_loop(0, 4, scale, 0)

        def mid(t, carry):
            rows = at(t, 256)
            MS[src, rows, :] = nn(MWT[rows, :], LM[:, lanes]).astype(BF)
            return carry

        lax.fori_loop(0, 4, mid, 0)

    def turn_slots(i):
        lanes = at(source(i), B)
        for k in range(4):
            XT[k, :, lanes] = XR[k, lanes, :].T

    own_slots.wait()
    leaf_chunk(0)
    own_mid = pltpu.make_async_copy(MS.at[p], MR.at[p], local_sem.at[1])
    own_mid.start()
    loads[3].wait()

    def turn_upper(t, carry):
        rows = at(t, 128)
        for side in range(2):
            block = UW[rows, side, :]
            WN[side, rows, :] = block
            WT[side, :, rows] = block.T
        return carry

    lax.fori_loop(0, 8, turn_upper, 0)
    turn_slots(0)

    def other_chunk(i, carry):
        src = source(i)
        await_bytes(XR.at[:, at(src, B), :], x1r.at[src])
        leaf_chunk(i)
        to_rep(MS.at[src], MR.at[p], x2s, x2r, src)
        turn_slots(i)
        return carry

    lax.fori_loop(1, REPS, other_chunk, 0)

    own_mid.wait()
    await_bytes(MR.at[0:3], x2r)
    base = lax.rem(s, 2) * D

    def mid_product(t, carry):
        rows = at(t, 128)
        product = 1.0 + MR[0, rows, :].astype(F32)
        for k in range(1, 4):
            product = product * (1.0 + MR[k, rows, :].astype(F32))
        MP[rows, :] = product
        A0[pl.ds(pl.multiple_of(base + t * 128, 128), 128), :] = product.astype(BF)
        return carry

    lax.fori_loop(0, 8, mid_product, 0)

    def spread(level, me, block):
        group = GROUP[level]

        def one(i, carry):
            peer = s - me + lax.rem(me + i, group)
            ref = A[level].at[at(me, block), :]
            to_sub(ref, ref, fs.at[level], fr.at[level], peer)
            return carry

        lax.fori_loop(1, group, one, 0)

    def share_rows(level):
        sides = 2 if level < LEVELS else 1

        def one(i, carry):
            peer = lax.rem(p + i, REPS)
            for side in range(sides):
                rows = pl.ds(pl.multiple_of(side * D + peer * 256, 256), 256)
                to_rep(
                    A[level].at[rows, :], AX.at[level, side, :, at(p, B)],
                    axs.at[level], axr.at[level], peer,
                )
            return carry

        lax.fori_loop(1, REPS, one, 0)
        for side in range(sides):
            rows = pl.ds(pl.multiple_of(side * D + p * 256, 256), 256)
            copy = pltpu.make_async_copy(
                A[level].at[rows, :], AX.at[level, side, :, at(p, B)], local_sem.at[2 + 2 * level + side]
            )
            copy.start()
            kept.append(copy)

    kept = []

    def squares_of(ref, start):
        def one(t, total):
            values = ref[pl.ds(pl.multiple_of(start + t * 256, 256), 256), :].astype(F32)
            return total + fold(values * values)

        return lax.fori_loop(0, 4, one, jnp.zeros((8, B), F32))

    spread(0, lax.rem(s, 2), D)
    scales = []
    for level in range(LEVELS):
        group, w, c = GROUP[level], WIDTH[level], COLUMN[level]
        block = 2 * D // group
        await_bytes(A[level].at[0 : (group - 1) * block], fr.at[level])
        share_rows(level)
        left = factor_of(squares_of(A[level], 0))
        right = factor_of(squares_of(A[level], D))
        scales.append((left, right))
        me = lax.rem(s, GROUP[level + 1])
        size = min(w, 256)
        for t in range(w // size):
            rows = slice(c + t * size, c + (t + 1) * size)
            ul = nn(WT[0, rows, :], A[level][0:D, :]) * left
            ur = nn(WT[1, rows, :], A[level][D : 2 * D, :]) * right
            joined = (1.0 + ul) * (1.0 + ur)
            UL[rows, :] = ul
            UR[rows, :] = ur
            JJ[rows, :] = joined
            A[level + 1][pl.ds(pl.multiple_of(me * w + t * size, size), size), :] = joined.astype(BF)
        spread(level + 1, me, w)

    def share_grads(level):
        w, c = WIDTH[level], COLUMN[level]
        ref = GX.at[:, c : c + w, at(p, B)]

        def one(i, carry):
            to_rep(ref, ref, gxs.at[level], gxr.at[level], lax.rem(p + i, REPS))
            return carry

        lax.fori_loop(1, REPS, one, 0)

    own = at(p, B)

    def scatter(level, me):
        group = GROUP[level]

        def one(i, carry):
            d = lax.rem(me + i, group)
            to_sub(BS[level].at[d], BR[level].at[me], bs.at[level], br.at[level], s - me + d)
            return carry

        lax.fori_loop(1, group, one, 0)
        copy = pltpu.make_async_copy(BS[level].at[me], BR[level].at[me], local_sem.at[14 + level])
        copy.start()
        return copy

    await_bytes(A5.at[0 : 31 * 32], fr.at[5])
    share_rows(5)
    root_scale = factor_of(squares_of(A5, 0))
    w, c = WIDTH[5], COLUMN[5]
    za = nn(WT[0, c:D, :], A5[...]) * root_scale
    zb = nn(WT[1, c:D, :], A5[...]) * root_scale
    sigma = 1.0 / (1.0 + jnp.exp(-zb))
    loads[4].wait()
    cotangent = COT[...].T
    ga = cotangent * sigma
    gb = cotangent * za * sigma * (1.0 - sigma)
    GX[0, c:D, own] = (ga * root_scale).astype(BF)
    GX[1, c:D, own] = (gb * root_scale).astype(BF)
    share_grads(5)
    ga = ga.astype(BF)
    gb = gb.astype(BF)
    GP[2, 0, 96:128, :] = ga
    GP[2, 1, 96:128, :] = gb
    dots = column_sum(ga.astype(F32) * za + gb.astype(F32) * zb)
    BS5[:, 32:48, :] = jnp.broadcast_to(split_tile(dots)[None], (SUBS, 16, B))

    def root_part(t, carry):
        rows = at(t, 256)
        part = nn(WN[0, rows, 896:1024], GP[2, 0]) + nn(WN[1, rows, 896:1024], GP[2, 1])
        BS5[at(t, 8), 0:32, :] = part.astype(BF).reshape(8, 32, B)
        return carry

    lax.fori_loop(0, 4, root_part, 0)
    own_chunk = scatter(5, s)

    def gathered(level, rows):
        group = GROUP[level]
        if group <= 8:
            total = BR[level][0, rows, :].astype(F32)
            for g in range(1, group):
                total = total + BR[level][g, rows, :].astype(F32)
            return total

        def one(i, total):
            for g in range(4):
                total = total + BR[level][4 * i + g, rows, :].astype(F32)
            return total

        size = rows.size if hasattr(rows, "size") else rows.stop - rows.start
        return lax.fori_loop(0, group // 4, one, jnp.zeros((size, B), F32))

    def await_chunks(level, copy):
        copy.wait()
        await_bytes(BR[level].at[0 : GROUP[level] - 1], br.at[level])
        size = CHUNK[level]
        return column_sum(gathered(level, slice(size, size + 16))) * (1.0 / D)

    for level in reversed(range(LEVELS)):
        group, w, c = GROUP[level], WIDTH[level], COLUMN[level]
        mean = await_chunks(level + 1, own_chunk)
        if level == LEVELS - 1:
            r = root_scale
        else:
            side_of = lax.rem(s // GROUP[level], 2)
            r = jnp.where(side_of == 1, scales[level + 1][1], scales[level + 1][0])
        left, right = scales[level]
        size = min(w, 64)

        def node_back(t, carry):
            dl, dr = carry
            rows = pl.ds(pl.multiple_of(c + t * size, size), size)
            total = gathered(level + 1, pl.ds(pl.multiple_of(t * size, size), size))
            ul, ur = UL[rows, :], UR[rows, :]
            v = r * (total - JJ[rows, :] * (r * mean))
            gl = v * (1.0 + ur)
            gr = v * (1.0 + ul)
            GX[0, rows, own] = (gl * left).astype(BF)
            GX[1, rows, own] = (gr * right).astype(BF)
            gl = gl.astype(BF)
            gr = gr.astype(BF)
            if level < 3:
                GB[0, rows, :] = gl
                GB[1, rows, :] = gr
            else:
                GP[level - 3, 0, c - 896 : c - 896 + w, :] = gl
                GP[level - 3, 1, c - 896 : c - 896 + w, :] = gr
            return dl + fold(gl.astype(F32) * ul), dr + fold(gr.astype(F32) * ur)

        zero = jnp.zeros((8, B), F32)
        dl, dr = lax.fori_loop(0, w // size, node_back, (zero, zero))
        half, chunk = group // 2, CHUNK[level]
        for side, dot in ((0, dl), (1, dr)):
            tile = split_tile(column_sum(dot))
            BS[level][side * half : (side + 1) * half, chunk : chunk + 16, :] = jnp.broadcast_to(
                tile[None], (half, 16, B)
            )

        def part(t, carry):
            rows = at(t, 256)
            for side in range(2):
                if level < 3:
                    value = nn(WN[side, rows, c : c + w], GB[side, c : c + w, :])
                else:
                    value = nn(WN[side, rows, 896:1024], GP[level - 3, side])
                value = value.astype(BF)
                if chunk >= 256:
                    per = chunk // 256
                    BS[level][side * half + t // per, at(lax.rem(t, per), 256), :] = value
                else:
                    n = 256 // chunk
                    BS[level][pl.ds(side * half + t * n, n), 0:chunk, :] = value.reshape(n, chunk, B)
            return carry

        lax.fori_loop(0, 4, part, 0)
        own_chunk = scatter(level, lax.rem(s, group))
        share_grads(level)

    mean = await_chunks(0, own_chunk)
    r = jnp.where(lax.rem(s, 2) == 1, scales[0][1], scales[0][0])

    def mid_back(t, carry):
        rows = at(t, 128)
        total = BR0[0, rows, :].astype(F32) + BR0[1, rows, :].astype(F32)
        v = r * (total - MP[rows, :] * (r * mean))
        rest = others([1.0 + MR[k, rows, :].astype(F32) for k in range(4)])
        for k in range(4):
            CS[k, rows, :] = (v * rest[k]).astype(BF)
        return carry

    lax.fori_loop(0, 8, mid_back, 0)

    def send_back(i, carry):
        peer = lax.rem(p + i, REPS)
        to_rep(CS.at[peer], CR.at[:, own], x3s, x3r.at[p], peer)
        return carry

    lax.fori_loop(1, REPS, send_back, 0)
    own_back = pltpu.make_async_copy(CS.at[p], CR.at[:, own], local_sem.at[20])
    own_back.start()

    for copy in kept:
        copy.wait()
    for level in range(LEVELS + 1):
        sides = 2 if level < LEVELS else 1
        for side in range(sides):
            await_bytes(AX.at[level, side, :, 0 : 3 * B], axr.at[level]) if sides == 1 else None
        if sides == 2:
            await_bytes(AX.at[level, :, :, 0 : 3 * B], axr.at[level])

    def await_grads(level):
        w, c = WIDTH[level], COLUMN[level]
        await_bytes(GX.at[:, c : c + w, 0 : 3 * B], gxr.at[level])

    for level in (5, 4, 3):
        await_grads(level)
    lane = lax.broadcasted_iota(jnp.int32, (256, 128), 1)
    for side in range(2):
        grads = GX[side, 896:1024, :]
        g3 = nt(AX[3, side], grads)
        g4 = nt(AX[4, side], grads)
        g5 = nt(AX[5, 0], grads)
        OU[side, :, 896:1024] = jnp.where(lane < 64, g3, jnp.where(lane < 96, g4, g5)).astype(BF)

    def upper_gradient(level):
        await_grads(level)
        w, c = WIDTH[level], COLUMN[level]
        for side in range(2):
            OU[side, :, c : c + w] = nt(AX[level, side], GX[side, c : c + w, :]).astype(BF)

    upper_gradient(2)
    upper_gradient(1)

    def leaf_back(i):
        lanes = at(source(i), B)

        def product(t, total):
            rows = at(t, 256)
            value = nn(MW[rows, :], CR[:, lanes])
            LB[rows, :] = value
            return total + fold(value * LP[rows, lanes])

        mean = column_sum(lax.fori_loop(0, 4, product, jnp.zeros((8, B), F32))) * (1.0 / D)
        r = RL[0:1, lanes]

        def cotangents(t, carry):
            rows = at(t, 128)
            v = r * (LB[rows, :] - LP[rows, lanes] * mean)
            rest = others([FK[k, rows, lanes] for k in range(4)])
            for k in range(4):
                CT[k, rows, lanes] = (v * rest[k]).astype(BF)
            return carry

        lax.fori_loop(0, 8, cotangents, 0)

    own_back.wait()
    leaf_back(0)

    def other_back(i, carry):
        src = source(i)
        await_bytes(CR.at[:, at(src, B)], x3r.at[src])
        leaf_back(i)
        return carry

    lax.fori_loop(1, REPS, other_back, 0)

    def leaf_gradient(k, carry):
        LW[k] = nt(XT[k], CT[k]).astype(BF)
        return carry

    lax.fori_loop(0, 4, leaf_gradient, 0)
    out_leaf = pltpu.make_async_copy(LW, lg_hbm, out_sem.at[0])
    out_leaf.start()

    def mid_gradient(t, carry):
        rows = at(t, 256)
        MWT[rows, :] = nt(LM[rows, :], CR[...]).astype(BF)
        return carry

    lax.fori_loop(0, 4, mid_gradient, 0)
    out_mid = pltpu.make_async_copy(MWT, mg_hbm, out_sem.at[1])
    out_mid.start()

    upper_gradient(0)

    def weave(t, carry):
        rows = at(t, 64)
        for side in range(2):
            OI[rows, side, :] = OU[side, rows, :]
        return carry

    lax.fori_loop(0, 4, weave, 0)
    out_upper = pltpu.make_async_copy(OI, ug_hbm, out_sem.at[2])
    out_upper.start()

    await_bytes(XS.at[0:3], x1s)
    await_bytes(MS.at[0:3], x2s)
    await_bytes(CS.at[0:3], x3s)
    for level in range(LEVELS + 1):
        group = GROUP[level]
        block = A[level].shape[0] // group
        await_bytes(A[level].at[0 : (group - 1) * block], fs.at[level])
        await_bytes(BS[level].at[0 : group - 1], bs.at[level])
        if level < LEVELS:
            await_bytes(AX.at[level, :, :, 0 : 3 * B], axs.at[level])
        else:
            await_bytes(AX.at[level, 0, :, 0 : 3 * B], axs.at[level])
        w, c = WIDTH[level], COLUMN[level]
        await_bytes(GX.at[:, c : c + w, 0 : 3 * B], gxs.at[level])
    out_leaf.wait()
    out_mid.wait()
    out_upper.wait()


def scratch():
    vm = pltpu.VMEM
    dma = pltpu.SemaphoreType.DMA
    chunks = [vm((GROUP[j], CHUNK[j] + 16, B), BF) for j in range(LEVELS + 1)]
    return (
        [
            vm((2048, F), BF), vm((256, 256), BF), vm((4, 4, B, F), BF), vm((4, ALL, F), BF),
            vm((4, F, D), BF), vm((4, D, F), BF), vm((D, D), BF), vm((D, D), BF),
            vm((D, 2, D), BF), vm((2, D, D), BF), vm((2, D, D), BF), vm((B, 32), F32),
            vm((4, D, ALL), F32), vm((D, ALL), F32), vm((8, ALL), F32), vm((D, ALL), BF),
            vm((4, D, B), BF), vm((4, D, B), BF), vm((D, B), F32),
        ]
        + [vm((2 * D, B), BF)] * 5
        + [vm((D, B), BF)]
        + [vm((D, B), F32)] * 3
        + [vm((3, 2, 128, B), BF), vm((2, D, B), BF)]
        + chunks
        + chunks
        + [
            vm((2, D, ALL), BF), vm((6, 2, 256, ALL), BF), vm((4, D, B), BF), vm((D, ALL), BF),
            vm((D, B), F32), vm((4, D, ALL), BF), vm((4, F, ALL), BF), vm((2, 256, D), BF),
            vm((256, 2, D), BF),
        ]
        + [
            dma((5,)), dma((21,)), dma, dma((4,)), dma, dma, dma, dma((4,)),
            dma((6,)), dma((6,)), dma((6,)), dma((6,)), dma((6,)), dma((6,)), dma((6,)), dma((6,)),
            dma((3,)),
        ]
    )


def on_device(regions, leaf_map, leaf_bond_weight, mid_weight, upper_weight, head_cotangent):
    anywhere = pl.BlockSpec(memory_space=pl.ANY)
    outs = pl.pallas_call(
        kernel,
        out_shape=(
            jax.ShapeDtypeStruct((4, F, D), BF),
            jax.ShapeDtypeStruct((D, D), BF),
            jax.ShapeDtypeStruct((256, 2, D), BF),
        ),
        in_specs=[pl.BlockSpec(memory_space=pltpu.SMEM)] + [anywhere] * 5,
        out_specs=(anywhere,) * 3,
        scratch_shapes=scratch(),
        compiler_params=pltpu.CompilerParams(
            collective_id=0, has_side_effects=True, vmem_limit_bytes=67000000
        ),
    )(
        leaf_map, regions.reshape(B * 16, F), leaf_bond_weight[0], mid_weight[0, 0],
        upper_weight[0], head_cotangent,
    )
    return (outs[0][None], outs[1][None, None], outs[2][None])


def solution(mesh):
    placed = (
        P("rep", "sub", None),
        P("sub"),
        P(("sub", "rep"), None, None, None),
        P("sub", "rep", None, None),
        P("sub", None, None, None),
        P("rep", "sub"),
    )
    return jax.shard_map(
        on_device,
        mesh=mesh,
        in_specs=placed,
        out_specs=(
            P(("sub", "rep"), None, None, None),
            P("sub", "rep", None, None),
            P("sub", "rep", None, None),
        ),
        check_vma=False,
    )
```

```python
import jax
import jax.numpy as jnp
from jax import lax
from jax.experimental import pallas as pl
from jax.experimental.pallas import tpu as pltpu
from jax.sharding import PartitionSpec as P

F32 = jnp.float32
BF = jnp.bfloat16
MESH = pl.DeviceIdType.MESH
EPSILON = 1e-06
D = 1024
F = 256
B = 128
REPS = 4
SUBS = 32
LEVELS = 5
ALL = REPS * B
WIDTH = [D // 2 ** (j + 1) for j in range(LEVELS)] + [D // SUBS]
COLUMN = [D - 2 * WIDTH[j] for j in range(LEVELS)] + [D - D // SUBS]
CHUNK = [2 * WIDTH[j] for j in range(LEVELS)] + [WIDTH[5]]
GROUP = [2 ** (j + 1) for j in range(LEVELS)] + [SUBS]


def nn(a, b):
    return jnp.dot(a, b, preferred_element_type=F32)


def nt(a, b):
    return lax.dot_general(a, b, (((1,), (1,)), ((), ())), preferred_element_type=F32)


def fold(values):
    return jnp.sum(values.reshape(values.shape[0] // 8, 8, values.shape[1]), axis=0)


def column_sum(values):
    return jnp.sum(values, axis=0, keepdims=True)


def factor_of(squares):
    return lax.rsqrt(column_sum(squares) * (1.0 / D) + EPSILON)


def at(index, size):
    return pl.ds(pl.multiple_of(index * size, size), size)


def others(f):
    p01 = f[0] * f[1]
    p23 = f[2] * f[3]
    return [f[1] * p23, f[0] * p23, p01 * f[3], p01 * f[2]]


def split_tile(row):
    high = row.astype(BF).astype(F32)
    index = lax.broadcasted_iota(jnp.int32, (16, B), 0)
    tile = jnp.where(index == 0, high, jnp.where(index == 1, row - high, 0.0))
    return tile.astype(BF)


def kernel(
    map_ref, reg_hbm, lw_hbm, mw_hbm, uw_hbm, cot_hbm,
    lg_hbm, mg_hbm, ug_hbm,
    R, Q, XS, XR, LW, LWT, MW, MWT, UW, WN, WT, COT, FK, RL, LM, MS, MR,
    A0, A1, A2, A3, A4, A5, UL, UR, JJ, GP, GB,
    BS1, BS2, BS3, BS4, BS5, BR1, BR2, BR3, BR4, BR5,
    GX, AX, CS, CR, LB, CT, XT, OU, OI, LO, H0, R0, PR, PM,
    load_sem, local_sem, x1s, x1r, x2s, x2r, x3s, x3r, h0s, h0r, fs, fr, ff, fo, bs, br,
    axs, axr, gxs, gxr, gx0, pss, prs, out_sem,
):
    A = [A0, A1, A2, A3, A4, A5]
    BS = [None, BS1, BS2, BS3, BS4, BS5]
    BR = [None, BR1, BR2, BR3, BR4, BR5]
    s = lax.axis_index("sub")
    p = lax.axis_index("rep")

    def to_rep(src, dst, send, recv, peer):
        pltpu.make_async_remote_copy(
            src_ref=src, dst_ref=dst, send_sem=send, recv_sem=recv,
            device_id={"rep": peer}, device_id_type=MESH,
        ).start()

    def to_sub(src, dst, send, recv, peer):
        pltpu.make_async_remote_copy(
            src_ref=src, dst_ref=dst, send_sem=send, recv_sem=recv,
            device_id={"sub": peer}, device_id_type=MESH,
        ).start()

    def await_bytes(ref, sem):
        pltpu.make_async_copy(ref, ref, sem).wait()

    loads = [
        pltpu.make_async_copy(src, dst, load_sem.at[i])
        for i, (src, dst) in enumerate(
            [(reg_hbm, R), (lw_hbm, LW), (mw_hbm, MW), (uw_hbm, UW), (cot_hbm, COT)]
        )
    ]
    for load in loads:
        load.start()

    barrier = pltpu.get_barrier_semaphore()

    def greet_sub(i, carry):
        pl.semaphore_signal(
            barrier, inc=1, device_id={"sub": lax.rem(s + i, SUBS)}, device_id_type=MESH
        )
        return carry

    def greet_rep(i, carry):
        pl.semaphore_signal(
            barrier, inc=1, device_id={"rep": lax.rem(p + i, REPS)}, device_id_type=MESH
        )
        return carry

    lax.fori_loop(1, SUBS, greet_sub, 0)
    lax.fori_loop(1, REPS, greet_rep, 0)

    column = lax.broadcasted_iota(jnp.int32, (16, 256), 1)
    sample = lax.broadcasted_iota(jnp.int32, (16, 256), 0)
    for l in range(16):
        wanted = sample * 16 + map_ref[l]
        Q[16 * l : 16 * l + 16, :] = jnp.where(column == wanted, 1.0, 0.0).astype(BF)
    loads[0].wait()

    def place(q, carry):
        got = nn(Q[...], R[at(q, 256), :]).astype(BF)
        for l in range(16):
            XS[l // 4, l % 4, at(q, 16), :] = got[16 * l : 16 * l + 16, :]
        return carry

    lax.fori_loop(0, 8, place, 0)
    pl.semaphore_wait(barrier, SUBS - 1 + REPS - 1)

    def source(i):
        return lax.rem(p + i + i // 2 - 2 * (i // 3), REPS)

    def send_slots(i, carry):
        peer = source(i)
        to_rep(XS.at[peer], XR.at[:, at(p, B), :], x1s, x1r.at[p], peer)
        return carry

    lax.fori_loop(1, REPS, send_slots, 0)
    own_slots = pltpu.make_async_copy(XS.at[p], XR.at[:, at(p, B), :], local_sem.at[0])
    own_slots.start()

    GP[...] = jnp.zeros(GP.shape, BF)
    loads[1].wait()

    def turn_leaf(i, carry):
        k, t = i // 4, lax.rem(i, 4)
        LWT[k, at(t, 256), :] = LW[k, :, at(t, 256)].T
        return carry

    lax.fori_loop(0, 16, turn_leaf, 0)
    loads[2].wait()

    def turn_mid(i, carry):
        a, b = i // 4, lax.rem(i, 4)
        MWT[at(b, 256), at(a, 256)] = MW[at(a, 256), at(b, 256)].T
        return carry

    lax.fori_loop(0, 16, turn_mid, 0)

    def leaf_chunk(i):
        src = source(i)
        lanes = at(src, B)

        def terms(t, squares):
            rows = at(t, 256)
            product = None
            for k in range(4):
                factor = 1.0 + nt(LWT[k, rows, :], XR[k, lanes, :])
                FK[k, rows, lanes] = factor
                product = factor if product is None else product * factor
            LB[rows, :] = product
            return squares + fold(product * product)

        r = factor_of(lax.fori_loop(0, 4, terms, jnp.zeros((8, B), F32)))
        RL[:, lanes] = jnp.broadcast_to(r, (8, B))

        def scale(t, carry):
            rows = at(t, 256)
            LM[rows, lanes] = (LB[rows, :] * r).astype(BF)
            return carry

        lax.fori_loop(0, 4, scale, 0)

        def mid(t, carry):
            rows = at(t, 256)
            MS[src, rows, :] = nn(MWT[rows, :], LM[:, lanes]).astype(BF)
            return carry

        lax.fori_loop(0, 4, mid, 0)

    def turn_slots(i):
        lanes = at(source(i), B)
        for k in range(4):
            XT[k, :, lanes] = XR[k, lanes, :].T

    own_slots.wait()
    leaf_chunk(0)
    own_mid = pltpu.make_async_copy(MS.at[p], MR.at[p], local_sem.at[1])
    own_mid.start()
    loads[3].wait()

    def part_sides(t, carry):
        WN[:, at(t, 32), :] = jnp.swapaxes(UW[at(t, 32)], 0, 1)
        return carry

    lax.fori_loop(0, 32, part_sides, 0)

    def turn_upper(t, carry):
        rows = at(t, 128)
        for side in range(2):
            WT[side, :, rows] = WN[side, rows, :].T
        return carry

    lax.fori_loop(0, 8, turn_upper, 0)
    turn_slots(0)

    def other_chunk(i, carry):
        src = source(i)
        await_bytes(XR.at[:, at(src, B), :], x1r.at[src])
        leaf_chunk(i)
        to_rep(MS.at[src], MR.at[p], x2s, x2r, src)
        turn_slots(i)
        return carry

    lax.fori_loop(1, REPS, other_chunk, 0)

    own_mid.wait()
    await_bytes(MR.at[0:3], x2r)
    c = lax.rem(s, 2)
    partner = s + 1 - 2 * c

    def mid_product(t, carry):
        rows = at(t, 128)
        product = 1.0 + MR[0, rows, :].astype(F32)
        for k in range(1, 4):
            product = product * (1.0 + MR[k, rows, :].astype(F32))
        A0[pl.ds(pl.multiple_of(c * D + t * 128, 128), 128), :] = product.astype(BF)
        return carry

    lax.fori_loop(0, 8, mid_product, 0)

    own = at(p, B)

    def spread(level, me, block):
        ref = A[level].at[at(me, block), :]
        to_sub(ref, ref, fs.at[level], fo.at[level], partner)

        def one(i, carry):
            peer = s - me + lax.rem(me + 2 * i, GROUP[level])
            to_sub(ref, ref, fs.at[level], fr.at[level, i], peer)
            return carry

        if GROUP[level] > 2:
            lax.fori_loop(1, GROUP[level] // 2, one, 0)

    def collect(level, me, block):
        half = GROUP[level] // 2

        def one(i, carry):
            ref = A[level].at[at(lax.rem(me - 2 * i + GROUP[level], GROUP[level]), block), :]
            await_bytes(ref, fr.at[level, i])
            to_sub(ref, ref, ff.at[level], fo.at[level], partner)
            return carry

        if half > 1:
            lax.fori_loop(1, half, one, 0)
        await_bytes(A[level].at[0 : half * block], fo.at[level])

    def share_rows(level):
        sides = 2 if 0 < level < LEVELS else 1

        def place_of(side, peer):
            first = 1 - c if level == 0 else side
            rows = pl.ds(pl.multiple_of(first * D + peer * 256, 256), 256)
            return A[level].at[rows, :], AX.at[level, first, :, own]

        def one(i, carry):
            peer = source(i)
            for side in range(sides):
                src, dst = place_of(side, peer)
                to_rep(src, dst, axs.at[level], axr.at[level], peer)
            return carry

        lax.fori_loop(1, REPS, one, 0)
        for side in range(sides):
            src, dst = place_of(side, p)
            copy = pltpu.make_async_copy(src, dst, local_sem.at[2 + 2 * level + side])
            copy.start()
            kept.append(copy)

    kept = []

    def squares_of(ref, start):
        def one(t, total):
            values = ref[pl.ds(pl.multiple_of(start + t * 256, 256), 256), :].astype(F32)
            return total + fold(values * values)

        return lax.fori_loop(0, 4, one, jnp.zeros((8, B), F32))

    spread(0, c, D)
    message = A0.at[at(c, D), :]

    def send_message(i, carry):
        to_rep(message, H0.at[:, own], h0s, h0r, source(i))
        return carry

    def leave_one(t, carry):
        rows = at(t, 128)
        rest = others([1.0 + MR[k, rows, :].astype(F32) for k in range(4)])
        for k in range(4):
            CS[k, rows, :] = rest[k].astype(BF)
        return carry

    lax.fori_loop(0, 8, leave_one, 0)

    def send_rest(i, carry):
        peer = source(i)
        to_rep(CS.at[peer], LO.at[:, own], x3s, x3r, peer)
        return carry

    lax.fori_loop(1, REPS, send_message, 0)
    lax.fori_loop(1, REPS, send_rest, 0)
    for copy in (
        pltpu.make_async_copy(CS.at[p], LO.at[:, own], local_sem.at[20]),
        pltpu.make_async_copy(message, H0.at[:, own], local_sem.at[21]),
    ):
        copy.start()
        kept.append(copy)
    scales = []
    for level in range(LEVELS):
        group, w, col = GROUP[level], WIDTH[level], COLUMN[level]
        collect(level, lax.rem(s, group), 2 * D // group)
        share_rows(level)
        left = factor_of(squares_of(A[level], 0))
        right = factor_of(squares_of(A[level], D))
        scales.append((left, right))
        me = lax.rem(s, GROUP[level + 1])
        size = min(w, 256)
        for t in range(w // size):
            rows = slice(col + t * size, col + (t + 1) * size)
            ul = nn(WT[0, rows, :], A[level][0:D, :]) * left
            ur = nn(WT[1, rows, :], A[level][D : 2 * D, :]) * right
            joined = (1.0 + ul) * (1.0 + ur)
            UL[rows, :] = ul
            UR[rows, :] = ur
            JJ[rows, :] = joined
            A[level + 1][pl.ds(pl.multiple_of(me * w + t * size, size), size), :] = joined.astype(BF)
        spread(level + 1, me, w)

    def share_grads(level):
        w, col = WIDTH[level], COLUMN[level]
        ref = GX.at[:, col : col + w, own]

        def one(i, carry):
            to_rep(ref, ref, gxs.at[level], gxr.at[level] if level else gx0.at[p], source(i))
            return carry

        lax.fori_loop(1, REPS, one, 0)

    def scatter(level, me):
        group = GROUP[level]

        def one(i, carry):
            d = lax.rem(me + i, group)
            to_sub(BS[level].at[d], BR[level].at[me], bs.at[level], br.at[level], s - me + d)
            return carry

        lax.fori_loop(1, group, one, 0)
        copy = pltpu.make_async_copy(BS[level].at[me], BR[level].at[me], local_sem.at[14 + level])
        copy.start()
        return copy

    collect(5, s, 32)
    share_rows(5)
    root_scale = factor_of(squares_of(A5, 0))
    col = COLUMN[5]
    za = nn(WT[0, col:D, :], A5[...]) * root_scale
    zb = nn(WT[1, col:D, :], A5[...]) * root_scale
    sigma = 1.0 / (1.0 + jnp.exp(-zb))
    loads[4].wait()
    cotangent = COT[...]
    ga = cotangent * sigma
    gb = cotangent * za * sigma * (1.0 - sigma)
    GX[0, col:D, own] = (ga * root_scale).astype(BF)
    GX[1, col:D, own] = (gb * root_scale).astype(BF)
    share_grads(5)
    ga = ga.astype(BF)
    gb = gb.astype(BF)
    GP[2, 0, 96:128, :] = ga
    GP[2, 1, 96:128, :] = gb
    dots = column_sum(ga.astype(F32) * za + gb.astype(F32) * zb)
    BS5[:, 32:48, :] = jnp.broadcast_to(split_tile(dots)[None], (SUBS, 16, B))

    def root_part(t, carry):
        rows = at(t, 256)
        part = nn(WN[0, rows, 896:1024], GP[2, 0]) + nn(WN[1, rows, 896:1024], GP[2, 1])
        BS5[at(t, 8), 0:32, :] = part.astype(BF).reshape(8, 32, B)
        return carry

    lax.fori_loop(0, 4, root_part, 0)
    own_chunk = scatter(5, s)

    def gathered(level, rows):
        group = GROUP[level]
        if group <= 8:
            total = BR[level][0, rows, :].astype(F32)
            for g in range(1, group):
                total = total + BR[level][g, rows, :].astype(F32)
            return total

        def one(i, total):
            for g in range(4):
                total = total + BR[level][4 * i + g, rows, :].astype(F32)
            return total

        size = rows.size if hasattr(rows, "size") else rows.stop - rows.start
        return lax.fori_loop(0, group // 4, one, jnp.zeros((size, B), F32))

    def await_chunks(level, copy):
        copy.wait()
        await_bytes(BR[level].at[0 : GROUP[level] - 1], br.at[level])
        size = CHUNK[level]
        return column_sum(gathered(level, slice(size, size + 16))) * (1.0 / D)

    for level in reversed(range(LEVELS)):
        group, w, col = GROUP[level], WIDTH[level], COLUMN[level]
        mean = await_chunks(level + 1, own_chunk)
        if level == LEVELS - 1:
            r = root_scale
        else:
            side_of = lax.rem(s // GROUP[level], 2)
            r = jnp.where(side_of == 1, scales[level + 1][1], scales[level + 1][0])
        left, right = scales[level]
        size = min(w, 64)

        def node_back(t, carry):
            dl, dr = carry
            rows = pl.ds(pl.multiple_of(col + t * size, size), size)
            total = gathered(level + 1, pl.ds(pl.multiple_of(t * size, size), size))
            ul, ur = UL[rows, :], UR[rows, :]
            v = r * (total - JJ[rows, :] * (r * mean))
            gl = v * (1.0 + ur)
            gr = v * (1.0 + ul)
            GX[0, rows, own] = (gl * left).astype(BF)
            GX[1, rows, own] = (gr * right).astype(BF)
            if level == 0:
                return carry
            gl = gl.astype(BF)
            gr = gr.astype(BF)
            if level < 3:
                GB[0, rows, :] = gl
                GB[1, rows, :] = gr
            else:
                GP[level - 3, 0, col - 896 : col - 896 + w, :] = gl
                GP[level - 3, 1, col - 896 : col - 896 + w, :] = gr
            return dl + fold(gl.astype(F32) * ul), dr + fold(gr.astype(F32) * ur)

        zero = jnp.zeros((8, B), F32)
        dl, dr = lax.fori_loop(0, w // size, node_back, (zero, zero))
        if level == 0:
            share_grads(0)
            break
        half, chunk = group // 2, CHUNK[level]
        for side, dot in ((0, dl), (1, dr)):
            tile = split_tile(column_sum(dot))
            BS[level][side * half : (side + 1) * half, chunk : chunk + 16, :] = jnp.broadcast_to(
                tile[None], (half, 16, B)
            )

        def part(t, carry):
            rows = at(t, 256)
            for side in range(2):
                if level < 3:
                    value = nn(WN[side, rows, col : col + w], GB[side, col : col + w, :])
                else:
                    value = nn(WN[side, rows, 896:1024], GP[level - 3, side])
                value = value.astype(BF)
                if chunk >= 256:
                    per = chunk // 256
                    BS[level][side * half + t // per, at(lax.rem(t, per), 256), :] = value
                else:
                    n = 256 // chunk
                    BS[level][pl.ds(side * half + t * n, n), 0:chunk, :] = value.reshape(n, chunk, B)
            return carry

        lax.fori_loop(0, 4, part, 0)
        own_chunk = scatter(level, lax.rem(s, group))
        share_grads(level)

    await_bytes(MS.at[0:3], x2s)

    def partial_sums(i):
        src = source(i)
        slot = i // 2 - i // 3
        lanes = at(src, B)
        if i:
            await_bytes(GX.at[:, 0:512, lanes], gx0.at[src])

        def other(t, carry):
            rows = at(t, 256)
            MS[src, rows, :] = nn(WN[1 - c, rows, 0:512], GX[1 - c, 0:512, lanes]).astype(BF)
            return carry

        def mine(t, carry):
            rows = at(t, 256)
            PM[slot, rows, :] = nn(WN[c, rows, 0:512], GX[c, 0:512, lanes])
            return carry

        lax.fori_loop(0, 4, other, 0)
        to_sub(MS.at[src], PR.at[src], pss, prs.at[src], partner)
        lax.fori_loop(0, 4, mine, 0)

    partial_sums(0)

    for copy in kept:
        copy.wait()
    for level in range(LEVELS + 1):
        if 0 < level < LEVELS:
            await_bytes(AX.at[level, :, :, 0 : 3 * B], axr.at[level])
        else:
            await_bytes(AX.at[level, 0, :, 0 : 3 * B], axr.at[level])
    await_bytes(LO.at[:, 0 : 3 * B], x3r)
    await_bytes(H0.at[:, 0 : 3 * B], h0r)

    def message_scale(t, total):
        values = H0[at(t, 128), :].astype(F32)
        return total + fold(values * values)

    R0[...] = jnp.broadcast_to(
        factor_of(lax.fori_loop(0, 8, message_scale, jnp.zeros((8, ALL), F32))), (8, ALL)
    )

    def await_grads(level):
        w, col = WIDTH[level], COLUMN[level]
        await_bytes(GX.at[:, col : col + w, 0 : 3 * B], gxr.at[level])

    for level in (5, 4, 3):
        await_grads(level)
    lane = lax.broadcasted_iota(jnp.int32, (256, 128), 1)
    for side in range(2):
        grads = GX[side, 896:1024, :]
        g3 = nt(AX[3, side], grads)
        g4 = nt(AX[4, side], grads)
        g5 = nt(AX[5, 0], grads)
        OU[side, :, 896:1024] = jnp.where(lane < 64, g3, jnp.where(lane < 96, g4, g5)).astype(BF)

    for level in (2, 1):
        await_grads(level)
        w, col = WIDTH[level], COLUMN[level]
        for side in range(2):
            OU[side, :, col : col + w] = nt(AX[level, side], GX[side, col : col + w, :]).astype(BF)

    def leaf_back(i):
        src = source(i)
        slot = i // 2 - i // 3
        lanes = at(src, B)
        await_bytes(PR.at[src], prs.at[src])
        scale0 = R0[0:1, lanes]

        def add_parts(t, total):
            rows = at(t, 128)
            value = PM[slot, rows, :] + PR[src, rows, :].astype(F32)
            PM[slot, rows, :] = value
            return total + fold(value * H0[rows, lanes].astype(F32))

        mean0 = column_sum(lax.fori_loop(0, 8, add_parts, jnp.zeros((8, B), F32))) * (1.0 / D)
        shift = scale0 * scale0 * mean0

        def mid_back(t, carry):
            rows = at(t, 128)
            v = PM[slot, rows, :] - H0[rows, lanes].astype(F32) * shift
            CR[rows, lanes] = (v * LO[rows, lanes].astype(F32)).astype(BF)
            return carry

        lax.fori_loop(0, 8, mid_back, 0)

        def product(t, total):
            rows = at(t, 256)
            value = nn(MW[rows, :], CR[:, lanes])
            LB[rows, :] = value
            return total + fold(value * LM[rows, lanes].astype(F32))

        mean = column_sum(lax.fori_loop(0, 4, product, jnp.zeros((8, B), F32))) * (1.0 / D)
        r = RL[0:1, lanes]

        def cotangents(t, carry):
            rows = at(t, 128)
            v = r * (LB[rows, :] - LM[rows, lanes].astype(F32) * mean)
            rest = others([FK[k, rows, lanes] for k in range(4)])
            for k in range(4):
                CT[k, rows, lanes] = (v * rest[k]).astype(BF)
            return carry

        lax.fori_loop(0, 8, cotangents, 0)

    leaf_back(0)
    partial_sums(1)
    partial_sums(2)
    leaf_back(1)
    leaf_back(2)
    partial_sums(3)

    rows = at(p, 256)
    OU[c, :, 0:512] = nt(H0[rows, :], GX[c, 0:512, :]).astype(BF)
    OU[1 - c, :, 0:512] = nt(AX[0, 1 - c], GX[1 - c, 0:512, :]).astype(BF)

    def weave(t, carry):
        rows = at(t, 64)
        for side in range(2):
            OI[rows, side, :] = OU[side, rows, :]
        return carry

    lax.fori_loop(0, 4, weave, 0)
    out_upper = pltpu.make_async_copy(OI, ug_hbm, out_sem.at[2])
    out_upper.start()
    leaf_back(3)

    def leaf_gradient(k, carry):
        LW[k] = nt(XT[k], CT[k]).astype(BF)
        return carry

    lax.fori_loop(0, 4, leaf_gradient, 0)
    out_leaf = pltpu.make_async_copy(LW, lg_hbm, out_sem.at[0])
    out_leaf.start()

    def mid_gradient(t, carry):
        rows = at(t, 256)
        MWT[rows, :] = nt(LM[rows, :], CR[...]).astype(BF)
        return carry

    lax.fori_loop(0, 4, mid_gradient, 0)
    out_mid = pltpu.make_async_copy(MWT, mg_hbm, out_sem.at[1])
    out_mid.start()

    await_bytes(XS.at[0:3], x1s)
    await_bytes(CS.at[0:3], x3s)
    await_bytes(H0.at[:, 0 : 3 * B], h0s)
    await_bytes(MS, pss)
    for level in range(LEVELS + 1):
        half = GROUP[level] // 2
        block = A[level].shape[0] // GROUP[level]
        await_bytes(A[level].at[0 : half * block], fs.at[level])
        if half > 1:
            await_bytes(A[level].at[0 : (half - 1) * block], ff.at[level])
        if level:
            await_bytes(BS[level].at[0 : GROUP[level] - 1], bs.at[level])
        if 0 < level < LEVELS:
            await_bytes(AX.at[level, :, :, 0 : 3 * B], axs.at[level])
        else:
            await_bytes(AX.at[level, 0, :, 0 : 3 * B], axs.at[level])
        w, col = WIDTH[level], COLUMN[level]
        await_bytes(GX.at[:, col : col + w, 0 : 3 * B], gxs.at[level])
    out_leaf.wait()
    out_mid.wait()
    out_upper.wait()


def scratch():
    vm = pltpu.VMEM
    dma = pltpu.SemaphoreType.DMA
    chunks = [vm((GROUP[j], CHUNK[j] + 16, B), BF) for j in range(1, LEVELS + 1)]
    return (
        [
            vm((2048, F), BF), vm((256, 256), BF), vm((4, 4, B, F), BF), vm((4, ALL, F), BF),
            vm((4, F, D), BF), vm((4, D, F), BF), vm((D, D), BF), vm((D, D), BF),
            vm((D, 2, D), BF), vm((2, D, D), BF), vm((2, D, D), BF), vm((32, B), F32),
            vm((4, D, ALL), F32), vm((8, ALL), F32), vm((D, ALL), BF),
            vm((4, D, B), BF), vm((4, D, B), BF),
        ]
        + [vm((2 * D, B), BF)] * 5
        + [vm((D, B), BF)]
        + [vm((D, B), F32)] * 3
        + [vm((3, 2, 128, B), BF), vm((2, D, B), BF)]
        + chunks
        + chunks
        + [
            vm((2, D, ALL), BF), vm((6, 2, 256, ALL), BF), vm((4, D, B), BF), vm((D, ALL), BF),
            vm((D, B), F32), vm((4, D, ALL), BF), vm((4, F, ALL), BF), vm((2, 256, D), BF),
            vm((256, 2, D), BF), vm((D, ALL), BF), vm((D, ALL), BF), vm((8, ALL), F32),
            vm((4, D, B), BF), vm((2, D, B), F32),
        ]
        + [
            dma((5,)), dma((22,)), dma, dma((4,)), dma, dma, dma, dma, dma, dma,
            dma((6,)), dma((6, 16)), dma((6,)), dma((6,)), dma((6,)), dma((6,)),
            dma((6,)), dma((6,)), dma((6,)), dma((6,)), dma((4,)), dma, dma((4,)), dma((3,)),
        ]
    )


def on_device(regions, leaf_map, leaf_bond_weight, mid_weight, upper_weight, head_cotangent):
    anywhere = pl.BlockSpec(memory_space=pl.ANY)
    outs = pl.pallas_call(
        kernel,
        out_shape=(
            jax.ShapeDtypeStruct((4, F, D), BF),
            jax.ShapeDtypeStruct((D, D), BF),
            jax.ShapeDtypeStruct((256, 2, D), BF),
        ),
        in_specs=[pl.BlockSpec(memory_space=pltpu.SMEM)] + [anywhere] * 5,
        out_specs=(anywhere,) * 3,
        scratch_shapes=scratch(),
        compiler_params=pltpu.CompilerParams(
            collective_id=0, has_side_effects=True, vmem_limit_bytes=67000000
        ),
    )(
        leaf_map, regions.reshape(B * 16, F), leaf_bond_weight[0], mid_weight[0, 0],
        upper_weight[0], head_cotangent.T,
    )
    return (outs[0][None], outs[1][None, None], outs[2][None])


def solution(mesh):
    placed = (
        P("rep", "sub", None),
        P("sub"),
        P(("sub", "rep"), None, None, None),
        P("sub", "rep", None, None),
        P("sub", None, None, None),
        P("rep", "sub"),
    )
    return jax.shard_map(
        on_device,
        mesh=mesh,
        in_specs=placed,
        out_specs=(
            P(("sub", "rep"), None, None, None),
            P("sub", "rep", None, None),
            P("sub", "rep", None, None),
        ),
        check_vma=False,
    )
```

```python
import jax
import jax.numpy as jnp
from jax import lax
from jax.experimental import pallas as pl
from jax.experimental.pallas import tpu as pltpu
from jax.sharding import PartitionSpec as P

F32 = jnp.float32
BF = jnp.bfloat16
MESH = pl.DeviceIdType.MESH
EPSILON = 1e-06
D = 1024
F = 256
B = 128
REPS = 4
SUBS = 32
LEVELS = 5
ALL = REPS * B
WIDTH = [D // 2 ** (j + 1) for j in range(LEVELS)] + [D // SUBS]
COLUMN = [D - 2 * WIDTH[j] for j in range(LEVELS)] + [D - D // SUBS]
CHUNK = [2 * WIDTH[j] for j in range(LEVELS)] + [WIDTH[5]]
GROUP = [2 ** (j + 1) for j in range(LEVELS)] + [SUBS]


def nn(a, b):
    return jnp.dot(a, b, preferred_element_type=F32)


def nt(a, b):
    return lax.dot_general(a, b, (((1,), (1,)), ((), ())), preferred_element_type=F32)


def fold(values):
    return jnp.sum(values.reshape(values.shape[0] // 8, 8, values.shape[1]), axis=0)


def column_sum(values):
    return jnp.sum(values, axis=0, keepdims=True)


def factor_of(squares):
    return lax.rsqrt(column_sum(squares) * (1.0 / D) + EPSILON)


def at(index, size):
    return pl.ds(pl.multiple_of(index * size, size), size)


def lanes_of(i):
    return slice(i * B, (i + 1) * B)


OFFSET = (0, 1, 3, 2)
BACK = (0, 2, 1, 3)


def others(f):
    p01 = f[0] * f[1]
    p23 = f[2] * f[3]
    return [f[1] * p23, f[0] * p23, p01 * f[3], p01 * f[2]]


def split_tile(row):
    high = row.astype(BF).astype(F32)
    index = lax.broadcasted_iota(jnp.int32, (16, B), 0)
    tile = jnp.where(index == 0, high, jnp.where(index == 1, row - high, 0.0))
    return tile.astype(BF)


def kernel(
    map_ref, reg_hbm, lw_hbm, mw_hbm, uw_hbm, cot_hbm,
    lg_hbm, mg_hbm, ug_hbm,
    R, Q, XS, XR, LW, LWT, MW, MWT, UW, WN, WT, COT, FK, RL, LM, MS, MR,
    A0, A1, A2, A3, A4, A5, UL, UR, JJ, GP, GB, WP, BO, BI, PF,
    BS1, BS2, BS3, BS4, BS5, BR1, BR2, BR3, BR4, BR5,
    GX, AX, CS, CR, LB, CT, XT, OU, OI, LO, H0, R0, PR, PM,
    load_sem, local_sem, x1s, x1r, x2s, x2r, x3s, x3r, h0s, h0r, fs, fr, ff, fo, bs, br, bos, bis,
    axs, axr, gxs, gxr, gx0, pss, prs, out_sem,
):
    A = [A0, A1, A2, A3, A4, A5]
    BS = [None, BS1, BS2, BS3, BS4, BS5]
    BR = [None, BR1, BR2, BR3, BR4, BR5]
    s = lax.axis_index("sub")
    p = lax.axis_index("rep")

    def to_rep(src, dst, send, recv, peer):
        pltpu.make_async_remote_copy(
            src_ref=src, dst_ref=dst, send_sem=send, recv_sem=recv,
            device_id={"rep": peer}, device_id_type=MESH,
        ).start()

    def to_sub(src, dst, send, recv, peer):
        pltpu.make_async_remote_copy(
            src_ref=src, dst_ref=dst, send_sem=send, recv_sem=recv,
            device_id={"sub": peer}, device_id_type=MESH,
        ).start()

    def await_bytes(ref, sem):
        pltpu.make_async_copy(ref, ref, sem).wait()

    loads = [
        pltpu.make_async_copy(src, dst, load_sem.at[i])
        for i, (src, dst) in enumerate(
            [(reg_hbm, R), (lw_hbm, LW), (mw_hbm, MW), (uw_hbm, UW), (cot_hbm, COT)]
        )
    ]
    for load in loads:
        load.start()

    barrier = pltpu.get_barrier_semaphore()

    def greet_sub(i, carry):
        pl.semaphore_signal(
            barrier, inc=1, device_id={"sub": lax.rem(s + i, SUBS)}, device_id_type=MESH
        )
        return carry

    def greet_rep(i, carry):
        pl.semaphore_signal(
            barrier, inc=1, device_id={"rep": lax.rem(p + i, REPS)}, device_id_type=MESH
        )
        return carry

    lax.fori_loop(1, SUBS, greet_sub, 0)
    lax.fori_loop(1, REPS, greet_rep, 0)

    column = lax.broadcasted_iota(jnp.int32, (16, 256), 1)
    sample = lax.broadcasted_iota(jnp.int32, (16, 256), 0)
    for l in range(16):
        wanted = sample * 16 + map_ref[l]
        Q[16 * l : 16 * l + 16, :] = jnp.where(column == wanted, 1.0, 0.0).astype(BF)
    loads[0].wait()

    def place(q, carry):
        got = nn(Q[...], R[at(q, 256), :]).astype(BF)
        for l in range(16):
            XS[l // 4, l % 4, at(q, 16), :] = got[16 * l : 16 * l + 16, :]
        return carry

    lax.fori_loop(0, 8, place, 0)
    pl.semaphore_wait(barrier, SUBS - 1 + REPS - 1)

    def source(i):
        return lax.rem(p + OFFSET[i], REPS)

    for i in range(1, REPS):
        peer = source(i)
        to_rep(XS.at[peer], XR.at[:, lanes_of(BACK[i]), :], x1s, x1r.at[BACK[i]], peer)
    own_slots = pltpu.make_async_copy(XS.at[p], XR.at[:, 0:B, :], local_sem.at[0])
    own_slots.start()

    GP[...] = jnp.zeros(GP.shape, BF)
    loads[1].wait()

    def turn_leaf(i, carry):
        k, t = i // 4, lax.rem(i, 4)
        LWT[k, at(t, 256), :] = LW[k, :, at(t, 256)].T
        return carry

    lax.fori_loop(0, 16, turn_leaf, 0)
    loads[2].wait()

    def turn_mid(i, carry):
        a, b = i // 4, lax.rem(i, 4)
        MWT[at(b, 256), at(a, 256)] = MW[at(a, 256), at(b, 256)].T
        return carry

    lax.fori_loop(0, 16, turn_mid, 0)

    def leaf_blocks(lanes):
        n = lanes.stop - lanes.start
        squares = jnp.zeros((8, n), F32)
        for t in range(4):
            rows = slice(256 * t, 256 * (t + 1))
            product = None
            for k in range(4):
                factor = 1.0 + nt(LWT[k, rows, :], XR[k, lanes, :])
                FK[k, rows, lanes] = factor.astype(BF)
                product = factor if product is None else product * factor
            LB[rows, 0:n] = product
            squares = squares + fold(product * product)
        r = factor_of(squares)
        RL[:, lanes] = jnp.broadcast_to(r, (8, n))
        for t in range(4):
            rows = slice(256 * t, 256 * (t + 1))
            LM[rows, lanes] = (LB[rows, 0:n] * r).astype(BF)
        for t in range(4):
            rows = slice(256 * t, 256 * (t + 1))
            value = nn(MWT[rows, :], LM[:, lanes]).astype(BF)
            for b in range(n // B):
                MS[lanes.start // B + b, rows, :] = value[:, lanes_of(b)]

    def turn_slots(lanes):
        for k in range(4):
            XT[k, :, lanes] = XR[k, lanes, :].T

    own_slots.wait()
    leaf_blocks(slice(0, B))
    own_mid = pltpu.make_async_copy(MS.at[0], MR.at[p], local_sem.at[1])
    own_mid.start()
    loads[3].wait()

    def part_sides(t, carry):
        WN[:, at(t, 32), :] = jnp.swapaxes(UW[at(t, 32)], 0, 1)
        return carry

    lax.fori_loop(0, 32, part_sides, 0)

    def turn_upper(t, carry):
        rows = at(t, 128)
        for side in range(2):
            WT[side, :, rows] = WN[side, rows, :].T
        return carry

    lax.fori_loop(0, 8, turn_upper, 0)
    for level in (2, 3, 4):
        size = CHUNK[level]
        col = min(COLUMN[level], 896)
        count = D // size
        for side in range(2):
            for q in range(count):
                to = (q % 2 * (count // 2) + q // 2) * size
                WP[level - 2, side, to : to + size, :] = WN[side, q * size : (q + 1) * size, col : col + 128]
    turn_slots(slice(0, B))

    for blocks in ((1, 2), (3,)):
        for i in blocks:
            await_bytes(XR.at[:, lanes_of(i), :], x1r.at[i])
        lanes = slice(blocks[0] * B, (blocks[-1] + 1) * B)
        leaf_blocks(lanes)
        for i in blocks:
            to_rep(MS.at[i], MR.at[p], x2s, x2r, source(i))
        turn_slots(lanes)

    own_mid.wait()
    await_bytes(MR.at[0:3], x2r)
    c = lax.rem(s, 2)
    partner = s + 1 - 2 * c

    for t in range(8):
        rows = slice(128 * t, 128 * (t + 1))
        product = 1.0 + MR[0, rows, :].astype(F32)
        for k in range(1, 4):
            product = product * (1.0 + MR[k, rows, :].astype(F32))
        A0[pl.ds(pl.multiple_of(c * D + t * 128, 128), 128), :] = product.astype(BF)

    own = slice(0, B)

    def spread(level, me, block):
        ref = A[level].at[at(me, block), :]
        to_sub(ref, ref, fs.at[level], fo.at[level], partner)

        def one(i, carry):
            peer = s - me + lax.rem(me + 2 * i, GROUP[level])
            to_sub(ref, ref, fs.at[level], fr.at[level, i], peer)
            return carry

        if GROUP[level] > 2:
            lax.fori_loop(1, GROUP[level] // 2, one, 0)

    def collect(level, me, block):
        half = GROUP[level] // 2

        def one(i, carry):
            ref = A[level].at[at(lax.rem(me - 2 * i + GROUP[level], GROUP[level]), block), :]
            await_bytes(ref, fr.at[level, i])
            to_sub(ref, ref, ff.at[level], fo.at[level], partner)
            return carry

        if half > 1:
            lax.fori_loop(1, half, one, 0)
        await_bytes(A[level].at[0 : half * block], fo.at[level])

    def share_rows(level):
        sides = 2 if 0 < level < LEVELS else 1

        def place_of(side, i):
            first = 1 - c if level == 0 else side
            rows = pl.ds(pl.multiple_of(first * D + source(i) * 256, 256), 256)
            return A[level].at[rows, :], AX.at[level, first, :, lanes_of(BACK[i])]

        for i in range(1, REPS):
            for side in range(sides):
                src, dst = place_of(side, i)
                to_rep(src, dst, axs.at[level], axr.at[level], source(i))
        for side in range(sides):
            src, dst = place_of(side, 0)
            copy = pltpu.make_async_copy(src, dst, local_sem.at[2 + 2 * level + side])
            copy.start()
            kept.append(copy)

    kept = []

    def squares_of(ref, start, lanes=slice(0, B)):
        total = jnp.zeros((8, B), F32)
        for t in range(4):
            values = ref[start + 256 * t : start + 256 * (t + 1), lanes].astype(F32)
            total = total + fold(values * values)
        return total

    spread(0, c, D)
    message = A0.at[at(c, D), :]

    def leave_one(t, carry):
        rows = at(t, 128)
        rest = others([1.0 + MR[k, rows, :].astype(F32) for k in range(4)])
        for k in range(4):
            CS[k, rows, :] = rest[k].astype(BF)
        return carry

    lax.fori_loop(0, 8, leave_one, 0)

    for i in range(1, REPS):
        to_rep(message, H0.at[:, lanes_of(BACK[i])], h0s, h0r, source(i))
    for i in range(1, REPS):
        to_rep(CS.at[source(i)], LO.at[:, lanes_of(BACK[i])], x3s, x3r, source(i))
    for copy in (
        pltpu.make_async_copy(CS.at[p], LO.at[:, own], local_sem.at[20]),
        pltpu.make_async_copy(message, H0.at[:, own], local_sem.at[21]),
    ):
        copy.start()
        kept.append(copy)
    scales = []
    for level in range(LEVELS):
        group, w, col = GROUP[level], WIDTH[level], COLUMN[level]
        collect(level, lax.rem(s, group), 2 * D // group)
        share_rows(level)
        left = factor_of(squares_of(A[level], 0))
        right = factor_of(squares_of(A[level], D))
        scales.append((left, right))
        me = lax.rem(s, GROUP[level + 1])
        size = min(w, 256)
        for t in range(w // size):
            rows = slice(col + t * size, col + (t + 1) * size)
            ul = nn(WT[0, rows, :], A[level][0:D, :]) * left
            ur = nn(WT[1, rows, :], A[level][D : 2 * D, :]) * right
            joined = (1.0 + ul) * (1.0 + ur)
            UL[rows, :] = ul
            UR[rows, :] = ur
            JJ[rows, :] = joined
            A[level + 1][pl.ds(pl.multiple_of(me * w + t * size, size), size), :] = joined.astype(BF)
        spread(level + 1, me, w)

    def share_grads(level):
        w, col = WIDTH[level], COLUMN[level]
        for i in range(1, REPS):
            to_rep(
                GX.at[:, col : col + w, own], GX.at[:, col : col + w, lanes_of(BACK[i])],
                gxs.at[level], gxr.at[level] if level else gx0.at[BACK[i]], source(i),
            )

    def scatter(level, me):
        chips = GROUP[level] // 2 if level < LEVELS else SUBS
        step = 2 if level < LEVELS else 1
        at_chip = me // step

        def one(i, carry):
            d = lax.rem(at_chip + i, chips)
            peer = s + (d - at_chip) * step
            to_sub(BS[level].at[d], BR[level].at[at_chip], bs.at[level], br.at[level], peer)
            return carry

        lax.fori_loop(1, chips, one, 0)
        copy = pltpu.make_async_copy(
            BS[level].at[at_chip], BR[level].at[at_chip], local_sem.at[14 + level]
        )
        copy.start()
        return copy

    collect(5, s, 32)
    share_rows(5)
    root_scale = factor_of(squares_of(A5, 0))
    col = COLUMN[5]
    za = nn(WT[0, col:D, :], A5[...]) * root_scale
    zb = nn(WT[1, col:D, :], A5[...]) * root_scale
    sigma = 1.0 / (1.0 + jnp.exp(-zb))
    loads[4].wait()
    cotangent = COT[...]
    ga = cotangent * sigma
    gb = cotangent * za * sigma * (1.0 - sigma)
    GX[0, col:D, own] = (ga * root_scale).astype(BF)
    GX[1, col:D, own] = (gb * root_scale).astype(BF)
    share_grads(5)
    ga = ga.astype(BF)
    gb = gb.astype(BF)
    GP[2, 0, 96:128, :] = ga
    GP[2, 1, 96:128, :] = gb
    dots = column_sum(ga.astype(F32) * za + gb.astype(F32) * zb)
    BS5[:, 32:48, :] = jnp.broadcast_to(split_tile(dots)[None], (SUBS, 16, B))

    for t in range(4):
        rows = slice(256 * t, 256 * (t + 1))
        part = nn(WN[0, rows, 896:1024], GP[2, 0]) + nn(WN[1, rows, 896:1024], GP[2, 1])
        BS5[8 * t : 8 * t + 8, 0:32, :] = part.astype(BF).reshape(8, 32, B)
    own_chunk = scatter(5, s)

    def gathered(level, rows):
        group = BR[level].shape[0]
        total = BR[level][0, rows, :].astype(F32)
        for g in range(1, group):
            total = total + BR[level][g, rows, :].astype(F32)
        return total

    def await_chunks(level, copy):
        copy.wait()
        await_bytes(BR[level].at[0 : BR[level].shape[0] - 1], br.at[level])
        size = CHUNK[level]
        return column_sum(gathered(level, slice(size, size + 16))) * (1.0 / D)

    for level in reversed(range(LEVELS)):
        group, w, col = GROUP[level], WIDTH[level], COLUMN[level]
        mean = await_chunks(level + 1, own_chunk)
        if level == LEVELS - 1:
            r = root_scale
        else:
            side_of = lax.rem(s // GROUP[level], 2)
            r = jnp.where(side_of == 1, scales[level + 1][1], scales[level + 1][0])
        left, right = scales[level]
        size = min(w, 64)

        def node_back(t, carry):
            dl, dr = carry
            rows = pl.ds(pl.multiple_of(col + t * size, size), size)
            total = gathered(level + 1, pl.ds(pl.multiple_of(t * size, size), size))
            ul, ur = UL[rows, :], UR[rows, :]
            v = r * (total - JJ[rows, :] * (r * mean))
            gl = v * (1.0 + ur)
            gr = v * (1.0 + ul)
            GX[0, rows, own] = (gl * left).astype(BF)
            GX[1, rows, own] = (gr * right).astype(BF)
            if level == 0:
                return carry
            gl = gl.astype(BF)
            gr = gr.astype(BF)
            if level < 3:
                GB[0, rows, :] = gl
                GB[1, rows, :] = gr
            else:
                GP[level - 3, 0, col - 896 : col - 896 + w, :] = gl
                GP[level - 3, 1, col - 896 : col - 896 + w, :] = gr
            return dl + fold(gl.astype(F32) * ul), dr + fold(gr.astype(F32) * ur)

        zero = jnp.zeros((8, B), F32)
        dl, dr = lax.fori_loop(0, w // size, node_back, (zero, zero))
        if level == 0:
            share_grads(0)
            break
        chunk = CHUNK[level]
        dots = [column_sum(dl), column_sum(dr)]

        def half_sums(side, parity):
            rows = pl.ds(pl.multiple_of(parity * 512, 512), 512)
            if level == 1:
                return nn(WN[side, rows, col : col + w], GB[side, col : col + w, :])
            if level == 2:
                return nn(WP[0, side, rows, :], GB[side, col : col + w, :])
            return nn(WP[level - 2, side, rows, :], GP[level - 3, side])

        for side in range(2):
            BO[level - 1, side, 0:512, :] = half_sums(side, 1 - c).astype(BF)
            BO[level - 1, side, 512:528, :] = split_tile(dots[side])
        to_sub(BO.at[level - 1], BI.at[level - 1], bos.at[level], bis.at[level], partner)
        for side in range(2):
            PF[side] = half_sums(side, c)
        await_bytes(BI.at[level - 1], bis.at[level])
        quarter = group // 4
        for side in range(2):
            tile = split_tile(dots[side] + column_sum(BI[level - 1, side, 512:528, :].astype(F32)))
            chunks = slice(side * quarter, (side + 1) * quarter)
            value = (PF[side] + BI[level - 1, side, 0:512, :].astype(F32)).astype(BF)
            BS[level][chunks, 0:chunk, :] = value.reshape(quarter, chunk, B)
            BS[level][chunks, chunk : chunk + 16, :] = jnp.broadcast_to(tile[None], (quarter, 16, B))
        own_chunk = scatter(level, lax.rem(s, group))
        share_grads(level)

    await_bytes(MS.at[0:3], x2s)

    def partial_sums(blocks):
        for i in blocks:
            if i:
                await_bytes(GX.at[:, 0:512, lanes_of(i)], gx0.at[i])
        lanes = slice(blocks[0] * B, (blocks[-1] + 1) * B)
        for t in range(4):
            rows = slice(256 * t, 256 * (t + 1))
            value = nn(WN[1 - c, rows, 0:512], GX[1 - c, 0:512, lanes]).astype(BF)
            for b, i in enumerate(blocks):
                MS[i, rows, :] = value[:, lanes_of(b)]
        for i in blocks:
            to_sub(MS.at[i], PR.at[i], pss, prs.at[i], partner)
        for t in range(4):
            rows = slice(256 * t, 256 * (t + 1))
            PM[rows, 0 : B * len(blocks)] = nn(WN[c, rows, 0:512], GX[c, 0:512, lanes])

    partial_sums((0,))

    for copy in kept:
        copy.wait()
    for level in range(LEVELS + 1):
        if 0 < level < LEVELS:
            await_bytes(AX.at[level, :, :, 0 : 3 * B], axr.at[level])
        else:
            await_bytes(AX.at[level, 0, :, 0 : 3 * B], axr.at[level])
    await_bytes(LO.at[:, 0 : 3 * B], x3r)
    await_bytes(H0.at[:, 0 : 3 * B], h0r)

    for i in range(REPS):
        R0[:, lanes_of(i)] = jnp.broadcast_to(factor_of(squares_of(H0, 0, lanes_of(i))), (8, B))

    def await_grads(level):
        w, col = WIDTH[level], COLUMN[level]
        await_bytes(GX.at[:, col : col + w, 0 : 3 * B], gxr.at[level])

    for level in (5, 4, 3):
        await_grads(level)
    lane = lax.broadcasted_iota(jnp.int32, (256, 128), 1)
    for side in range(2):
        grads = GX[side, 896:1024, :]
        g3 = nt(AX[3, side], grads)
        g4 = nt(AX[4, side], grads)
        g5 = nt(AX[5, 0], grads)
        OU[side, :, 896:1024] = jnp.where(lane < 64, g3, jnp.where(lane < 96, g4, g5)).astype(BF)

    for level in (2, 1):
        await_grads(level)
        w, col = WIDTH[level], COLUMN[level]
        for side in range(2):
            OU[side, :, col : col + w] = nt(AX[level, side], GX[side, col : col + w, :]).astype(BF)

    def leaf_back(blocks):
        lanes = slice(blocks[0] * B, (blocks[-1] + 1) * B)
        n = B * len(blocks)
        for i in blocks:
            await_bytes(PR.at[i], prs.at[i])
        for b, i in enumerate(blocks):
            part = lanes_of(b)
            total = jnp.zeros((8, B), F32)
            for t in range(8):
                rows = slice(128 * t, 128 * (t + 1))
                value = PM[rows, part] + PR[i, rows, :].astype(F32)
                PM[rows, part] = value
                total = total + fold(value * H0[rows, lanes_of(i)].astype(F32))
            scale0 = R0[0:1, lanes_of(i)]
            shift = scale0 * scale0 * (column_sum(total) * (1.0 / D))
            for t in range(8):
                rows = slice(128 * t, 128 * (t + 1))
                v = PM[rows, part] - H0[rows, lanes_of(i)].astype(F32) * shift
                CR[rows, lanes_of(i)] = (v * LO[rows, lanes_of(i)].astype(F32)).astype(BF)
        total = jnp.zeros((8, n), F32)
        for t in range(4):
            rows = slice(256 * t, 256 * (t + 1))
            value = nn(MW[rows, :], CR[:, lanes])
            LB[rows, 0:n] = value
            total = total + fold(value * LM[rows, lanes].astype(F32))
        mean = column_sum(total) * (1.0 / D)
        r = RL[0:1, lanes]
        for t in range(16):
            rows = slice(64 * t, 64 * (t + 1))
            v = r * (LB[rows, 0:n] - LM[rows, lanes].astype(F32) * mean)
            rest = others([FK[k, rows, lanes].astype(F32) for k in range(4)])
            for k in range(4):
                CT[k, rows, lanes] = (v * rest[k]).astype(BF)

    leaf_back((0,))
    partial_sums((1, 2))
    leaf_back((1, 2))
    partial_sums((3,))

    rows = at(p, 256)
    OU[c, :, 0:512] = nt(H0[rows, :], GX[c, 0:512, :]).astype(BF)
    OU[1 - c, :, 0:512] = nt(AX[0, 1 - c], GX[1 - c, 0:512, :]).astype(BF)

    def weave(t, carry):
        rows = at(t, 64)
        for side in range(2):
            OI[rows, side, :] = OU[side, rows, :]
        return carry

    lax.fori_loop(0, 4, weave, 0)
    out_upper = pltpu.make_async_copy(OI, ug_hbm, out_sem.at[2])
    out_upper.start()
    leaf_back((3,))

    def leaf_gradient(k, carry):
        LW[k] = nt(XT[k], CT[k]).astype(BF)
        return carry

    lax.fori_loop(0, 4, leaf_gradient, 0)
    out_leaf = pltpu.make_async_copy(LW, lg_hbm, out_sem.at[0])
    out_leaf.start()

    def mid_gradient(t, carry):
        rows = at(t, 256)
        MWT[rows, :] = nt(LM[rows, :], CR[...]).astype(BF)
        return carry

    lax.fori_loop(0, 4, mid_gradient, 0)
    out_mid = pltpu.make_async_copy(MWT, mg_hbm, out_sem.at[1])
    out_mid.start()

    await_bytes(XS.at[0:3], x1s)
    await_bytes(CS.at[0:3], x3s)
    await_bytes(H0.at[:, 0 : 3 * B], h0s)
    await_bytes(MS, pss)
    for level in range(1, LEVELS):
        await_bytes(BO.at[level - 1], bos.at[level])
    for level in range(LEVELS + 1):
        half = GROUP[level] // 2
        block = A[level].shape[0] // GROUP[level]
        await_bytes(A[level].at[0 : half * block], fs.at[level])
        if half > 1:
            await_bytes(A[level].at[0 : (half - 1) * block], ff.at[level])
        if level:
            await_bytes(BS[level].at[0 : BS[level].shape[0] - 1], bs.at[level])
        if 0 < level < LEVELS:
            await_bytes(AX.at[level, :, :, 0 : 3 * B], axs.at[level])
        else:
            await_bytes(AX.at[level, 0, :, 0 : 3 * B], axs.at[level])
        w, col = WIDTH[level], COLUMN[level]
        await_bytes(GX.at[:, col : col + w, 0 : 3 * B], gxs.at[level])
    out_leaf.wait()
    out_mid.wait()
    out_upper.wait()


def scratch():
    vm = pltpu.VMEM
    dma = pltpu.SemaphoreType.DMA
    counts = [g // 2 for g in GROUP[:LEVELS]] + [SUBS]
    chunks = [vm((counts[j], CHUNK[j] + 16, B), BF) for j in range(1, LEVELS + 1)]
    return (
        [
            vm((2048, F), BF), vm((256, 256), BF), vm((4, 4, B, F), BF), vm((4, ALL, F), BF),
            vm((4, F, D), BF), vm((4, D, F), BF), vm((D, D), BF), vm((D, D), BF),
            vm((D, 2, D), BF), vm((2, D, D), BF), vm((2, D, D), BF), vm((32, B), F32),
            vm((4, D, ALL), BF), vm((8, ALL), F32), vm((D, ALL), BF),
            vm((4, D, B), BF), vm((4, D, B), BF),
        ]
        + [vm((2 * D, B), BF)] * 5
        + [vm((D, B), BF)]
        + [vm((D, B), F32)] * 3
        + [vm((3, 2, 128, B), BF), vm((2, D, B), BF), vm((3, 2, D, 128), BF)]
        + [vm((4, 2, 528, B), BF)] * 2
        + [vm((2, 512, B), F32)]
        + chunks
        + chunks
        + [
            vm((2, D, ALL), BF), vm((6, 2, 256, ALL), BF), vm((4, D, B), BF), vm((D, ALL), BF),
            vm((D, 2 * B), F32), vm((4, D, ALL), BF), vm((4, F, ALL), BF), vm((2, 256, D), BF),
            vm((256, 2, D), BF), vm((D, ALL), BF), vm((D, ALL), BF), vm((8, ALL), F32),
            vm((4, D, B), BF), vm((D, 2 * B), F32),
        ]
        + [
            dma((5,)), dma((22,)), dma, dma((4,)), dma, dma, dma, dma, dma, dma,
            dma((6,)), dma((6, 16)), dma((6,)), dma((6,)), dma((6,)), dma((6,)), dma((6,)), dma((6,)),
            dma((6,)), dma((6,)), dma((6,)), dma((6,)), dma((4,)), dma, dma((4,)), dma((3,)),
        ]
    )


def on_device(regions, leaf_map, leaf_bond_weight, mid_weight, upper_weight, head_cotangent):
    anywhere = pl.BlockSpec(memory_space=pl.ANY)
    outs = pl.pallas_call(
        kernel,
        out_shape=(
            jax.ShapeDtypeStruct((4, F, D), BF),
            jax.ShapeDtypeStruct((D, D), BF),
            jax.ShapeDtypeStruct((256, 2, D), BF),
        ),
        in_specs=[pl.BlockSpec(memory_space=pltpu.SMEM)] + [anywhere] * 5,
        out_specs=(anywhere,) * 3,
        scratch_shapes=scratch(),
        compiler_params=pltpu.CompilerParams(
            collective_id=0, has_side_effects=True, vmem_limit_bytes=67000000
        ),
    )(
        leaf_map, regions.reshape(B * 16, F), leaf_bond_weight[0], mid_weight[0, 0],
        upper_weight[0], head_cotangent.T,
    )
    return (outs[0][None], outs[1][None, None], outs[2][None])


def solution(mesh):
    placed = (
        P("rep", "sub", None),
        P("sub"),
        P(("sub", "rep"), None, None, None),
        P("sub", "rep", None, None),
        P("sub", None, None, None),
        P("rep", "sub"),
    )
    return jax.shard_map(
        on_device,
        mesh=mesh,
        in_specs=placed,
        out_specs=(
            P(("sub", "rep"), None, None, None),
            P("sub", "rep", None, None),
            P("sub", "rep", None, None),
        ),
        check_vma=False,
    )
```

```python
import jax
import jax.numpy as jnp
from jax import lax
from jax.experimental import pallas as pl
from jax.experimental.pallas import tpu as pltpu
from jax.sharding import PartitionSpec as P

F32 = jnp.float32
BF = jnp.bfloat16
MESH = pl.DeviceIdType.MESH
EPSILON = 1e-06
VMEM_LIMIT = 58500000
D = 1024
F = 256
B = 128
REPS = 4
SUBS = 32
LEVELS = 5
ALL = REPS * B
WIDTH = [D // 2 ** (j + 1) for j in range(LEVELS)] + [D // SUBS]
COLUMN = [D - 2 * WIDTH[j] for j in range(LEVELS)] + [D - D // SUBS]
CHUNK = [2 * WIDTH[j] for j in range(LEVELS)] + [WIDTH[5]]
GROUP = [2 ** (j + 1) for j in range(LEVELS)] + [SUBS]


def nn(a, b):
    return jnp.dot(a, b, preferred_element_type=F32)


def nt(a, b):
    return lax.dot_general(a, b, (((1,), (1,)), ((), ())), preferred_element_type=F32)


def fold(values):
    return jnp.sum(values.reshape(values.shape[0] // 8, 8, values.shape[1]), axis=0)


def column_sum(values):
    return jnp.sum(values, axis=0, keepdims=True)


def factor_of(squares):
    return lax.rsqrt(column_sum(squares) * (1.0 / D) + EPSILON)


def at(index, size):
    return pl.ds(pl.multiple_of(index * size, size), size)


def lanes_of(i):
    return slice(i * B, (i + 1) * B)


OFFSET = (0, 1, 3, 2)
BACK = (0, 2, 1, 3)


STEP_SLOT = {(dy, dz): 4 * dy + dz for dy in range(4) for dz in range(4)}
EXTENT = ((1, 1), (1, 2), (1, 4), (2, 4), (4, 4))


def steps_of(level):
    ny, nz = EXTENT[level]
    steps = [(dy, dz) for dy in range(ny) for dz in range(nz) if dy or dz]
    return sorted(steps, key=lambda d: min(d[0], ny - d[0]) + min(d[1], nz - d[1]))


def others(f):
    p01 = f[0] * f[1]
    p23 = f[2] * f[3]
    return [f[1] * p23, f[0] * p23, p01 * f[3], p01 * f[2]]


def split_tile(row):
    high = row.astype(BF).astype(F32)
    index = lax.broadcasted_iota(jnp.int32, (16, B), 0)
    tile = jnp.where(index == 0, high, jnp.where(index == 1, row - high, 0.0))
    return tile.astype(BF)


def kernel(
    map_ref, reg_hbm, lw_hbm, mw_hbm, uw_hbm, cot_hbm,
    WT, LM, CR, XT, OU,
    R, Q, XS, XR, LW, LWT, MW, MWT, UW, WN, CF, FK, RL, MS, MR,
    A0, A1, A2, A3, A4, A5, UL, UR, JJ, GP, GB, WP, BO, BI,
    BS1, BS2, BS3, BR1, BR2, BR3,
    GX, AX, CS, LB, LO, H0, R0, PR, PM, WF, W4, UF, GH, PB,
    load_sem, local_sem, x1s, x1r, x2s, x2r, x3s, x3r, h0s, h0r, fs, fr, ff, fo, bs, br, bos, bis,
    axs, axr, aps, apr, gxs, gxr, gx0, gxt, pss, prs, cfs, cfr, w1s, w1r, w2s, w2r, w3s, w3r, w4s, w4r,
):
    A = [A0, A1, A2, A3, A4, A5]
    BS = [None, BS1, BS2, BS3]
    BR = [None, BR1, BR2, BR3]
    s = lax.axis_index("sub")
    p = lax.axis_index("rep")

    def to_rep(src, dst, send, recv, peer):
        pltpu.make_async_remote_copy(
            src_ref=src, dst_ref=dst, send_sem=send, recv_sem=recv,
            device_id={"rep": peer}, device_id_type=MESH,
        ).start()

    def to_sub(src, dst, send, recv, peer):
        pltpu.make_async_remote_copy(
            src_ref=src, dst_ref=dst, send_sem=send, recv_sem=recv,
            device_id={"sub": peer}, device_id_type=MESH,
        ).start()

    def await_bytes(ref, sem):
        pltpu.make_async_copy(ref, ref, sem).wait()

    c = lax.rem(s, 2)
    z = lax.rem(s // 2, 4)
    y = s // 8
    partner = s + 1 - 2 * c

    def upper_part(t):
        return pltpu.make_async_copy(uw_hbm.at[128 * t : 128 * (t + 1)], UW.at[t % 4], load_sem.at[4 + t % 4])

    loads = [
        pltpu.make_async_copy(src, dst, load_sem.at[i])
        for i, (src, dst) in enumerate([(reg_hbm, R), (lw_hbm, LW), (mw_hbm, MW), (cot_hbm, CF.at[y, z, c])])
    ]
    loads[0].start()
    loads[3].start()
    for t in range(4):
        upper_part(t).start()
    loads[1].start()
    loads[2].start()

    barrier = pltpu.get_barrier_semaphore()

    def greet_sub(i, carry):
        pl.semaphore_signal(
            barrier, inc=1, device_id={"sub": lax.rem(s + i, SUBS)}, device_id_type=MESH
        )
        return carry

    def greet_rep(i, carry):
        pl.semaphore_signal(
            barrier, inc=1, device_id={"rep": lax.rem(p + i, REPS)}, device_id_type=MESH
        )
        return carry

    lax.fori_loop(1, SUBS, greet_sub, 0)
    lax.fori_loop(1, REPS, greet_rep, 0)

    column = lax.broadcasted_iota(jnp.int32, (16, 256), 1)
    sample = lax.broadcasted_iota(jnp.int32, (16, 256), 0)
    for l in range(16):
        wanted = sample * 16 + map_ref[l]
        Q[16 * l : 16 * l + 16, :] = jnp.where(column == wanted, 1.0, 0.0).astype(BF)
    loads[0].wait()

    for q in range(8):
        got = nn(Q[...], R[256 * q : 256 * (q + 1), :]).astype(BF)
        for l in range(16):
            XS[l // 4, l % 4, 16 * q : 16 * q + 16, :] = got[16 * l : 16 * l + 16, :]
    pl.semaphore_wait(barrier, SUBS - 1 + REPS - 1)

    def source(i):
        return lax.rem(p + OFFSET[i], REPS)

    for i in range(1, REPS):
        peer = source(i)
        to_rep(XS.at[peer], XR.at[:, lanes_of(BACK[i]), :], x1s, x1r.at[BACK[i]], peer)
    own_slots = pltpu.make_async_copy(XS.at[p], XR.at[:, 0:B, :], local_sem.at[0])
    own_slots.start()

    for t in range(8):
        upper_part(t).wait()
        for q in range(4):
            rows = slice(128 * t + 32 * q, 128 * t + 32 * (q + 1))
            WN[:, rows, :] = jnp.swapaxes(UW[t % 4, 32 * q : 32 * (q + 1)], 0, 1)
        if t < 4:
            upper_part(t + 4).start()
    for side in range(2):
        for t in range(4):
            rows = slice(256 * t, 256 * (t + 1))
            WF[y, z, c, side, :, rows] = WN[side, rows, 896:1024].T[64:128, :]

    def chip(dy, dz):
        return (lax.rem(y + dy, 4) * 4 + lax.rem(z + dz, 4)) * 2 + c

    for k in range(1, 4):
        ref = WF.at[y, z, c, 0]
        to_sub(ref, ref, w1s, w1r.at[0], chip(k, 0))
        ref = WF.at[y, z, c, 1]
        to_sub(ref, ref, w1s, w1r.at[1], chip(0, k))
    for side in range(2):
        ref = WF.at[y, z, c, side]
        for way, step in ((0, 1), (1, 3)):
            to_sub(ref, ref, w2s, w2r.at[side, way], chip(0, step) if side == 0 else chip(step, 0))
    loads[3].wait()
    for k in range(1, 4):
        ref = CF.at[y, z, c]
        to_sub(ref, ref, cfs.at[0], cfr.at[0], chip(k, 0))

    def maps_to_neighbours():
        for side in range(2):
            await_bytes(WF.at[0:3, 0, 0, side], w1r.at[side])
            for k in range(1, 4):
                ref = WF.at[lax.rem(y + k, 4), z, c, 0] if side == 0 else WF.at[y, lax.rem(z + k, 4), c, 1]
                for way, step in ((0, 1), (1, 3)):
                    to_sub(ref, ref, w2s, w2r.at[side, way], chip(0, step) if side == 0 else chip(step, 0))
        await_bytes(CF.at[0:3, 0, 0], cfr.at[0])
        ref = CF.at[:, z, c]
        for k in range(1, 4):
            to_sub(ref, ref, cfs.at[1], cfr.at[1], chip(0, k))

    def maps_to_opposite():
        for side in range(2):
            for way, step in ((0, 1), (1, 3)):
                half = slice(2 * way, 2 * way + 2)
                if side == 0:
                    came = lax.rem(z + 4 - step, 4)
                    await_bytes(WF.at[:, came, c, 0], w2r.at[side, way])
                    ref = WF.at[half, came, c, 0]
                    to_sub(ref, ref, w3s, w3r.at[side, way], chip(0, step))
                else:
                    came = lax.rem(y + 4 - step, 4)
                    await_bytes(WF.at[came, :, c, 1], w2r.at[side, way])
                    ref = WF.at[came, half, c, 1]
                    to_sub(ref, ref, w3s, w3r.at[side, way], chip(step, 0))

    def maps_arrived():
        await_bytes(CF.at[:, 0:3, 0], cfr.at[1])
        to_sub(CF.at[:, :, c], CF.at[:, :, c], cfs.at[2], cfr.at[2], partner)
        for side in range(2):
            for way in range(2):
                await_bytes(WF.at[0:2, 0, 0, 0], w3r.at[side, way])

    def maps_to_partner(part):
        for row in part:
            to_sub(WF.at[row, :, c], WF.at[row, :, c], w4s, w4r, partner)

    GP[...] = jnp.zeros(GP.shape, BF)
    loads[1].wait()

    def turn_leaf(i, carry):
        k, t = i // 4, lax.rem(i, 4)
        LWT[k, at(t, 256), :] = LW[k, :, at(t, 256)].T
        return carry

    lax.fori_loop(0, 16, turn_leaf, 0)
    loads[2].wait()

    def turn_mid(i, carry):
        a, b = i // 4, lax.rem(i, 4)
        MWT[at(b, 256), at(a, 256)] = MW[at(a, 256), at(b, 256)].T
        return carry

    lax.fori_loop(0, 16, turn_mid, 0)

    def leaf_blocks(lanes):
        n = lanes.stop - lanes.start
        squares = jnp.zeros((8, n), F32)
        for t in range(4):
            rows = slice(256 * t, 256 * (t + 1))
            product = None
            for k in range(4):
                factor = 1.0 + nt(LWT[k, rows, :], XR[k, lanes, :])
                FK[k, rows, lanes] = factor.astype(BF)
                product = factor if product is None else product * factor
            LB[rows, 0:n] = product
            squares = squares + fold(product * product)
        r = factor_of(squares)
        RL[:, lanes] = jnp.broadcast_to(r, (8, n))
        for t in range(4):
            rows = slice(256 * t, 256 * (t + 1))
            LM[rows, lanes] = (LB[rows, 0:n] * r).astype(BF)
        for t in range(4):
            rows = slice(256 * t, 256 * (t + 1))
            value = nn(MWT[rows, :], LM[:, lanes]).astype(BF)
            for b in range(n // B):
                MS[lanes.start // B + b, rows, :] = value[:, lanes_of(b)]

    def turn_slots(lanes):
        for k in range(4):
            XT[k, :, lanes] = XR[k, lanes, :].T

    own_slots.wait()
    leaf_blocks(slice(0, B))
    own_mid = pltpu.make_async_copy(MS.at[0], MR.at[p], local_sem.at[1])
    own_mid.start()
    for t in range(8):
        rows = slice(128 * t, 128 * (t + 1))
        for side in range(2):
            WT[2 * side + t // 4, 0:960, 128 * (t % 4) : 128 * (t % 4 + 1)] = WN[side, rows, 0:960].T
    for level in (2, 3):
        size = CHUNK[level]
        col = min(COLUMN[level], 896)
        count = D // size
        for side in range(2):
            for q in range(count):
                to = (q % 2 * (count // 2) + q // 2) * size
                WP[level - 2, side, to : to + size, :] = WN[side, q * size : (q + 1) * size, col : col + 128]
    turn_slots(slice(0, B))
    for blocks in ((1, 2), (3,)):
        for i in blocks:
            await_bytes(XR.at[:, lanes_of(i), :], x1r.at[i])
        lanes = slice(blocks[0] * B, (blocks[-1] + 1) * B)
        leaf_blocks(lanes)
        for i in blocks:
            to_rep(MS.at[i], MR.at[p], x2s, x2r, source(i))
        turn_slots(lanes)
        if len(blocks) == 2:
            maps_to_neighbours()

    maps_to_opposite()
    own_mid.wait()
    await_bytes(MR.at[0:3], x2r)
    for t in range(8):
        rows = slice(128 * t, 128 * (t + 1))
        product = 1.0 + MR[0, rows, :].astype(F32)
        for k in range(1, 4):
            product = product * (1.0 + MR[k, rows, :].astype(F32))
        A0[pl.ds(pl.multiple_of(c * D + t * 128, 128), 128), :] = product.astype(BF)

    own = slice(0, B)

    def spread(level, me, block):
        ref = A[level].at[at(me, block), :]
        to_sub(ref, ref, fs.at[level], fo.at[level], partner)

        for step in reversed(steps_of(level)):
            to_sub(ref, ref, fs.at[level], fr.at[level, STEP_SLOT[step]], chip_of(level, step, 1))

    def chip_of(level, step, sign):
        ny, nz = EXTENT[level]
        yy = y // ny * ny + lax.rem(lax.rem(y, ny) + (step[0] if sign > 0 else ny - step[0]), ny)
        zz = z // nz * nz + lax.rem(lax.rem(z, nz) + (step[1] if sign > 0 else nz - step[1]), nz)
        return (yy * 4 + zz) * 2 + c

    def collect(level, me, block):
        half = GROUP[level] // 2

        for step in steps_of(level):
            ref = A[level].at[at(chip_of(level, step, -1) - s + me, block), :]
            await_bytes(ref, fr.at[level, STEP_SLOT[step]])
            to_sub(ref, ref, ff.at[level], fo.at[level], partner)
        await_bytes(A[level].at[0 : half * block], fo.at[level])

    def share_rows(level):
        for i in range(1, REPS):
            if level < LEVELS:
                rows = pl.ds(pl.multiple_of(c * D + source(i) * 256, 256), 256)
                dst = AX.at[level, c, :, lanes_of(BACK[i])]
            else:
                rows = pl.ds(pl.multiple_of(source(i) * 256 + c * 128, 128), 128)
                dst = AX.at[level, 0, at(c, 128), lanes_of(BACK[i])]
            to_rep(A[level].at[rows, :], dst, axs.at[level], axr.at[level], source(i))
        for side in range(2 if level < LEVELS else 1):
            rows = pl.ds(pl.multiple_of(side * D + p * 256, 256), 256)
            copy = pltpu.make_async_copy(
                A[level].at[rows, :], AX.at[level, side, :, own], local_sem.at[2 + 2 * level + side]
            )
            copy.start()
            kept.append(copy)

    def pass_rows(level):
        if level == 0:
            await_bytes(H0.at[:, 0 : 3 * B], h0r)
            for copy in message_copies:
                copy.wait()
            src, dst = H0.at[at(p, 256), :], AX.at[0, c]
        elif level < LEVELS:
            await_bytes(AX.at[level, 0, :, 0 : 3 * B], axr.at[level])
            src = dst = AX.at[level, c, :, B:ALL]
        else:
            await_bytes(AX.at[level, 0, 0:128, 0 : 3 * B], axr.at[level])
            src = dst = AX.at[level, 0, at(c, 128), B:ALL]
        to_sub(src, dst, aps.at[level], apr.at[level], partner)

    def passed(level):
        if level == 0:
            return AX.at[0, 0]
        if level < LEVELS:
            return AX.at[level, 0, :, 0 : 3 * B]
        return AX.at[level, 0, 0:128, 0 : 3 * B]

    kept = []

    def squares_of(ref, start, lanes=slice(0, B)):
        total = jnp.zeros((8, B), F32)
        for t in range(4):
            values = ref[start + 256 * t : start + 256 * (t + 1), lanes].astype(F32)
            total = total + fold(values * values)
        return total

    spread(0, c, D)
    message = A0.at[at(c, D), :]

    def leave_one(t, carry):
        rows = at(t, 128)
        rest = others([1.0 + MR[k, rows, :].astype(F32) for k in range(4)])
        for k in range(4):
            CS[k, rows, :] = rest[k].astype(BF)
        return carry

    lax.fori_loop(0, 8, leave_one, 0)

    for i in range(1, REPS):
        to_rep(message, H0.at[:, lanes_of(BACK[i])], h0s, h0r, source(i))
    for i in range(1, REPS):
        to_rep(CS.at[source(i)], LO.at[:, lanes_of(BACK[i])], x3s, x3r, source(i))
    message_copies = [
        pltpu.make_async_copy(CS.at[p], LO.at[:, own], local_sem.at[20]),
        pltpu.make_async_copy(message, H0.at[:, own], local_sem.at[21]),
    ]
    for copy in message_copies:
        copy.start()
    scales = []
    for level in range(LEVELS - 1):
        group, w, col = GROUP[level], WIDTH[level], COLUMN[level]
        collect(level, lax.rem(s, group), 2 * D // group)
        if level:
            share_rows(level)
        left = factor_of(squares_of(A[level], 0))
        right = factor_of(squares_of(A[level], D))
        scales.append((left, right))
        me = lax.rem(s, GROUP[level + 1])
        size = min(w, 256)
        for t in range(w // size):
            rows = slice(col + t * size, col + (t + 1) * size)
            ul = (nn(WT[0, rows, :], A[level][0:512, :]) + nn(WT[1, rows, :], A[level][512:D, :])) * left
            ur = (nn(WT[2, rows, :], A[level][D:1536, :]) + nn(WT[3, rows, :], A[level][1536 : 2 * D, :])) * right
            joined = (1.0 + ul) * (1.0 + ur)
            UL[rows, :] = ul
            UR[rows, :] = ur
            JJ[rows, :] = joined
            A[level + 1][pl.ds(pl.multiple_of(me * w + t * size, size), size), :] = joined.astype(BF)
        spread(level + 1, me, w)
        if level == 1:
            maps_arrived()
            maps_to_partner((0, 1))
        if level == 2:
            maps_to_partner((2, 3))

    def share_grads(level):
        w, col = WIDTH[level], COLUMN[level]
        for i in range(1, REPS):
            to_rep(
                GX.at[:, col : col + w, own], GX.at[:, col : col + w, lanes_of(BACK[i])],
                gxs.at[level], gxr.at[level], source(i),
            )

    def share_last_grads():
        for i in (1, 2):
            for side in (i - 1, 2 - i):
                to_rep(
                    GX.at[side, 0:512, own], GX.at[side, 0:512, lanes_of(BACK[i])],
                    gxs.at[0], gx0.at[BACK[i], side], source(i),
                )

    def relay_last_grads():
        for i in (1, 2):
            side = i - 1
            ref = GX.at[side, 0:512, lanes_of(BACK[i])]
            await_bytes(ref, gx0.at[BACK[i], side])
            to_rep(ref, GX.at[side, 0:512, lanes_of(3)], gxt, gx0.at[3, side], source(i))

    def scatter(level, me):
        at_chip = me // 2
        for step in reversed(steps_of(level)):
            peer = chip_of(level, step, 1)
            d = at_chip + (peer - s) // 2
            to_sub(BS[level].at[d], BR[level].at[at_chip], bs.at[level], br.at[level], peer)
        copy = pltpu.make_async_copy(
            BS[level].at[at_chip], BR[level].at[at_chip], local_sem.at[14 + level]
        )
        copy.start()
        return copy

    await_bytes(WF.at[:, :, 0], w4r)
    mine = s // 16
    block = lax.rem(s, 16)
    for g in range(4):
        cols = slice(256 * g, 256 * (g + 1))
        lanes = pl.ds(pl.multiple_of(block // 2 * 128, 128), 128)
        W4[:, cols] = WF[g, :, :, mine, 0:32, lanes].reshape(256, 128).T
    collect(4, s, 2 * D // SUBS)
    share_rows(4)
    left = factor_of(squares_of(A4, 0))
    right = factor_of(squares_of(A4, D))
    scales.append((left, right))
    squares = jnp.zeros((8, B), F32)
    for g in range(4):
        rows = slice(256 * g, 256 * (g + 1))
        ul = nn(WF[g, :, :, 0, 0:32, :].reshape(256, D), A4[0:D, :]) * left
        ur = nn(WF[g, :, :, 1, 0:32, :].reshape(256, D), A4[D : 2 * D, :]) * right
        joined = ((1.0 + ul) * (1.0 + ur)).astype(BF)
        UF[0, rows, :] = ul
        UF[1, rows, :] = ur
        A5[rows, :] = joined
        squares = squares + fold(joined.astype(F32) * joined.astype(F32))
    root_scale = factor_of(squares)
    share_rows(5)
    await_bytes(CF.at[:, :, 0], cfr.at[2])
    for g in range(4):
        rows = slice(256 * g, 256 * (g + 1))
        za = nn(WF[g, :, :, 0, 32:64, :].reshape(256, D), A5[...]) * root_scale
        zb = nn(WF[g, :, :, 1, 32:64, :].reshape(256, D), A5[...]) * root_scale
        sigma = 1.0 / (1.0 + jnp.exp(-zb))
        cotangent = CF[g].reshape(256, B)
        GH[0, rows, :] = (cotangent * sigma).astype(BF)
        GH[1, rows, :] = (cotangent * za * sigma * (1.0 - sigma)).astype(BF)
    block_rows = pl.ds(pl.multiple_of(s * 32, 32), 32)
    for side in range(2):
        GX[side, 992:1024, own] = (GH[side, block_rows, :].astype(F32) * root_scale).astype(BF)
    share_grads(5)
    turned = [GH[side].T for side in range(2)]
    total = jnp.zeros((8, B), F32)
    for t in range(4):
        rows = slice(256 * t, 256 * (t + 1))
        part = None
        for side in range(2):
            term = nn(turned[side], WF[:, :, :, side, 32:64, rows].reshape(D, 256))
            part = term if part is None else part + term
        part = part.T
        PB[rows, :] = part
        total = total + fold(part * A5[rows, :].astype(F32))
    mean = column_sum(total) * (1.0 / D)
    shift = root_scale * root_scale * mean
    dl = jnp.zeros((8, B), F32)
    dr = jnp.zeros((8, B), F32)
    for t in range(8):
        rows = slice(128 * t, 128 * (t + 1))
        ul, ur = UF[0, rows, :], UF[1, rows, :]
        v = root_scale * (PB[rows, :] - (1.0 + ul) * (1.0 + ur) * shift)
        gl = (v * (1.0 + ur)).astype(BF)
        gr = (v * (1.0 + ul)).astype(BF)
        GH[0, rows, :] = gl
        GH[1, rows, :] = gr
        dl = dl + fold(gl.astype(F32) * ul)
        dr = dr + fold(gr.astype(F32) * ur)
    root_mean = jnp.where(mine == 1, column_sum(dr), column_sum(dl)) * (1.0 / D)
    part_rows = pl.ds(pl.multiple_of(lax.rem(block, 2) * 64, 64), 64)
    PB[0:64, :] = nn(W4[part_rows, :], GH[mine])
    for side in range(2):
        GX[side, 960:992, own] = (GH[side, block_rows, :].astype(F32) * scales[4][side]).astype(BF)
    share_grads(4)

    def gathered(level, rows):
        if level == LEVELS - 1:
            return PB[rows, :]
        group = BR[level].shape[0]
        total = BR[level][0, rows, :].astype(F32)
        for g in range(1, group):
            total = total + BR[level][g, rows, :].astype(F32)
        return total

    def await_chunks(level, copy):
        if level == LEVELS - 1:
            return root_mean
        copy.wait()
        await_bytes(BR[level].at[0 : BR[level].shape[0] - 1], br.at[level])
        size = CHUNK[level]
        return column_sum(gathered(level, slice(size, size + 16))) * (1.0 / D)

    own_chunk = None
    for level in reversed(range(LEVELS - 1)):
        group, w, col = GROUP[level], WIDTH[level], COLUMN[level]
        mean = await_chunks(level + 1, own_chunk)
        side_of = lax.rem(s // GROUP[level], 2)
        r = jnp.where(side_of == 1, scales[level + 1][1], scales[level + 1][0])
        left, right = scales[level]
        size = min(w, 64)

        def node_back(t, carry):
            dl, dr = carry
            rows = pl.ds(pl.multiple_of(col + t * size, size), size)
            total = gathered(level + 1, pl.ds(pl.multiple_of(t * size, size), size))
            ul, ur = UL[rows, :], UR[rows, :]
            v = r * (total - JJ[rows, :] * (r * mean))
            gl = v * (1.0 + ur)
            gr = v * (1.0 + ul)
            GX[0, rows, own] = (gl * left).astype(BF)
            GX[1, rows, own] = (gr * right).astype(BF)
            if level == 0:
                return carry
            gl = gl.astype(BF)
            gr = gr.astype(BF)
            if level < 3:
                near = pl.ds(pl.multiple_of(col - 512 + t * size, size), size)
                GB[0, near, :] = gl
                GB[1, near, :] = gr
            else:
                GP[level - 3, 0, col - 896 : col - 896 + w, :] = gl
                GP[level - 3, 1, col - 896 : col - 896 + w, :] = gr
            return dl + fold(gl.astype(F32) * ul), dr + fold(gr.astype(F32) * ur)

        zero = jnp.zeros((8, B), F32)
        dl, dr = lax.fori_loop(0, w // size, node_back, (zero, zero))
        if level == 0:
            share_last_grads()
            break
        chunk = CHUNK[level]
        dots = [column_sum(dl), column_sum(dr)]

        def half_sums(side, parity):
            rows = pl.ds(pl.multiple_of(parity * 512, 512), 512)
            if level == 1:
                return nn(WN[side, rows, col : col + w], GB[side, col - 512 : col - 512 + w, :])
            if level == 2:
                return nn(WP[0, side, rows, :], GB[side, col - 512 : col - 512 + w, :])
            return nn(WP[level - 2, side, rows, :], GP[level - 3, side])

        for side in range(2):
            BO[level - 1, side, 0:512, :] = half_sums(side, 1 - c).astype(BF)
            BO[level - 1, side, 512:528, :] = split_tile(dots[side])
        to_sub(BO.at[level - 1], BI.at[level - 1], bos.at[level], bis.at[level], partner)
        for side in range(2):
            LB[side * 512 : (side + 1) * 512, 0:B] = half_sums(side, c)
        await_bytes(BI.at[level - 1], bis.at[level])
        quarter = group // 4
        for side in range(2):
            tile = split_tile(dots[side] + column_sum(BI[level - 1, side, 512:528, :].astype(F32)))
            chunks = slice(side * quarter, (side + 1) * quarter)
            value = (LB[side * 512 : (side + 1) * 512, 0:B] + BI[level - 1, side, 0:512, :].astype(F32)).astype(BF)
            BS[level][chunks, 0:chunk, :] = value.reshape(quarter, chunk, B)
            BS[level][chunks, chunk : chunk + 16, :] = jnp.broadcast_to(tile[None], (quarter, 16, B))
        own_chunk = scatter(level, lax.rem(s, group))
        if level > 1:
            share_grads(level)
        for done in {3: (0, 1, 2), 2: (3, 4), 1: (5,)}[level]:
            pass_rows(done)

    await_bytes(MS.at[0:3], x2s)

    def partial_sums(blocks):
        for i in blocks:
            for side in {0: (), 1: (0,), 2: (1,), 3: (0, 1)}[i]:
                await_bytes(GX.at[side, 0:512, lanes_of(i)], gx0.at[i, side])
        lanes = slice(blocks[0] * B, (blocks[-1] + 1) * B)
        for t in range(4):
            rows = slice(256 * t, 256 * (t + 1))
            value = nn(WN[1 - c, rows, 0:512], GX[1 - c, 0:512, lanes]).astype(BF)
            for b, i in enumerate(blocks):
                MS[i, rows, :] = value[:, lanes_of(b)]
        for i in blocks:
            to_sub(MS.at[i], PR.at[i], pss, prs.at[i], partner)
        for t in range(4):
            rows = slice(256 * t, 256 * (t + 1))
            PM[rows, 0 : B * len(blocks)] = nn(WN[c, rows, 0:512], GX[c, 0:512, lanes])

    partial_sums((0,))

    await_bytes(LO.at[:, 0 : 3 * B], x3r)
    for i in range(REPS):
        R0[:, lanes_of(i)] = jnp.broadcast_to(factor_of(squares_of(H0, 0, lanes_of(i))), (8, B))

    def leaf_back(blocks):
        lanes = slice(blocks[0] * B, (blocks[-1] + 1) * B)
        n = B * len(blocks)
        for i in blocks:
            await_bytes(PR.at[i], prs.at[i])
        for b, i in enumerate(blocks):
            part = lanes_of(b)
            total = jnp.zeros((8, B), F32)
            for t in range(8):
                rows = slice(128 * t, 128 * (t + 1))
                value = PM[rows, part] + PR[i, rows, :].astype(F32)
                PM[rows, part] = value
                total = total + fold(value * H0[rows, lanes_of(i)].astype(F32))
            scale0 = R0[0:1, lanes_of(i)]
            shift = scale0 * scale0 * (column_sum(total) * (1.0 / D))
            for t in range(8):
                rows = slice(128 * t, 128 * (t + 1))
                v = PM[rows, part] - H0[rows, lanes_of(i)].astype(F32) * shift
                CR[rows, lanes_of(i)] = (v * LO[rows, lanes_of(i)].astype(F32)).astype(BF)
        total = jnp.zeros((8, n), F32)
        for t in range(4):
            rows = slice(256 * t, 256 * (t + 1))
            value = nn(MW[rows, :], CR[:, lanes])
            LB[rows, 0:n] = value
            total = total + fold(value * LM[rows, lanes].astype(F32))
        mean = column_sum(total) * (1.0 / D)
        r = RL[0:1, lanes]
        for t in range(16):
            rows = slice(64 * t, 64 * (t + 1))
            v = r * (LB[rows, 0:n] - LM[rows, lanes].astype(F32) * mean)
            rest = others([FK[k, rows, lanes].astype(F32) for k in range(4)])
            for k in range(4):
                WT[k, rows, lanes] = (v * rest[k]).astype(BF)

    def await_grads(level):
        w, col = WIDTH[level], COLUMN[level]
        await_bytes(GX.at[:, col : col + w, 0 : 3 * B], gxr.at[level])

    leaf_back((0,))
    relay_last_grads()
    share_grads(1)
    partial_sums((1, 2))

    for copy in kept:
        copy.wait()
    for level in range(LEVELS + 1):
        await_bytes(passed(level), apr.at[level])
    for level in (5, 4, 3):
        await_grads(level)
    lane = lax.broadcasted_iota(jnp.int32, (256, 128), 1)
    for side in range(2):
        grads = GX[side, 896:1024, :]
        g3 = nt(AX[3, side], grads)
        g4 = nt(AX[4, side], grads)
        g5 = nt(AX[5, 0], grads)
        OU[side, :, 896:1024] = jnp.where(lane < 64, g3, jnp.where(lane < 96, g4, g5)).astype(BF)

    def upper_gradient(level):
        await_grads(level)
        w, col = WIDTH[level], COLUMN[level]
        for side in range(2):
            OU[side, :, col : col + w] = nt(AX[level, side], GX[side, col : col + w, :]).astype(BF)

    upper_gradient(2)

    leaf_back((1, 2))
    partial_sums((3,))

    rows = at(p, 256)
    OU[c, :, 0:512] = nt(H0[rows, :], GX[c, 0:512, :]).astype(BF)
    OU[1 - c, :, 0:512] = nt(AX[0, 1 - c], GX[1 - c, 0:512, :]).astype(BF)

    leaf_back((3,))

    upper_gradient(1)

    await_bytes(XS.at[0:3], x1s)
    await_bytes(CS.at[0:3], x3s)
    await_bytes(H0.at[:, 0 : 3 * B], h0s)
    await_bytes(MS, pss)
    for level in range(1, LEVELS - 1):
        await_bytes(BO.at[level - 1], bos.at[level])
    await_bytes(CF.at[0:3, 0, 0], cfs.at[0])
    await_bytes(CF.at[0:3, :, 0], cfs.at[1])
    await_bytes(CF.at[:, :, 0], cfs.at[2])
    await_bytes(WF.at[0:3, 0, 0], w1s)
    await_bytes(WF.at[:, :, 0, 0], w2s)
    await_bytes(WF.at[0:2, :, 0, 0], w3s)
    await_bytes(WF.at[:, :, 0], w4s)
    for level in range(LEVELS + 1):
        if level < LEVELS:
            half = GROUP[level] // 2
            block = A[level].shape[0] // GROUP[level]
            await_bytes(A[level].at[0 : half * block], fs.at[level])
            if half > 1:
                await_bytes(A[level].at[0 : (half - 1) * block], ff.at[level])
        if 0 < level < LEVELS - 1:
            await_bytes(BS[level].at[0 : BS[level].shape[0] - 1], bs.at[level])
        if level:
            await_bytes(passed(level), axs.at[level])
            w, col = WIDTH[level], COLUMN[level]
            await_bytes(GX.at[:, col : col + w, 0 : 3 * B], gxs.at[level])
        await_bytes(passed(level), aps.at[level])
    await_bytes(GX.at[:, 0:512, 0 : 2 * B], gxs.at[0])
    await_bytes(GX.at[:, 0:512, own], gxt)


def scratch():
    vm = pltpu.VMEM
    dma = pltpu.SemaphoreType.DMA
    chunks = [vm((GROUP[j] // 2, CHUNK[j] + 16, B), BF) for j in range(1, LEVELS - 1)]
    return (
        [
            vm((2048, F), BF), vm((256, 256), BF), vm((4, 4, B, F), BF), vm((4, ALL, F), BF),
            vm((4, F, D), BF), vm((4, D, F), BF), vm((D, D), BF), vm((D, D), BF),
            vm((4, 128, 2, D), BF), vm((2, D, D), BF), vm((4, 4, 2, 32, B), F32),
            vm((4, D, ALL), BF), vm((8, ALL), F32),
            vm((4, D, B), BF), vm((4, D, B), BF),
        ]
        + [vm((2 * D, B), BF)] * 5
        + [vm((D, B), BF)]
        + [vm((D, B), F32)] * 3
        + [vm((1, 2, 128, B), BF), vm((2, 384, B), BF), vm((2, 2, D, 128), BF)]
        + [vm((3, 2, 528, B), BF)] * 2
        + chunks
        + chunks
        + [
            vm((2, D, ALL), BF), vm((6, 2, 256, ALL), BF), vm((4, D, B), BF),
            vm((D, 2 * B), F32),
            vm((D, ALL), BF), vm((D, ALL), BF), vm((8, ALL), F32),
            vm((4, D, B), BF), vm((D, 2 * B), F32),
            vm((4, 4, 2, 2, 64, D), BF), vm((128, D), BF), vm((2, D, B), F32), vm((2, D, B), BF), vm((D, B), F32),
        ]
        + [
            dma((8,)), dma((22,)), dma, dma((4,)), dma, dma, dma, dma, dma, dma,
            dma((6,)), dma((6, 16)), dma((6,)), dma((6,)), dma((6,)), dma((6,)), dma((6,)), dma((6,)),
            dma((6,)), dma((6,)), dma((6,)), dma((6,)), dma((6,)), dma((6,)), dma((4, 2)), dma, dma, dma((4,)),
            dma((3,)), dma((3,)), dma, dma((2,)), dma, dma((2, 2)), dma, dma((2, 2)), dma, dma,
        ]
    )


def gradients(CT, LM, CR, XT, OU, lg_hbm, mg_hbm, ug_hbm, LW, OM, OI, sem):
    copies = []

    def out(src, dst):
        copies.append(pltpu.make_async_copy(src, dst, sem.at[len(copies)]))
        copies[-1].start()

    for t in range(4):
        rows = slice(64 * t, 64 * (t + 1))
        for side in range(2):
            OI[rows, side, :] = OU[side, rows, :]
    out(OI, ug_hbm)
    for k in range(4):
        LW[k] = nt(XT[k], CT[k]).astype(BF)
        out(LW.at[k], lg_hbm.at[k])
    for t in range(4):
        rows = slice(256 * t, 256 * (t + 1))
        OM[rows, :] = nt(LM[rows, :], CR[...]).astype(BF)
        out(OM.at[rows], mg_hbm.at[rows])
    for copy in copies:
        copy.wait()


def on_device(regions, leaf_map, leaf_bond_weight, mid_weight, upper_weight, head_cotangent):
    anywhere = pl.BlockSpec(memory_space=pl.ANY)
    local = pl.BlockSpec(memory_space=pltpu.VMEM)
    kept = pl.pallas_call(
        kernel,
        out_shape=(
            pltpu.VMEM((4, D, ALL), BF),
            pltpu.VMEM((D, ALL), BF),
            pltpu.VMEM((D, ALL), BF),
            pltpu.VMEM((4, F, ALL), BF),
            pltpu.VMEM((2, 256, D), BF),
        ),
        in_specs=[pl.BlockSpec(memory_space=pltpu.SMEM)] + [anywhere] * 5,
        out_specs=(local,) * 5,
        scratch_shapes=scratch(),
        compiler_params=pltpu.CompilerParams(
            collective_id=0, has_side_effects=True, vmem_limit_bytes=VMEM_LIMIT
        ),
    )(
        leaf_map, regions.reshape(B * 16, F), leaf_bond_weight[0], mid_weight[0, 0],
        upper_weight[0], head_cotangent.T,
    )
    kept = [pltpu.with_memory_space_constraint(array, pltpu.VMEM) for array in kept]
    outs = pl.pallas_call(
        gradients,
        out_shape=(
            jax.ShapeDtypeStruct((4, F, D), BF),
            jax.ShapeDtypeStruct((D, D), BF),
            jax.ShapeDtypeStruct((256, 2, D), BF),
        ),
        in_specs=[local] * 5,
        out_specs=(anywhere,) * 3,
        scratch_shapes=[
            pltpu.VMEM((4, F, D), BF), pltpu.VMEM((D, D), BF), pltpu.VMEM((256, 2, D), BF),
            pltpu.SemaphoreType.DMA((9,)),
        ],
        compiler_params=pltpu.CompilerParams(vmem_limit_bytes=32000000),
    )(*kept)
    return (outs[0][None], outs[1][None, None], outs[2][None])


def solution(mesh):
    placed = (
        P("rep", "sub", None),
        P("sub"),
        P(("sub", "rep"), None, None, None),
        P("sub", "rep", None, None),
        P("sub", None, None, None),
        P("rep", "sub"),
    )
    return jax.shard_map(
        on_device,
        mesh=mesh,
        in_specs=placed,
        out_specs=(
            P(("sub", "rep"), None, None, None),
            P("sub", "rep", None, None),
            P("sub", "rep", None, None),
        ),
        check_vma=False,
    )
```

```python
import jax
import jax.numpy as jnp
from jax import lax
from jax.experimental import pallas as pl
from jax.experimental.pallas import tpu as pltpu
from jax.sharding import PartitionSpec as P

F32 = jnp.float32
BF = jnp.bfloat16
MESH = pl.DeviceIdType.MESH
EPSILON = 1e-06
VMEM_LIMIT = 58500000
D = 1024
F = 256
B = 128
REPS = 4
SUBS = 32
LEVELS = 5
ALL = REPS * B
WIDTH = [D // 2 ** (j + 1) for j in range(LEVELS)] + [D // SUBS]
COLUMN = [D - 2 * WIDTH[j] for j in range(LEVELS)] + [D - D // SUBS]
CHUNK = [2 * WIDTH[j] for j in range(LEVELS)] + [WIDTH[5]]
GROUP = [2 ** (j + 1) for j in range(LEVELS)] + [SUBS]


def nn(a, b):
    return jnp.dot(a, b, preferred_element_type=F32)


def nt(a, b):
    return lax.dot_general(a, b, (((1,), (1,)), ((), ())), preferred_element_type=F32)


def fold(values):
    return jnp.sum(values.reshape(values.shape[0] // 8, 8, values.shape[1]), axis=0)


def column_sum(values):
    return jnp.sum(values, axis=0, keepdims=True)


def factor_of(squares):
    return lax.rsqrt(column_sum(squares) * (1.0 / D) + EPSILON)


def at(index, size):
    return pl.ds(pl.multiple_of(index * size, size), size)


def lanes_of(i):
    return slice(i * B, (i + 1) * B)


OFFSET = (0, 1, 3, 2)
BACK = (0, 2, 1, 3)


STEP_SLOT = {(dy, dz): 4 * dy + dz for dy in range(4) for dz in range(4)}
EXTENT = ((1, 1), (1, 2), (1, 4), (2, 4), (4, 4))


def steps_of(level):
    ny, nz = EXTENT[level]
    steps = [(dy, dz) for dy in range(ny) for dz in range(nz) if dy or dz]
    return sorted(steps, key=lambda d: min(d[0], ny - d[0]) + min(d[1], nz - d[1]))


def others(f):
    p01 = f[0] * f[1]
    p23 = f[2] * f[3]
    return [f[1] * p23, f[0] * p23, p01 * f[3], p01 * f[2]]


def split_tile(row):
    high = row.astype(BF).astype(F32)
    index = lax.broadcasted_iota(jnp.int32, (16, B), 0)
    tile = jnp.where(index == 0, high, jnp.where(index == 1, row - high, 0.0))
    return tile.astype(BF)


def kernel(
    map_ref, reg_hbm, lw_hbm, mw_hbm, uw_hbm, cot_hbm,
    WT, LM, CR, XT, OU,
    R, Q, XS, XR, LW, LWT, MW, MWT, UW, WN, CF, FK, RL, MS, MR,
    A0, A1, A2, A3, A4, A5, UL, UR, JJ, GP, GB, WP, BO, BI,
    BS1, BS2, BS3, BR1, BR2, BR3,
    GX, AX, CS, LB, LO, H0, R0, PR, PM, WF, W4, UF, GH, PB,
    load_sem, local_sem, x1s, x1r, x2s, x2r, x3s, x3r, h0s, h0r, fs, fr, ff, fo, bs, br, bos, bis,
    axs, axr, aps, apr, gxs, gxr, gx0, gxt, pss, prs, cfs, cfr, w1s, w1r, w2s, w2r, w3s, w3r, w4s, w4r,
):
    A = [A0, A1, A2, A3, A4, A5]
    BS = [None, BS1, BS2, BS3]
    BR = [None, BR1, BR2, BR3]
    s = lax.axis_index("sub")
    p = lax.axis_index("rep")

    def to_rep(src, dst, send, recv, peer):
        pltpu.make_async_remote_copy(
            src_ref=src, dst_ref=dst, send_sem=send, recv_sem=recv,
            device_id={"rep": peer}, device_id_type=MESH,
        ).start()

    def to_sub(src, dst, send, recv, peer):
        pltpu.make_async_remote_copy(
            src_ref=src, dst_ref=dst, send_sem=send, recv_sem=recv,
            device_id={"sub": peer}, device_id_type=MESH,
        ).start()

    def await_bytes(ref, sem):
        pltpu.make_async_copy(ref, ref, sem).wait()

    c = lax.rem(s, 2)
    z = lax.rem(s // 2, 4)
    y = s // 8
    partner = s + 1 - 2 * c

    def upper_part(t):
        return pltpu.make_async_copy(uw_hbm.at[128 * t : 128 * (t + 1)], UW.at[t % 4], load_sem.at[4 + t % 4])

    loads = [
        pltpu.make_async_copy(src, dst, load_sem.at[i])
        for i, (src, dst) in enumerate([(reg_hbm, R), (lw_hbm, LW), (mw_hbm, MW), (cot_hbm, CF.at[y, z, c])])
    ]
    loads[0].start()
    loads[3].start()
    for t in range(4):
        upper_part(t).start()
    loads[1].start()
    loads[2].start()

    barrier = pltpu.get_barrier_semaphore()

    def chip(dy, dz):
        return (lax.rem(y + dy, 4) * 4 + lax.rem(z + dz, 4)) * 2 + c

    far_first = list(reversed(steps_of(LEVELS - 1)))
    for dy, dz in far_first:
        pl.semaphore_signal(barrier, inc=1, device_id={"sub": chip(dy, dz)}, device_id_type=MESH)
    for i in (2, 1, 3):
        pl.semaphore_signal(
            barrier, inc=1, device_id={"rep": lax.rem(p + i, REPS)}, device_id_type=MESH
        )
    pl.semaphore_signal(barrier, inc=1, device_id={"sub": partner}, device_id_type=MESH)

    column = lax.broadcasted_iota(jnp.int32, (16, 256), 1)
    sample = lax.broadcasted_iota(jnp.int32, (16, 256), 0)
    for l in range(16):
        wanted = sample * 16 + map_ref[l]
        Q[16 * l : 16 * l + 16, :] = jnp.where(column == wanted, 1.0, 0.0).astype(BF)
    loads[0].wait()

    for q in range(8):
        got = nn(Q[...], R[256 * q : 256 * (q + 1), :]).astype(BF)
        for l in range(16):
            XS[l // 4, l % 4, 16 * q : 16 * q + 16, :] = got[16 * l : 16 * l + 16, :]
    pl.semaphore_wait(barrier, len(far_first) + 1 + REPS - 1)

    def source(i):
        return lax.rem(p + OFFSET[i], REPS)

    for i in range(1, REPS):
        peer = source(i)
        to_rep(XS.at[peer], XR.at[:, lanes_of(BACK[i]), :], x1s, x1r.at[BACK[i]], peer)
    own_slots = pltpu.make_async_copy(XS.at[p], XR.at[:, 0:B, :], local_sem.at[0])
    own_slots.start()

    for t in range(8):
        upper_part(t).wait()
        for q in range(4):
            rows = slice(128 * t + 32 * q, 128 * t + 32 * (q + 1))
            WN[:, rows, :] = jnp.swapaxes(UW[t % 4, 32 * q : 32 * (q + 1)], 0, 1)
        if t < 4:
            upper_part(t + 4).start()
    for side in range(2):
        for t in range(4):
            rows = slice(256 * t, 256 * (t + 1))
            WF[y, z, c, side, :, rows] = WN[side, rows, 896:1024].T[64:128, :]

    for k in range(1, 4):
        ref = WF.at[y, z, c, 0]
        to_sub(ref, ref, w1s, w1r.at[0], chip(k, 0))
        ref = WF.at[y, z, c, 1]
        to_sub(ref, ref, w1s, w1r.at[1], chip(0, k))
    for side in range(2):
        ref = WF.at[y, z, c, side]
        for way, step in ((0, 1), (1, 3)):
            to_sub(ref, ref, w2s, w2r.at[side, way], chip(0, step) if side == 0 else chip(step, 0))
    loads[3].wait()
    for k in range(1, 4):
        ref = CF.at[y, z, c]
        to_sub(ref, ref, cfs.at[0], cfr.at[0], chip(k, 0))

    def maps_to_neighbours():
        for side in range(2):
            await_bytes(WF.at[0:3, 0, 0, side], w1r.at[side])
            for k in range(1, 4):
                ref = WF.at[lax.rem(y + k, 4), z, c, 0] if side == 0 else WF.at[y, lax.rem(z + k, 4), c, 1]
                for way, step in ((0, 1), (1, 3)):
                    to_sub(ref, ref, w2s, w2r.at[side, way], chip(0, step) if side == 0 else chip(step, 0))
        await_bytes(CF.at[0:3, 0, 0], cfr.at[0])
        ref = CF.at[:, z, c]
        for k in range(1, 4):
            to_sub(ref, ref, cfs.at[1], cfr.at[1], chip(0, k))

    def maps_to_opposite():
        for side in range(2):
            for way, step in ((0, 1), (1, 3)):
                half = slice(2 * way, 2 * way + 2)
                if side == 0:
                    came = lax.rem(z + 4 - step, 4)
                    await_bytes(WF.at[:, came, c, 0], w2r.at[side, way])
                    ref = WF.at[half, came, c, 0]
                    to_sub(ref, ref, w3s, w3r.at[side, way], chip(0, step))
                else:
                    came = lax.rem(y + 4 - step, 4)
                    await_bytes(WF.at[came, :, c, 1], w2r.at[side, way])
                    ref = WF.at[came, half, c, 1]
                    to_sub(ref, ref, w3s, w3r.at[side, way], chip(step, 0))

    def maps_arrived():
        await_bytes(CF.at[:, 0:3, 0], cfr.at[1])
        to_sub(CF.at[:, :, c], CF.at[:, :, c], cfs.at[2], cfr.at[2], partner)
        for side in range(2):
            for way in range(2):
                await_bytes(WF.at[0:2, 0, 0, 0], w3r.at[side, way])

    def maps_to_partner(part):
        for row in part:
            to_sub(WF.at[row, :, c], WF.at[row, :, c], w4s, w4r, partner)

    GP[...] = jnp.zeros(GP.shape, BF)
    loads[1].wait()

    def turn_leaf(i, carry):
        k, t = i // 4, lax.rem(i, 4)
        LWT[k, at(t, 256), :] = LW[k, :, at(t, 256)].T
        return carry

    lax.fori_loop(0, 16, turn_leaf, 0)
    loads[2].wait()

    def turn_mid(i, carry):
        a, b = i // 4, lax.rem(i, 4)
        MWT[at(b, 256), at(a, 256)] = MW[at(a, 256), at(b, 256)].T
        return carry

    lax.fori_loop(0, 16, turn_mid, 0)

    def leaf_blocks(lanes):
        n = lanes.stop - lanes.start
        squares = jnp.zeros((8, n), F32)
        for t in range(4):
            rows = slice(256 * t, 256 * (t + 1))
            product = None
            for k in range(4):
                factor = 1.0 + nt(LWT[k, rows, :], XR[k, lanes, :])
                FK[k, rows, lanes] = factor.astype(BF)
                product = factor if product is None else product * factor
            LB[rows, 0:n] = product
            squares = squares + fold(product * product)
        r = factor_of(squares)
        RL[:, lanes] = jnp.broadcast_to(r, (8, n))
        for t in range(4):
            rows = slice(256 * t, 256 * (t + 1))
            LM[rows, lanes] = (LB[rows, 0:n] * r).astype(BF)
        for t in range(4):
            rows = slice(256 * t, 256 * (t + 1))
            value = nn(MWT[rows, :], LM[:, lanes]).astype(BF)
            for b in range(n // B):
                MS[lanes.start // B + b, rows, :] = value[:, lanes_of(b)]

    def turn_slots(lanes):
        for k in range(4):
            XT[k, :, lanes] = XR[k, lanes, :].T

    own_slots.wait()
    leaf_blocks(slice(0, B))
    own_mid = pltpu.make_async_copy(MS.at[0], MR.at[p], local_sem.at[1])
    own_mid.start()
    for t in range(8):
        rows = slice(128 * t, 128 * (t + 1))
        for side in range(2):
            WT[2 * side + t // 4, 0:960, 128 * (t % 4) : 128 * (t % 4 + 1)] = WN[side, rows, 0:960].T
    for level in (2, 3):
        size = CHUNK[level]
        col = min(COLUMN[level], 896)
        count = D // size
        for side in range(2):
            for q in range(count):
                to = (q % 2 * (count // 2) + q // 2) * size
                WP[level - 2, side, to : to + size, :] = WN[side, q * size : (q + 1) * size, col : col + 128]
    turn_slots(slice(0, B))
    for blocks in ((1, 2), (3,)):
        for i in blocks:
            await_bytes(XR.at[:, lanes_of(i), :], x1r.at[i])
        lanes = slice(blocks[0] * B, (blocks[-1] + 1) * B)
        leaf_blocks(lanes)
        for i in blocks:
            to_rep(MS.at[i], MR.at[p], x2s, x2r, source(i))
        turn_slots(lanes)
        if len(blocks) == 2:
            maps_to_neighbours()

    maps_to_opposite()
    own_mid.wait()
    await_bytes(MR.at[0:3], x2r)
    for t in range(8):
        rows = slice(128 * t, 128 * (t + 1))
        product = 1.0 + MR[0, rows, :].astype(F32)
        for k in range(1, 4):
            product = product * (1.0 + MR[k, rows, :].astype(F32))
        A0[pl.ds(pl.multiple_of(c * D + t * 128, 128), 128), :] = product.astype(BF)

    own = slice(0, B)

    def spread(level, me, block):
        ref = A[level].at[at(me, block), :]
        to_sub(ref, ref, fs.at[level], fo.at[level], partner)

        for step in reversed(steps_of(level)):
            to_sub(ref, ref, fs.at[level], fr.at[level, STEP_SLOT[step]], chip_of(level, step, 1))

    def chip_of(level, step, sign):
        ny, nz = EXTENT[level]
        yy = y // ny * ny + lax.rem(lax.rem(y, ny) + (step[0] if sign > 0 else ny - step[0]), ny)
        zz = z // nz * nz + lax.rem(lax.rem(z, nz) + (step[1] if sign > 0 else nz - step[1]), nz)
        return (yy * 4 + zz) * 2 + c

    def collect(level, me, block):
        half = GROUP[level] // 2

        for step in steps_of(level):
            ref = A[level].at[at(chip_of(level, step, -1) - s + me, block), :]
            await_bytes(ref, fr.at[level, STEP_SLOT[step]])
            to_sub(ref, ref, ff.at[level], fo.at[level], partner)
        await_bytes(A[level].at[0 : half * block], fo.at[level])

    def share_rows(level):
        for i in range(1, REPS):
            if level < LEVELS:
                rows = pl.ds(pl.multiple_of(c * D + source(i) * 256, 256), 256)
                dst = AX.at[level, c, :, lanes_of(BACK[i])]
            else:
                rows = pl.ds(pl.multiple_of(source(i) * 256 + c * 128, 128), 128)
                dst = AX.at[level, 0, at(c, 128), lanes_of(BACK[i])]
            to_rep(A[level].at[rows, :], dst, axs.at[level], axr.at[level], source(i))
        for side in range(2 if level < LEVELS else 1):
            rows = pl.ds(pl.multiple_of(side * D + p * 256, 256), 256)
            copy = pltpu.make_async_copy(
                A[level].at[rows, :], AX.at[level, side, :, own], local_sem.at[2 + 2 * level + side]
            )
            copy.start()
            kept.append(copy)

    def pass_rows(level):
        if level == 0:
            await_bytes(H0.at[:, 0 : 3 * B], h0r)
            for copy in message_copies:
                copy.wait()
            src, dst = H0.at[at(p, 256), :], AX.at[0, c]
        elif level < LEVELS:
            await_bytes(AX.at[level, 0, :, 0 : 3 * B], axr.at[level])
            src = dst = AX.at[level, c, :, B:ALL]
        else:
            await_bytes(AX.at[level, 0, 0:128, 0 : 3 * B], axr.at[level])
            src = dst = AX.at[level, 0, at(c, 128), B:ALL]
        to_sub(src, dst, aps.at[level], apr.at[level], partner)

    def passed(level):
        if level == 0:
            return AX.at[0, 0]
        if level < LEVELS:
            return AX.at[level, 0, :, 0 : 3 * B]
        return AX.at[level, 0, 0:128, 0 : 3 * B]

    kept = []

    def squares_of(ref, start, lanes=slice(0, B)):
        total = jnp.zeros((8, B), F32)
        for t in range(4):
            values = ref[start + 256 * t : start + 256 * (t + 1), lanes].astype(F32)
            total = total + fold(values * values)
        return total

    spread(0, c, D)
    message = A0.at[at(c, D), :]

    def leave_one(t, carry):
        rows = at(t, 128)
        rest = others([1.0 + MR[k, rows, :].astype(F32) for k in range(4)])
        for k in range(4):
            CS[k, rows, :] = rest[k].astype(BF)
        return carry

    lax.fori_loop(0, 8, leave_one, 0)

    for i in range(1, REPS):
        to_rep(message, H0.at[:, lanes_of(BACK[i])], h0s, h0r, source(i))
    for i in range(1, REPS):
        to_rep(CS.at[source(i)], LO.at[:, lanes_of(BACK[i])], x3s, x3r, source(i))
    message_copies = [
        pltpu.make_async_copy(CS.at[p], LO.at[:, own], local_sem.at[20]),
        pltpu.make_async_copy(message, H0.at[:, own], local_sem.at[21]),
    ]
    for copy in message_copies:
        copy.start()
    scales = []
    for level in range(LEVELS - 1):
        group, w, col = GROUP[level], WIDTH[level], COLUMN[level]
        collect(level, lax.rem(s, group), 2 * D // group)
        if level:
            share_rows(level)
        left = factor_of(squares_of(A[level], 0))
        right = factor_of(squares_of(A[level], D))
        scales.append((left, right))
        me = lax.rem(s, GROUP[level + 1])
        size = min(w, 256)
        for t in range(w // size):
            rows = slice(col + t * size, col + (t + 1) * size)
            ul = (nn(WT[0, rows, :], A[level][0:512, :]) + nn(WT[1, rows, :], A[level][512:D, :])) * left
            ur = (nn(WT[2, rows, :], A[level][D:1536, :]) + nn(WT[3, rows, :], A[level][1536 : 2 * D, :])) * right
            joined = (1.0 + ul) * (1.0 + ur)
            UL[rows, :] = ul
            UR[rows, :] = ur
            JJ[rows, :] = joined
            A[level + 1][pl.ds(pl.multiple_of(me * w + t * size, size), size), :] = joined.astype(BF)
        spread(level + 1, me, w)
        if level == 1:
            maps_arrived()
            maps_to_partner((0, 1))
        if level == 2:
            maps_to_partner((2, 3))

    def share_grads(level):
        w, col = WIDTH[level], COLUMN[level]
        for i in range(1, REPS):
            to_rep(
                GX.at[:, col : col + w, own], GX.at[:, col : col + w, lanes_of(BACK[i])],
                gxs.at[level], gxr.at[level], source(i),
            )

    def share_last_grads():
        for i in (1, 2):
            for side in (i - 1, 2 - i):
                to_rep(
                    GX.at[side, 0:512, own], GX.at[side, 0:512, lanes_of(BACK[i])],
                    gxs.at[0], gx0.at[BACK[i], side], source(i),
                )

    def relay_last_grads():
        for i in (1, 2):
            side = i - 1
            ref = GX.at[side, 0:512, lanes_of(BACK[i])]
            await_bytes(ref, gx0.at[BACK[i], side])
            to_rep(ref, GX.at[side, 0:512, lanes_of(3)], gxt, gx0.at[3, side], source(i))

    def scatter(level, me):
        at_chip = me // 2
        for step in reversed(steps_of(level)):
            peer = chip_of(level, step, 1)
            d = at_chip + (peer - s) // 2
            to_sub(BS[level].at[d], BR[level].at[at_chip], bs.at[level], br.at[level], peer)
        copy = pltpu.make_async_copy(
            BS[level].at[at_chip], BR[level].at[at_chip], local_sem.at[14 + level]
        )
        copy.start()
        return copy

    await_bytes(WF.at[:, :, 0], w4r)
    mine = s // 16
    block = lax.rem(s, 16)
    for g in range(4):
        cols = slice(256 * g, 256 * (g + 1))
        lanes = pl.ds(pl.multiple_of(block // 2 * 128, 128), 128)
        W4[:, cols] = WF[g, :, :, mine, 0:32, lanes].reshape(256, 128).T
    collect(4, s, 2 * D // SUBS)
    share_rows(4)
    left = factor_of(squares_of(A4, 0))
    right = factor_of(squares_of(A4, D))
    scales.append((left, right))
    squares = jnp.zeros((8, B), F32)
    for g in range(4):
        rows = slice(256 * g, 256 * (g + 1))
        ul = nn(WF[g, :, :, 0, 0:32, :].reshape(256, D), A4[0:D, :]) * left
        ur = nn(WF[g, :, :, 1, 0:32, :].reshape(256, D), A4[D : 2 * D, :]) * right
        joined = ((1.0 + ul) * (1.0 + ur)).astype(BF)
        UF[0, rows, :] = ul
        UF[1, rows, :] = ur
        A5[rows, :] = joined
        squares = squares + fold(joined.astype(F32) * joined.astype(F32))
    root_scale = factor_of(squares)
    share_rows(5)
    await_bytes(CF.at[:, :, 0], cfr.at[2])
    for g in range(4):
        rows = slice(256 * g, 256 * (g + 1))
        za = nn(WF[g, :, :, 0, 32:64, :].reshape(256, D), A5[...]) * root_scale
        zb = nn(WF[g, :, :, 1, 32:64, :].reshape(256, D), A5[...]) * root_scale
        sigma = 1.0 / (1.0 + jnp.exp(-zb))
        cotangent = CF[g].reshape(256, B)
        GH[0, rows, :] = (cotangent * sigma).astype(BF)
        GH[1, rows, :] = (cotangent * za * sigma * (1.0 - sigma)).astype(BF)
    block_rows = pl.ds(pl.multiple_of(s * 32, 32), 32)
    for side in range(2):
        GX[side, 992:1024, own] = (GH[side, block_rows, :].astype(F32) * root_scale).astype(BF)
    share_grads(5)
    turned = [GH[side].T for side in range(2)]
    total = jnp.zeros((8, B), F32)
    for t in range(4):
        rows = slice(256 * t, 256 * (t + 1))
        part = None
        for side in range(2):
            term = nn(turned[side], WF[:, :, :, side, 32:64, rows].reshape(D, 256))
            part = term if part is None else part + term
        part = part.T
        PB[rows, :] = part
        total = total + fold(part * A5[rows, :].astype(F32))
    mean = column_sum(total) * (1.0 / D)
    shift = root_scale * root_scale * mean
    dl = jnp.zeros((8, B), F32)
    dr = jnp.zeros((8, B), F32)
    for t in range(8):
        rows = slice(128 * t, 128 * (t + 1))
        ul, ur = UF[0, rows, :], UF[1, rows, :]
        v = root_scale * (PB[rows, :] - (1.0 + ul) * (1.0 + ur) * shift)
        gl = (v * (1.0 + ur)).astype(BF)
        gr = (v * (1.0 + ul)).astype(BF)
        GH[0, rows, :] = gl
        GH[1, rows, :] = gr
        dl = dl + fold(gl.astype(F32) * ul)
        dr = dr + fold(gr.astype(F32) * ur)
    root_mean = jnp.where(mine == 1, column_sum(dr), column_sum(dl)) * (1.0 / D)
    part_rows = pl.ds(pl.multiple_of(lax.rem(block, 2) * 64, 64), 64)
    PB[0:64, :] = nn(W4[part_rows, :], GH[mine])
    for side in range(2):
        GX[side, 960:992, own] = (GH[side, block_rows, :].astype(F32) * scales[4][side]).astype(BF)
    share_grads(4)

    def gathered(level, rows):
        if level == LEVELS - 1:
            return PB[rows, :]
        group = BR[level].shape[0]
        total = BR[level][0, rows, :].astype(F32)
        for g in range(1, group):
            total = total + BR[level][g, rows, :].astype(F32)
        return total

    def await_chunks(level, copy):
        if level == LEVELS - 1:
            return root_mean
        copy.wait()
        await_bytes(BR[level].at[0 : BR[level].shape[0] - 1], br.at[level])
        size = CHUNK[level]
        return column_sum(gathered(level, slice(size, size + 16))) * (1.0 / D)

    own_chunk = None
    for level in reversed(range(LEVELS - 1)):
        group, w, col = GROUP[level], WIDTH[level], COLUMN[level]
        mean = await_chunks(level + 1, own_chunk)
        side_of = lax.rem(s // GROUP[level], 2)
        r = jnp.where(side_of == 1, scales[level + 1][1], scales[level + 1][0])
        left, right = scales[level]
        size = min(w, 64)

        def node_back(t, carry):
            dl, dr = carry
            rows = pl.ds(pl.multiple_of(col + t * size, size), size)
            total = gathered(level + 1, pl.ds(pl.multiple_of(t * size, size), size))
            ul, ur = UL[rows, :], UR[rows, :]
            v = r * (total - JJ[rows, :] * (r * mean))
            gl = v * (1.0 + ur)
            gr = v * (1.0 + ul)
            GX[0, rows, own] = (gl * left).astype(BF)
            GX[1, rows, own] = (gr * right).astype(BF)
            if level == 0:
                return carry
            gl = gl.astype(BF)
            gr = gr.astype(BF)
            if level < 3:
                near = pl.ds(pl.multiple_of(col - 512 + t * size, size), size)
                GB[0, near, :] = gl
                GB[1, near, :] = gr
            else:
                GP[level - 3, 0, col - 896 : col - 896 + w, :] = gl
                GP[level - 3, 1, col - 896 : col - 896 + w, :] = gr
            return dl + fold(gl.astype(F32) * ul), dr + fold(gr.astype(F32) * ur)

        zero = jnp.zeros((8, B), F32)
        dl, dr = lax.fori_loop(0, w // size, node_back, (zero, zero))
        if level == 0:
            share_last_grads()
            break
        share_grads(level)
        chunk = CHUNK[level]
        dots = [column_sum(dl), column_sum(dr)]

        def half_sums(side, parity):
            rows = pl.ds(pl.multiple_of(parity * 512, 512), 512)
            if level == 1:
                return nn(WN[side, rows, col : col + w], GB[side, col - 512 : col - 512 + w, :])
            if level == 2:
                return nn(WP[0, side, rows, :], GB[side, col - 512 : col - 512 + w, :])
            return nn(WP[level - 2, side, rows, :], GP[level - 3, side])

        for side in range(2):
            BO[level - 1, side, 0:512, :] = half_sums(side, 1 - c).astype(BF)
            BO[level - 1, side, 512:528, :] = split_tile(dots[side])
        to_sub(BO.at[level - 1], BI.at[level - 1], bos.at[level], bis.at[level], partner)
        for side in range(2):
            LB[side * 512 : (side + 1) * 512, 0:B] = half_sums(side, c)
        await_bytes(BI.at[level - 1], bis.at[level])
        quarter = group // 4
        for side in range(2):
            tile = split_tile(dots[side] + column_sum(BI[level - 1, side, 512:528, :].astype(F32)))
            chunks = slice(side * quarter, (side + 1) * quarter)
            value = (LB[side * 512 : (side + 1) * 512, 0:B] + BI[level - 1, side, 0:512, :].astype(F32)).astype(BF)
            BS[level][chunks, 0:chunk, :] = value.reshape(quarter, chunk, B)
            BS[level][chunks, chunk : chunk + 16, :] = jnp.broadcast_to(tile[None], (quarter, 16, B))
        own_chunk = scatter(level, lax.rem(s, group))
        for done in {3: (0, 1, 2), 2: (3, 4), 1: (5,)}[level]:
            pass_rows(done)

    await_bytes(MS.at[0:3], x2s)

    def partial_sums(blocks):
        for i in blocks:
            for side in {0: (), 1: (0,), 2: (1,), 3: (0, 1)}[i]:
                await_bytes(GX.at[side, 0:512, lanes_of(i)], gx0.at[i, side])
        lanes = slice(blocks[0] * B, (blocks[-1] + 1) * B)
        for t in range(4):
            rows = slice(256 * t, 256 * (t + 1))
            value = nn(WN[1 - c, rows, 0:512], GX[1 - c, 0:512, lanes]).astype(BF)
            for b, i in enumerate(blocks):
                MS[i, rows, :] = value[:, lanes_of(b)]
        for i in blocks:
            to_sub(MS.at[i], PR.at[i], pss, prs.at[i], partner)
        for t in range(4):
            rows = slice(256 * t, 256 * (t + 1))
            PM[rows, 0 : B * len(blocks)] = nn(WN[c, rows, 0:512], GX[c, 0:512, lanes])

    partial_sums((0,))

    await_bytes(LO.at[:, 0 : 3 * B], x3r)
    for i in range(REPS):
        R0[:, lanes_of(i)] = jnp.broadcast_to(factor_of(squares_of(H0, 0, lanes_of(i))), (8, B))

    def middle_back(blocks):
        for i in blocks:
            await_bytes(PR.at[i], prs.at[i])
        for b, i in enumerate(blocks):
            part = lanes_of(b)
            total = jnp.zeros((8, B), F32)
            for t in range(8):
                rows = slice(128 * t, 128 * (t + 1))
                value = PM[rows, part] + PR[i, rows, :].astype(F32)
                PM[rows, part] = value
                total = total + fold(value * H0[rows, lanes_of(i)].astype(F32))
            scale0 = R0[0:1, lanes_of(i)]
            shift = scale0 * scale0 * (column_sum(total) * (1.0 / D))
            for t in range(8):
                rows = slice(128 * t, 128 * (t + 1))
                v = PM[rows, part] - H0[rows, lanes_of(i)].astype(F32) * shift
                CR[rows, lanes_of(i)] = (v * LO[rows, lanes_of(i)].astype(F32)).astype(BF)

    def leaf_back(blocks):
        lanes = slice(blocks[0] * B, (blocks[-1] + 1) * B)
        n = B * len(blocks)
        total = jnp.zeros((8, n), F32)
        for t in range(4):
            rows = slice(256 * t, 256 * (t + 1))
            value = nn(MW[rows, :], CR[:, lanes])
            LB[rows, 0:n] = value
            total = total + fold(value * LM[rows, lanes].astype(F32))
        mean = column_sum(total) * (1.0 / D)
        r = RL[0:1, lanes]
        for t in range(16):
            rows = slice(64 * t, 64 * (t + 1))
            v = r * (LB[rows, 0:n] - LM[rows, lanes].astype(F32) * mean)
            rest = others([FK[k, rows, lanes].astype(F32) for k in range(4)])
            for k in range(4):
                WT[k, rows, lanes] = (v * rest[k]).astype(BF)

    def await_grads(level):
        w, col = WIDTH[level], COLUMN[level]
        await_bytes(GX.at[:, col : col + w, 0 : 3 * B], gxr.at[level])

    middle_back((0,))
    leaf_back((0,))
    relay_last_grads()

    for copy in kept:
        copy.wait()
    for level in range(LEVELS + 1):
        await_bytes(passed(level), apr.at[level])
    for level in (5, 4, 3):
        await_grads(level)
    lane = lax.broadcasted_iota(jnp.int32, (256, 128), 1)
    for side in range(2):
        grads = GX[side, 896:1024, :]
        g3 = nt(AX[3, side], grads)
        g4 = nt(AX[4, side], grads)
        g5 = nt(AX[5, 0], grads)
        OU[side, :, 896:1024] = jnp.where(lane < 64, g3, jnp.where(lane < 96, g4, g5)).astype(BF)

    def upper_gradient(level):
        await_grads(level)
        w, col = WIDTH[level], COLUMN[level]
        for side in range(2):
            OU[side, :, col : col + w] = nt(AX[level, side], GX[side, col : col + w, :]).astype(BF)

    upper_gradient(2)
    upper_gradient(1)

    partial_sums((1, 2))
    middle_back((1, 2))
    partial_sums((3,))
    leaf_back((1, 2))

    rows = at(p, 256)
    OU[c, :, 0:512] = nt(H0[rows, :], GX[c, 0:512, :]).astype(BF)
    OU[1 - c, :, 0:512] = nt(AX[0, 1 - c], GX[1 - c, 0:512, :]).astype(BF)

    middle_back((3,))
    leaf_back((3,))

    await_bytes(XS.at[0:3], x1s)
    await_bytes(CS.at[0:3], x3s)
    await_bytes(H0.at[:, 0 : 3 * B], h0s)
    await_bytes(MS, pss)
    for level in range(1, LEVELS - 1):
        await_bytes(BO.at[level - 1], bos.at[level])
    await_bytes(CF.at[0:3, 0, 0], cfs.at[0])
    await_bytes(CF.at[0:3, :, 0], cfs.at[1])
    await_bytes(CF.at[:, :, 0], cfs.at[2])
    await_bytes(WF.at[0:3, 0, 0], w1s)
    await_bytes(WF.at[:, :, 0, 0], w2s)
    await_bytes(WF.at[0:2, :, 0, 0], w3s)
    await_bytes(WF.at[:, :, 0], w4s)
    for level in range(LEVELS + 1):
        if level < LEVELS:
            half = GROUP[level] // 2
            block = A[level].shape[0] // GROUP[level]
            await_bytes(A[level].at[0 : half * block], fs.at[level])
            if half > 1:
                await_bytes(A[level].at[0 : (half - 1) * block], ff.at[level])
        if 0 < level < LEVELS - 1:
            await_bytes(BS[level].at[0 : BS[level].shape[0] - 1], bs.at[level])
        if level:
            await_bytes(passed(level), axs.at[level])
            w, col = WIDTH[level], COLUMN[level]
            await_bytes(GX.at[:, col : col + w, 0 : 3 * B], gxs.at[level])
        await_bytes(passed(level), aps.at[level])
    await_bytes(GX.at[:, 0:512, 0 : 2 * B], gxs.at[0])
    await_bytes(GX.at[:, 0:512, own], gxt)


def scratch():
    vm = pltpu.VMEM
    dma = pltpu.SemaphoreType.DMA
    chunks = [vm((GROUP[j] // 2, CHUNK[j] + 16, B), BF) for j in range(1, LEVELS - 1)]
    return (
        [
            vm((2048, F), BF), vm((256, 256), BF), vm((4, 4, B, F), BF), vm((4, ALL, F), BF),
            vm((4, F, D), BF), vm((4, D, F), BF), vm((D, D), BF), vm((D, D), BF),
            vm((4, 128, 2, D), BF), vm((2, D, D), BF), vm((4, 4, 2, 32, B), F32),
            vm((4, D, ALL), BF), vm((8, ALL), F32),
            vm((4, D, B), BF), vm((4, D, B), BF),
        ]
        + [vm((2 * D, B), BF)] * 5
        + [vm((D, B), BF)]
        + [vm((D, B), F32)] * 3
        + [vm((1, 2, 128, B), BF), vm((2, 384, B), BF), vm((2, 2, D, 128), BF)]
        + [vm((3, 2, 528, B), BF)] * 2
        + chunks
        + chunks
        + [
            vm((2, D, ALL), BF), vm((6, 2, 256, ALL), BF), vm((4, D, B), BF),
            vm((D, 2 * B), F32),
            vm((D, ALL), BF), vm((D, ALL), BF), vm((8, ALL), F32),
            vm((4, D, B), BF), vm((D, 2 * B), F32),
            vm((4, 4, 2, 2, 64, D), BF), vm((128, D), BF), vm((2, D, B), F32), vm((2, D, B), BF), vm((D, B), F32),
        ]
        + [
            dma((8,)), dma((22,)), dma, dma((4,)), dma, dma, dma, dma, dma, dma,
            dma((6,)), dma((6, 16)), dma((6,)), dma((6,)), dma((6,)), dma((6,)), dma((6,)), dma((6,)),
            dma((6,)), dma((6,)), dma((6,)), dma((6,)), dma((6,)), dma((6,)), dma((4, 2)), dma, dma, dma((4,)),
            dma((3,)), dma((3,)), dma, dma((2,)), dma, dma((2, 2)), dma, dma((2, 2)), dma, dma,
        ]
    )


def gradients(CT, LM, CR, XT, OU, lg_hbm, mg_hbm, ug_hbm, LW, OM, OI, sem):
    copies = []

    def out(src, dst):
        copies.append(pltpu.make_async_copy(src, dst, sem.at[len(copies)]))
        copies[-1].start()

    for t in range(4):
        rows = slice(64 * t, 64 * (t + 1))
        for side in range(2):
            OI[rows, side, :] = OU[side, rows, :]
    out(OI, ug_hbm)
    for k in range(4):
        LW[k] = nt(XT[k], CT[k]).astype(BF)
        out(LW.at[k], lg_hbm.at[k])
    for t in range(4):
        rows = slice(256 * t, 256 * (t + 1))
        OM[rows, :] = nt(LM[rows, :], CR[...]).astype(BF)
        out(OM.at[rows], mg_hbm.at[rows])
    for copy in copies:
        copy.wait()


def on_device(regions, leaf_map, leaf_bond_weight, mid_weight, upper_weight, head_cotangent):
    anywhere = pl.BlockSpec(memory_space=pl.ANY)
    local = pl.BlockSpec(memory_space=pltpu.VMEM)
    kept = pl.pallas_call(
        kernel,
        out_shape=(
            pltpu.VMEM((4, D, ALL), BF),
            pltpu.VMEM((D, ALL), BF),
            pltpu.VMEM((D, ALL), BF),
            pltpu.VMEM((4, F, ALL), BF),
            pltpu.VMEM((2, 256, D), BF),
        ),
        in_specs=[pl.BlockSpec(memory_space=pltpu.SMEM)] + [anywhere] * 5,
        out_specs=(local,) * 5,
        scratch_shapes=scratch(),
        compiler_params=pltpu.CompilerParams(
            collective_id=0, has_side_effects=True, vmem_limit_bytes=VMEM_LIMIT
        ),
    )(
        leaf_map, regions.reshape(B * 16, F), leaf_bond_weight[0], mid_weight[0, 0],
        upper_weight[0], head_cotangent.T,
    )
    kept = [pltpu.with_memory_space_constraint(array, pltpu.VMEM) for array in kept]
    outs = pl.pallas_call(
        gradients,
        out_shape=(
            jax.ShapeDtypeStruct((4, F, D), BF),
            jax.ShapeDtypeStruct((D, D), BF),
            jax.ShapeDtypeStruct((256, 2, D), BF),
        ),
        in_specs=[local] * 5,
        out_specs=(anywhere,) * 3,
        scratch_shapes=[
            pltpu.VMEM((4, F, D), BF), pltpu.VMEM((D, D), BF), pltpu.VMEM((256, 2, D), BF),
            pltpu.SemaphoreType.DMA((9,)),
        ],
        compiler_params=pltpu.CompilerParams(vmem_limit_bytes=32000000),
    )(*kept)
    return (outs[0][None], outs[1][None, None], outs[2][None])


def solution(mesh):
    placed = (
        P("rep", "sub", None),
        P("sub"),
        P(("sub", "rep"), None, None, None),
        P("sub", "rep", None, None),
        P("sub", None, None, None),
        P("rep", "sub"),
    )
    return jax.shard_map(
        on_device,
        mesh=mesh,
        in_specs=placed,
        out_specs=(
            P(("sub", "rep"), None, None, None),
            P("sub", "rep", None, None),
            P("sub", "rep", None, None),
        ),
        check_vma=False,
    )
```

```python
import jax
import jax.numpy as jnp
from jax import lax
from jax.experimental import pallas as pl
from jax.experimental.pallas import tpu as pltpu
from jax.sharding import PartitionSpec as P

F32 = jnp.float32
BF = jnp.bfloat16
MESH = pl.DeviceIdType.MESH
EPSILON = 1e-06
VMEM_LIMIT = 58500000
D = 1024
F = 256
B = 128
REPS = 4
SUBS = 32
LEVELS = 5
ALL = REPS * B
WIDTH = [D // 2 ** (j + 1) for j in range(LEVELS)] + [D // SUBS]
COLUMN = [D - 2 * WIDTH[j] for j in range(LEVELS)] + [D - D // SUBS]
CHUNK = [2 * WIDTH[j] for j in range(LEVELS)] + [WIDTH[5]]
GROUP = [2 ** (j + 1) for j in range(LEVELS)] + [SUBS]


def nn(a, b):
    return jnp.dot(a, b, preferred_element_type=F32)


def nt(a, b):
    return lax.dot_general(a, b, (((1,), (1,)), ((), ())), preferred_element_type=F32)


def fold(values):
    return jnp.sum(values.reshape(values.shape[0] // 8, 8, values.shape[1]), axis=0)


def column_sum(values):
    return jnp.sum(values, axis=0, keepdims=True)


def factor_of(squares):
    return lax.rsqrt(column_sum(squares) * (1.0 / D) + EPSILON)


def at(index, size):
    return pl.ds(pl.multiple_of(index * size, size), size)


def lanes_of(i):
    return slice(i * B, (i + 1) * B)


OFFSET = (0, 1, 3, 2)
BACK = (0, 2, 1, 3)


STEP_SLOT = {(dy, dz): 4 * dy + dz for dy in range(4) for dz in range(4)}
EXTENT = ((1, 1), (1, 2), (1, 4), (2, 4), (4, 4))


def steps_of(level):
    ny, nz = EXTENT[level]
    steps = [(dy, dz) for dy in range(ny) for dz in range(nz) if dy or dz]
    return sorted(steps, key=lambda d: min(d[0], ny - d[0]) + min(d[1], nz - d[1]))


def others(f):
    p01 = f[0] * f[1]
    p23 = f[2] * f[3]
    return [f[1] * p23, f[0] * p23, p01 * f[3], p01 * f[2]]


def split_tile(row):
    high = row.astype(BF).astype(F32)
    index = lax.broadcasted_iota(jnp.int32, (16, B), 0)
    tile = jnp.where(index == 0, high, jnp.where(index == 1, row - high, 0.0))
    return tile.astype(BF)


def kernel(
    map_ref, reg_hbm, lw_hbm, mw_hbm, uw_hbm, cot_hbm,
    WT, LM, CR, XT, OU,
    R, Q, XS, XR, LW, LWT, MW, MWT, UW, WN, CF, FK, RL, MS, MR,
    A0, A1, A2, A3, A4, A5, UL, UR, JJ, GP, GB, WP, BO, BI,
    BS1, BS2, BS3, BR1, BR2, BR3,
    GX, AX, CS, LB, LO, H0, R0, PR, PM, WF, W4, UF, GH, PB,
    load_sem, local_sem, x1s, x1r, x2s, x2r, x3s, x3r, h0s, h0r, fs, fr, ff, fo, bs, br, bos, bis,
    axs, axr, aps, apr, gxs, gxr, gx0, gxt, pss, prs, cfs, cfr, w1s, w1r, w2s, w2r, w3s, w3r, w4s, w4r,
):
    A = [A0, A1, A2, A3, A4, A5]
    BS = [None, BS1, BS2, BS3]
    BR = [None, BR1, BR2, BR3]
    s = lax.axis_index("sub")
    p = lax.axis_index("rep")

    def to_rep(src, dst, send, recv, peer):
        pltpu.make_async_remote_copy(
            src_ref=src, dst_ref=dst, send_sem=send, recv_sem=recv,
            device_id={"rep": peer}, device_id_type=MESH,
        ).start()

    def to_sub(src, dst, send, recv, peer):
        pltpu.make_async_remote_copy(
            src_ref=src, dst_ref=dst, send_sem=send, recv_sem=recv,
            device_id={"sub": peer}, device_id_type=MESH,
        ).start()

    def await_bytes(ref, sem):
        pltpu.make_async_copy(ref, ref, sem).wait()

    c = lax.rem(s, 2)
    z = lax.rem(s // 2, 4)
    y = s // 8
    partner = s + 1 - 2 * c

    def upper_part(t):
        return pltpu.make_async_copy(uw_hbm.at[128 * t : 128 * (t + 1)], UW.at[t % 4], load_sem.at[4 + t % 4])

    loads = [
        pltpu.make_async_copy(src, dst, load_sem.at[i])
        for i, (src, dst) in enumerate([(reg_hbm, R), (lw_hbm, LW), (mw_hbm, MW), (cot_hbm, CF.at[y, z, c])])
    ]
    loads[0].start()
    loads[3].start()
    for t in range(4):
        upper_part(t).start()
    loads[1].start()
    loads[2].start()

    barrier = pltpu.get_barrier_semaphore()

    def chip(dy, dz):
        return (lax.rem(y + dy, 4) * 4 + lax.rem(z + dz, 4)) * 2 + c

    far_first = list(reversed(steps_of(LEVELS - 1)))
    for dy, dz in far_first:
        pl.semaphore_signal(barrier, inc=1, device_id={"sub": chip(dy, dz)}, device_id_type=MESH)
    for i in (2, 1, 3):
        pl.semaphore_signal(
            barrier, inc=1, device_id={"rep": lax.rem(p + i, REPS)}, device_id_type=MESH
        )
    pl.semaphore_signal(barrier, inc=1, device_id={"sub": partner}, device_id_type=MESH)

    column = lax.broadcasted_iota(jnp.int32, (16, 256), 1)
    sample = lax.broadcasted_iota(jnp.int32, (16, 256), 0)
    for l in range(16):
        wanted = sample * 16 + map_ref[l]
        Q[16 * l : 16 * l + 16, :] = jnp.where(column == wanted, 1.0, 0.0).astype(BF)
    loads[0].wait()

    for q in range(8):
        got = nn(Q[...], R[256 * q : 256 * (q + 1), :]).astype(BF)
        for l in range(16):
            XS[l // 4, l % 4, 16 * q : 16 * q + 16, :] = got[16 * l : 16 * l + 16, :]
    pl.semaphore_wait(barrier, len(far_first) + 1 + REPS - 1)

    def source(i):
        return lax.rem(p + OFFSET[i], REPS)

    for i in range(1, REPS):
        peer = source(i)
        to_rep(XS.at[peer], XR.at[:, lanes_of(BACK[i]), :], x1s, x1r.at[BACK[i]], peer)
    own_slots = pltpu.make_async_copy(XS.at[p], XR.at[:, 0:B, :], local_sem.at[0])
    own_slots.start()

    for t in range(8):
        upper_part(t).wait()
        for q in range(4):
            rows = slice(128 * t + 32 * q, 128 * t + 32 * (q + 1))
            WN[:, rows, :] = jnp.swapaxes(UW[t % 4, 32 * q : 32 * (q + 1)], 0, 1)
        if t < 4:
            upper_part(t + 4).start()
    for side in range(2):
        for t in range(4):
            rows = slice(256 * t, 256 * (t + 1))
            WF[y, z, c, side, :, rows] = WN[side, rows, 896:1024].T[64:128, :]

    for k in range(1, 4):
        ref = WF.at[y, z, c, 0]
        to_sub(ref, ref, w1s, w1r.at[0], chip(k, 0))
        ref = WF.at[y, z, c, 1]
        to_sub(ref, ref, w1s, w1r.at[1], chip(0, k))
    for side in range(2):
        ref = WF.at[y, z, c, side]
        for way, step in ((0, 1), (1, 3)):
            to_sub(ref, ref, w2s, w2r.at[side, way], chip(0, step) if side == 0 else chip(step, 0))
    loads[3].wait()
    for k in range(1, 4):
        ref = CF.at[y, z, c]
        to_sub(ref, ref, cfs.at[0], cfr.at[0], chip(k, 0))

    def maps_to_neighbours():
        for side in range(2):
            await_bytes(WF.at[0:3, 0, 0, side], w1r.at[side])
            for k in range(1, 4):
                ref = WF.at[lax.rem(y + k, 4), z, c, 0] if side == 0 else WF.at[y, lax.rem(z + k, 4), c, 1]
                for way, step in ((0, 1), (1, 3)):
                    to_sub(ref, ref, w2s, w2r.at[side, way], chip(0, step) if side == 0 else chip(step, 0))
        await_bytes(CF.at[0:3, 0, 0], cfr.at[0])
        ref = CF.at[:, z, c]
        for k in range(1, 4):
            to_sub(ref, ref, cfs.at[1], cfr.at[1], chip(0, k))

    def maps_to_opposite():
        for side in range(2):
            for way, step in ((0, 1), (1, 3)):
                half = slice(2 * way, 2 * way + 2)
                if side == 0:
                    came = lax.rem(z + 4 - step, 4)
                    await_bytes(WF.at[:, came, c, 0], w2r.at[side, way])
                    ref = WF.at[half, came, c, 0]
                    to_sub(ref, ref, w3s, w3r.at[side, way], chip(0, step))
                else:
                    came = lax.rem(y + 4 - step, 4)
                    await_bytes(WF.at[came, :, c, 1], w2r.at[side, way])
                    ref = WF.at[came, half, c, 1]
                    to_sub(ref, ref, w3s, w3r.at[side, way], chip(step, 0))

    def maps_arrived():
        await_bytes(CF.at[:, 0:3, 0], cfr.at[1])
        to_sub(CF.at[:, :, c], CF.at[:, :, c], cfs.at[2], cfr.at[2], partner)
        for side in range(2):
            for way in range(2):
                await_bytes(WF.at[0:2, 0, 0, 0], w3r.at[side, way])

    def maps_to_partner(part):
        for row in part:
            to_sub(WF.at[row, :, c], WF.at[row, :, c], w4s, w4r, partner)

    GP[...] = jnp.zeros(GP.shape, BF)
    loads[1].wait()

    def turn_leaf(i, carry):
        k, t = i // 4, lax.rem(i, 4)
        LWT[k, at(t, 256), :] = LW[k, :, at(t, 256)].T
        return carry

    lax.fori_loop(0, 16, turn_leaf, 0)
    loads[2].wait()

    def turn_mid(i, carry):
        a, b = i // 4, lax.rem(i, 4)
        MWT[at(b, 256), at(a, 256)] = MW[at(a, 256), at(b, 256)].T
        return carry

    lax.fori_loop(0, 16, turn_mid, 0)

    def leaf_blocks(lanes):
        n = lanes.stop - lanes.start
        squares = jnp.zeros((8, n), F32)
        for t in range(4):
            rows = slice(256 * t, 256 * (t + 1))
            product = None
            for k in range(4):
                factor = 1.0 + nt(LWT[k, rows, :], XR[k, lanes, :])
                FK[k, rows, lanes] = factor.astype(BF)
                product = factor if product is None else product * factor
            LB[rows, 0:n] = product
            squares = squares + fold(product * product)
        r = factor_of(squares)
        RL[:, lanes] = jnp.broadcast_to(r, (8, n))
        for t in range(4):
            rows = slice(256 * t, 256 * (t + 1))
            LM[rows, lanes] = (LB[rows, 0:n] * r).astype(BF)
        for t in range(4):
            rows = slice(256 * t, 256 * (t + 1))
            value = nn(MWT[rows, :], LM[:, lanes]).astype(BF)
            for b in range(n // B):
                MS[lanes.start // B + b, rows, :] = value[:, lanes_of(b)]

    def turn_slots(lanes):
        for k in range(4):
            XT[k, :, lanes] = XR[k, lanes, :].T

    own_slots.wait()
    leaf_blocks(slice(0, B))
    own_mid = pltpu.make_async_copy(MS.at[0], MR.at[p], local_sem.at[1])
    own_mid.start()
    for t in range(8):
        rows = slice(128 * t, 128 * (t + 1))
        for side in range(2):
            WT[2 * side + t // 4, 0:960, 128 * (t % 4) : 128 * (t % 4 + 1)] = WN[side, rows, 0:960].T
    for level in (2, 3):
        size = CHUNK[level]
        col = min(COLUMN[level], 896)
        count = D // size
        for side in range(2):
            for q in range(count):
                to = (q % 2 * (count // 2) + q // 2) * size
                WP[level - 2, side, to : to + size, :] = WN[side, q * size : (q + 1) * size, col : col + 128]
    turn_slots(slice(0, B))
    for blocks in ((1, 2), (3,)):
        for i in blocks:
            await_bytes(XR.at[:, lanes_of(i), :], x1r.at[i])
        lanes = slice(blocks[0] * B, (blocks[-1] + 1) * B)
        leaf_blocks(lanes)
        for i in blocks:
            to_rep(MS.at[i], MR.at[p], x2s, x2r, source(i))
        turn_slots(lanes)
        if len(blocks) == 2:
            maps_to_neighbours()

    maps_to_opposite()
    own_mid.wait()
    await_bytes(MR.at[0:3], x2r)
    for t in range(8):
        rows = slice(128 * t, 128 * (t + 1))
        product = 1.0 + MR[0, rows, :].astype(F32)
        for k in range(1, 4):
            product = product * (1.0 + MR[k, rows, :].astype(F32))
        A0[pl.ds(pl.multiple_of(c * D + t * 128, 128), 128), :] = product.astype(BF)

    own = slice(0, B)

    def spread(level, me, block):
        ref = A[level].at[at(me, block), :]
        to_sub(ref, ref, fs.at[level], fo.at[level], partner)

        for step in reversed(steps_of(level)):
            to_sub(ref, ref, fs.at[level], fr.at[level, STEP_SLOT[step]], chip_of(level, step, 1))

    def chip_of(level, step, sign):
        ny, nz = EXTENT[level]
        yy = y // ny * ny + lax.rem(lax.rem(y, ny) + (step[0] if sign > 0 else ny - step[0]), ny)
        zz = z // nz * nz + lax.rem(lax.rem(z, nz) + (step[1] if sign > 0 else nz - step[1]), nz)
        return (yy * 4 + zz) * 2 + c

    def collect(level, me, block):
        half = GROUP[level] // 2

        for step in steps_of(level):
            ref = A[level].at[at(chip_of(level, step, -1) - s + me, block), :]
            await_bytes(ref, fr.at[level, STEP_SLOT[step]])
            to_sub(ref, ref, ff.at[level], fo.at[level], partner)
        await_bytes(A[level].at[0 : half * block], fo.at[level])

    def share_rows(level):
        for i in range(1, REPS):
            if level < LEVELS:
                rows = pl.ds(pl.multiple_of(c * D + source(i) * 256, 256), 256)
                dst = AX.at[level, c, :, lanes_of(BACK[i])]
            else:
                rows = pl.ds(pl.multiple_of(source(i) * 256 + c * 128, 128), 128)
                dst = AX.at[level, 0, at(c, 128), lanes_of(BACK[i])]
            to_rep(A[level].at[rows, :], dst, axs.at[level], axr.at[level], source(i))
        for side in range(2 if level < LEVELS else 1):
            rows = pl.ds(pl.multiple_of(side * D + p * 256, 256), 256)
            copy = pltpu.make_async_copy(
                A[level].at[rows, :], AX.at[level, side, :, own], local_sem.at[2 + 2 * level + side]
            )
            copy.start()
            kept.append(copy)

    def pass_rows(level):
        if level == 0:
            await_bytes(H0.at[:, 0 : 3 * B], h0r)
            for copy in message_copies:
                copy.wait()
            src, dst = H0.at[at(p, 256), :], AX.at[0, c]
        elif level < LEVELS:
            await_bytes(AX.at[level, 0, :, 0 : 3 * B], axr.at[level])
            src = dst = AX.at[level, c, :, B:ALL]
        else:
            await_bytes(AX.at[level, 0, 0:128, 0 : 3 * B], axr.at[level])
            src = dst = AX.at[level, 0, at(c, 128), B:ALL]
        to_sub(src, dst, aps.at[level], apr.at[level], partner)

    def passed(level):
        if level == 0:
            return AX.at[0, 0]
        if level < LEVELS:
            return AX.at[level, 0, :, 0 : 3 * B]
        return AX.at[level, 0, 0:128, 0 : 3 * B]

    kept = []

    def squares_of(ref, start, lanes=slice(0, B)):
        total = jnp.zeros((8, B), F32)
        for t in range(4):
            values = ref[start + 256 * t : start + 256 * (t + 1), lanes].astype(F32)
            total = total + fold(values * values)
        return total

    spread(0, c, D)
    message = A0.at[at(c, D), :]

    def leave_one(t, carry):
        rows = at(t, 128)
        rest = others([1.0 + MR[k, rows, :].astype(F32) for k in range(4)])
        for k in range(4):
            CS[k, rows, :] = rest[k].astype(BF)
        return carry

    lax.fori_loop(0, 8, leave_one, 0)

    for i in range(1, REPS):
        to_rep(message, H0.at[:, lanes_of(BACK[i])], h0s, h0r, source(i))
    for i in range(1, REPS):
        to_rep(CS.at[source(i)], LO.at[:, lanes_of(BACK[i])], x3s, x3r, source(i))
    message_copies = [
        pltpu.make_async_copy(CS.at[p], LO.at[:, own], local_sem.at[20]),
        pltpu.make_async_copy(message, H0.at[:, own], local_sem.at[21]),
    ]
    for copy in message_copies:
        copy.start()
    scales = []
    for level in range(LEVELS - 1):
        group, w, col = GROUP[level], WIDTH[level], COLUMN[level]
        collect(level, lax.rem(s, group), 2 * D // group)
        if level:
            share_rows(level)
        left = factor_of(squares_of(A[level], 0))
        right = factor_of(squares_of(A[level], D))
        scales.append((left, right))
        me = lax.rem(s, GROUP[level + 1])
        size = min(w, 256)
        for t in range(w // size):
            rows = slice(col + t * size, col + (t + 1) * size)
            ul = (nn(WT[0, rows, :], A[level][0:512, :]) + nn(WT[1, rows, :], A[level][512:D, :])) * left
            ur = (nn(WT[2, rows, :], A[level][D:1536, :]) + nn(WT[3, rows, :], A[level][1536 : 2 * D, :])) * right
            joined = (1.0 + ul) * (1.0 + ur)
            UL[rows, :] = ul
            UR[rows, :] = ur
            JJ[rows, :] = joined
            A[level + 1][pl.ds(pl.multiple_of(me * w + t * size, size), size), :] = joined.astype(BF)
        spread(level + 1, me, w)
        if level == 1:
            maps_arrived()
            maps_to_partner((0, 1))
        if level == 2:
            maps_to_partner((2, 3))

    def share_grads(level):
        w, col = WIDTH[level], COLUMN[level]
        for i in range(1, REPS):
            to_rep(
                GX.at[:, col : col + w, own], GX.at[:, col : col + w, lanes_of(BACK[i])],
                gxs.at[level], gxr.at[level], source(i),
            )

    def share_last_grads():
        for i in (1, 2):
            for side in (i - 1, 2 - i):
                to_rep(
                    GX.at[side, 0:512, own], GX.at[side, 0:512, lanes_of(BACK[i])],
                    gxs.at[0], gx0.at[BACK[i], side], source(i),
                )

    def relay_last_grads():
        for i in (1, 2):
            side = i - 1
            ref = GX.at[side, 0:512, lanes_of(BACK[i])]
            await_bytes(ref, gx0.at[BACK[i], side])
            to_rep(ref, GX.at[side, 0:512, lanes_of(3)], gxt, gx0.at[3, side], source(i))

    def scatter(level, me):
        at_chip = me // 2
        for step in reversed(steps_of(level)):
            peer = chip_of(level, step, 1)
            d = at_chip + (peer - s) // 2
            to_sub(BS[level].at[d], BR[level].at[at_chip], bs.at[level], br.at[level], peer)
        copy = pltpu.make_async_copy(
            BS[level].at[at_chip], BR[level].at[at_chip], local_sem.at[14 + level]
        )
        copy.start()
        return copy

    await_bytes(WF.at[:, :, 0], w4r)
    mine = s // 16
    block = lax.rem(s, 16)
    for g in range(4):
        cols = slice(256 * g, 256 * (g + 1))
        lanes = pl.ds(pl.multiple_of(block // 2 * 128, 128), 128)
        W4[:, cols] = WF[g, :, :, mine, 0:32, lanes].reshape(256, 128).T
    collect(4, s, 2 * D // SUBS)
    share_rows(4)
    left = factor_of(squares_of(A4, 0))
    right = factor_of(squares_of(A4, D))
    scales.append((left, right))
    squares = jnp.zeros((8, B), F32)
    for g in range(4):
        rows = slice(256 * g, 256 * (g + 1))
        ul = nn(WF[g, :, :, 0, 0:32, :].reshape(256, D), A4[0:D, :]) * left
        ur = nn(WF[g, :, :, 1, 0:32, :].reshape(256, D), A4[D : 2 * D, :]) * right
        joined = ((1.0 + ul) * (1.0 + ur)).astype(BF)
        UF[0, rows, :] = ul
        UF[1, rows, :] = ur
        A5[rows, :] = joined
        squares = squares + fold(joined.astype(F32) * joined.astype(F32))
    root_scale = factor_of(squares)
    share_rows(5)
    await_bytes(CF.at[:, :, 0], cfr.at[2])
    for g in range(4):
        rows = slice(256 * g, 256 * (g + 1))
        za = nn(WF[g, :, :, 0, 32:64, :].reshape(256, D), A5[...]) * root_scale
        zb = nn(WF[g, :, :, 1, 32:64, :].reshape(256, D), A5[...]) * root_scale
        sigma = 1.0 / (1.0 + jnp.exp(-zb))
        cotangent = CF[g].reshape(256, B)
        GH[0, rows, :] = (cotangent * sigma).astype(BF)
        GH[1, rows, :] = (cotangent * za * sigma * (1.0 - sigma)).astype(BF)
    block_rows = pl.ds(pl.multiple_of(s * 32, 32), 32)
    for side in range(2):
        GX[side, 992:1024, own] = (GH[side, block_rows, :].astype(F32) * root_scale).astype(BF)
    share_grads(5)
    turned = [GH[side].T for side in range(2)]
    total = jnp.zeros((8, B), F32)
    for t in range(4):
        rows = slice(256 * t, 256 * (t + 1))
        part = None
        for side in range(2):
            term = nn(turned[side], WF[:, :, :, side, 32:64, rows].reshape(D, 256))
            part = term if part is None else part + term
        part = part.T
        PB[rows, :] = part
        total = total + fold(part * A5[rows, :].astype(F32))
    mean = column_sum(total) * (1.0 / D)
    shift = root_scale * root_scale * mean
    dl = jnp.zeros((8, B), F32)
    dr = jnp.zeros((8, B), F32)
    for t in range(8):
        rows = slice(128 * t, 128 * (t + 1))
        ul, ur = UF[0, rows, :], UF[1, rows, :]
        v = root_scale * (PB[rows, :] - (1.0 + ul) * (1.0 + ur) * shift)
        gl = (v * (1.0 + ur)).astype(BF)
        gr = (v * (1.0 + ul)).astype(BF)
        GH[0, rows, :] = gl
        GH[1, rows, :] = gr
        dl = dl + fold(gl.astype(F32) * ul)
        dr = dr + fold(gr.astype(F32) * ur)
    root_mean = jnp.where(mine == 1, column_sum(dr), column_sum(dl)) * (1.0 / D)
    part_rows = pl.ds(pl.multiple_of(lax.rem(block, 2) * 64, 64), 64)
    PB[0:64, :] = nn(W4[part_rows, :], GH[mine])
    for side in range(2):
        GX[side, 960:992, own] = (GH[side, block_rows, :].astype(F32) * scales[4][side]).astype(BF)
    share_grads(4)

    def gathered(level, rows):
        if level == LEVELS - 1:
            return PB[rows, :]
        group = BR[level].shape[0]
        total = BR[level][0, rows, :].astype(F32)
        for g in range(1, group):
            total = total + BR[level][g, rows, :].astype(F32)
        return total

    def await_chunks(level, copy):
        if level == LEVELS - 1:
            return root_mean
        copy.wait()
        await_bytes(BR[level].at[0 : BR[level].shape[0] - 1], br.at[level])
        size = CHUNK[level]
        return column_sum(gathered(level, slice(size, size + 16))) * (1.0 / D)

    own_chunk = None
    for level in reversed(range(LEVELS - 1)):
        group, w, col = GROUP[level], WIDTH[level], COLUMN[level]
        mean = await_chunks(level + 1, own_chunk)
        side_of = lax.rem(s // GROUP[level], 2)
        r = jnp.where(side_of == 1, scales[level + 1][1], scales[level + 1][0])
        left, right = scales[level]
        size = min(w, 64)

        def node_back(t, carry):
            dl, dr = carry
            rows = pl.ds(pl.multiple_of(col + t * size, size), size)
            total = gathered(level + 1, pl.ds(pl.multiple_of(t * size, size), size))
            ul, ur = UL[rows, :], UR[rows, :]
            v = r * (total - JJ[rows, :] * (r * mean))
            gl = v * (1.0 + ur)
            gr = v * (1.0 + ul)
            GX[0, rows, own] = (gl * left).astype(BF)
            GX[1, rows, own] = (gr * right).astype(BF)
            if level == 0:
                return carry
            gl = gl.astype(BF)
            gr = gr.astype(BF)
            if level < 3:
                near = pl.ds(pl.multiple_of(col - 512 + t * size, size), size)
                GB[0, near, :] = gl
                GB[1, near, :] = gr
            else:
                GP[level - 3, 0, col - 896 : col - 896 + w, :] = gl
                GP[level - 3, 1, col - 896 : col - 896 + w, :] = gr
            return dl + fold(gl.astype(F32) * ul), dr + fold(gr.astype(F32) * ur)

        zero = jnp.zeros((8, B), F32)
        dl, dr = lax.fori_loop(0, w // size, node_back, (zero, zero))
        if level == 0:
            share_last_grads()
            break
        share_grads(level)
        chunk = CHUNK[level]
        dots = [column_sum(dl), column_sum(dr)]

        def half_sums(side, parity):
            rows = pl.ds(pl.multiple_of(parity * 512, 512), 512)
            if level == 1:
                return nn(WN[side, rows, col : col + w], GB[side, col - 512 : col - 512 + w, :])
            if level == 2:
                return nn(WP[0, side, rows, :], GB[side, col - 512 : col - 512 + w, :])
            return nn(WP[level - 2, side, rows, :], GP[level - 3, side])

        for side in range(2):
            BO[level - 1, side, 0:512, :] = half_sums(side, 1 - c).astype(BF)
            BO[level - 1, side, 512:528, :] = split_tile(dots[side])
            to_sub(BO.at[level - 1, side], BI.at[level - 1, side], bos.at[level], bis.at[level], partner)
        for side in range(2):
            LB[side * 512 : (side + 1) * 512, 0:B] = half_sums(side, c)
        await_bytes(BI.at[level - 1], bis.at[level])
        quarter = group // 4
        for side in range(2):
            tile = split_tile(dots[side] + column_sum(BI[level - 1, side, 512:528, :].astype(F32)))
            chunks = slice(side * quarter, (side + 1) * quarter)
            value = (LB[side * 512 : (side + 1) * 512, 0:B] + BI[level - 1, side, 0:512, :].astype(F32)).astype(BF)
            BS[level][chunks, 0:chunk, :] = value.reshape(quarter, chunk, B)
            BS[level][chunks, chunk : chunk + 16, :] = jnp.broadcast_to(tile[None], (quarter, 16, B))
        own_chunk = scatter(level, lax.rem(s, group))
        for done in {3: (0, 1, 2), 2: (3, 4), 1: (5,)}[level]:
            pass_rows(done)

    await_bytes(MS.at[0:3], x2s)

    def partial_sums(blocks):
        for i in blocks:
            for side in {0: (), 1: (0,), 2: (1,), 3: (0, 1)}[i]:
                await_bytes(GX.at[side, 0:512, lanes_of(i)], gx0.at[i, side])
        lanes = slice(blocks[0] * B, (blocks[-1] + 1) * B)
        for t in range(4):
            rows = slice(256 * t, 256 * (t + 1))
            value = nn(WN[1 - c, rows, 0:512], GX[1 - c, 0:512, lanes]).astype(BF)
            for b, i in enumerate(blocks):
                MS[i, rows, :] = value[:, lanes_of(b)]
        for i in blocks:
            to_sub(MS.at[i], PR.at[i], pss, prs.at[i], partner)
        for t in range(4):
            rows = slice(256 * t, 256 * (t + 1))
            PM[rows, 0 : B * len(blocks)] = nn(WN[c, rows, 0:512], GX[c, 0:512, lanes])

    partial_sums((0,))

    await_bytes(LO.at[:, 0 : 3 * B], x3r)
    for i in range(REPS):
        R0[:, lanes_of(i)] = jnp.broadcast_to(factor_of(squares_of(H0, 0, lanes_of(i))), (8, B))

    def middle_back(blocks):
        for i in blocks:
            await_bytes(PR.at[i], prs.at[i])
        for b, i in enumerate(blocks):
            part = lanes_of(b)
            total = jnp.zeros((8, B), F32)
            for t in range(8):
                rows = slice(128 * t, 128 * (t + 1))
                value = PM[rows, part] + PR[i, rows, :].astype(F32)
                PM[rows, part] = value
                total = total + fold(value * H0[rows, lanes_of(i)].astype(F32))
            scale0 = R0[0:1, lanes_of(i)]
            shift = scale0 * scale0 * (column_sum(total) * (1.0 / D))
            for t in range(8):
                rows = slice(128 * t, 128 * (t + 1))
                v = PM[rows, part] - H0[rows, lanes_of(i)].astype(F32) * shift
                CR[rows, lanes_of(i)] = (v * LO[rows, lanes_of(i)].astype(F32)).astype(BF)

    def leaf_back(blocks):
        lanes = slice(blocks[0] * B, (blocks[-1] + 1) * B)
        n = B * len(blocks)
        total = jnp.zeros((8, n), F32)
        for t in range(4):
            rows = slice(256 * t, 256 * (t + 1))
            value = nn(MW[rows, :], CR[:, lanes])
            LB[rows, 0:n] = value
            total = total + fold(value * LM[rows, lanes].astype(F32))
        mean = column_sum(total) * (1.0 / D)
        r = RL[0:1, lanes]
        for t in range(16):
            rows = slice(64 * t, 64 * (t + 1))
            v = r * (LB[rows, 0:n] - LM[rows, lanes].astype(F32) * mean)
            rest = others([FK[k, rows, lanes].astype(F32) for k in range(4)])
            for k in range(4):
                WT[k, rows, lanes] = (v * rest[k]).astype(BF)

    def await_grads(level):
        w, col = WIDTH[level], COLUMN[level]
        await_bytes(GX.at[:, col : col + w, 0 : 3 * B], gxr.at[level])

    middle_back((0,))
    leaf_back((0,))
    relay_last_grads()

    for copy in kept:
        copy.wait()
    for level in range(LEVELS + 1):
        await_bytes(passed(level), apr.at[level])
    for level in (5, 4, 3):
        await_grads(level)
    lane = lax.broadcasted_iota(jnp.int32, (256, 128), 1)
    for side in range(2):
        grads = GX[side, 896:1024, :]
        g3 = nt(AX[3, side], grads)
        g4 = nt(AX[4, side], grads)
        g5 = nt(AX[5, 0], grads)
        OU[side, :, 896:1024] = jnp.where(lane < 64, g3, jnp.where(lane < 96, g4, g5)).astype(BF)

    def upper_gradient(level):
        await_grads(level)
        w, col = WIDTH[level], COLUMN[level]
        for side in range(2):
            OU[side, :, col : col + w] = nt(AX[level, side], GX[side, col : col + w, :]).astype(BF)

    upper_gradient(2)
    upper_gradient(1)

    partial_sums((1, 2))
    middle_back((1, 2))
    partial_sums((3,))
    leaf_back((1, 2))

    rows = at(p, 256)
    OU[c, :, 0:512] = nt(H0[rows, :], GX[c, 0:512, :]).astype(BF)
    OU[1 - c, :, 0:512] = nt(AX[0, 1 - c], GX[1 - c, 0:512, :]).astype(BF)

    middle_back((3,))
    leaf_back((3,))

    await_bytes(XS.at[0:3], x1s)
    await_bytes(CS.at[0:3], x3s)
    await_bytes(H0.at[:, 0 : 3 * B], h0s)
    await_bytes(MS, pss)
    for level in range(1, LEVELS - 1):
        await_bytes(BO.at[level - 1], bos.at[level])
    await_bytes(CF.at[0:3, 0, 0], cfs.at[0])
    await_bytes(CF.at[0:3, :, 0], cfs.at[1])
    await_bytes(CF.at[:, :, 0], cfs.at[2])
    await_bytes(WF.at[0:3, 0, 0], w1s)
    await_bytes(WF.at[:, :, 0, 0], w2s)
    await_bytes(WF.at[0:2, :, 0, 0], w3s)
    await_bytes(WF.at[:, :, 0], w4s)
    for level in range(LEVELS + 1):
        if level < LEVELS:
            half = GROUP[level] // 2
            block = A[level].shape[0] // GROUP[level]
            await_bytes(A[level].at[0 : half * block], fs.at[level])
            if half > 1:
                await_bytes(A[level].at[0 : (half - 1) * block], ff.at[level])
        if 0 < level < LEVELS - 1:
            await_bytes(BS[level].at[0 : BS[level].shape[0] - 1], bs.at[level])
        if level:
            await_bytes(passed(level), axs.at[level])
            w, col = WIDTH[level], COLUMN[level]
            await_bytes(GX.at[:, col : col + w, 0 : 3 * B], gxs.at[level])
        await_bytes(passed(level), aps.at[level])
    await_bytes(GX.at[:, 0:512, 0 : 2 * B], gxs.at[0])
    await_bytes(GX.at[:, 0:512, own], gxt)


def scratch():
    vm = pltpu.VMEM
    dma = pltpu.SemaphoreType.DMA
    chunks = [vm((GROUP[j] // 2, CHUNK[j] + 16, B), BF) for j in range(1, LEVELS - 1)]
    return (
        [
            vm((2048, F), BF), vm((256, 256), BF), vm((4, 4, B, F), BF), vm((4, ALL, F), BF),
            vm((4, F, D), BF), vm((4, D, F), BF), vm((D, D), BF), vm((D, D), BF),
            vm((4, 128, 2, D), BF), vm((2, D, D), BF), vm((4, 4, 2, 32, B), F32),
            vm((4, D, ALL), BF), vm((8, ALL), F32),
            vm((4, D, B), BF), vm((4, D, B), BF),
        ]
        + [vm((2 * D, B), BF)] * 5
        + [vm((D, B), BF)]
        + [vm((D, B), F32)] * 3
        + [vm((1, 2, 128, B), BF), vm((2, 384, B), BF), vm((2, 2, D, 128), BF)]
        + [vm((3, 2, 528, B), BF)] * 2
        + chunks
        + chunks
        + [
            vm((2, D, ALL), BF), vm((6, 2, 256, ALL), BF), vm((4, D, B), BF),
            vm((D, 2 * B), F32),
            vm((D, ALL), BF), vm((D, ALL), BF), vm((8, ALL), F32),
            vm((4, D, B), BF), vm((D, 2 * B), F32),
            vm((4, 4, 2, 2, 64, D), BF), vm((128, D), BF), vm((2, D, B), F32), vm((2, D, B), BF), vm((D, B), F32),
        ]
        + [
            dma((8,)), dma((22,)), dma, dma((4,)), dma, dma, dma, dma, dma, dma,
            dma((6,)), dma((6, 16)), dma((6,)), dma((6,)), dma((6,)), dma((6,)), dma((6,)), dma((6,)),
            dma((6,)), dma((6,)), dma((6,)), dma((6,)), dma((6,)), dma((6,)), dma((4, 2)), dma, dma, dma((4,)),
            dma((3,)), dma((3,)), dma, dma((2,)), dma, dma((2, 2)), dma, dma((2, 2)), dma, dma,
        ]
    )


def gradients(CT, LM, CR, XT, OU, lg_hbm, mg_hbm, ug_hbm, LW, OM, OI, sem):
    copies = []

    def out(src, dst):
        copies.append(pltpu.make_async_copy(src, dst, sem.at[len(copies)]))
        copies[-1].start()

    for k in range(4):
        rows = slice(64 * k, 64 * (k + 1))
        for side in range(2):
            OI[rows, side, :] = OU[side, rows, :]
        LW[k] = nt(XT[k], CT[k]).astype(BF)
        out(LW.at[k], lg_hbm.at[k])
    out(OI, ug_hbm)
    for t in range(4):
        rows = slice(256 * t, 256 * (t + 1))
        OM[rows, :] = nt(LM[rows, :], CR[...]).astype(BF)
        out(OM.at[rows], mg_hbm.at[rows])
    for copy in copies:
        copy.wait()


def on_device(regions, leaf_map, leaf_bond_weight, mid_weight, upper_weight, head_cotangent):
    anywhere = pl.BlockSpec(memory_space=pl.ANY)
    local = pl.BlockSpec(memory_space=pltpu.VMEM)
    kept = pl.pallas_call(
        kernel,
        out_shape=(
            pltpu.VMEM((4, D, ALL), BF),
            pltpu.VMEM((D, ALL), BF),
            pltpu.VMEM((D, ALL), BF),
            pltpu.VMEM((4, F, ALL), BF),
            pltpu.VMEM((2, 256, D), BF),
        ),
        in_specs=[pl.BlockSpec(memory_space=pltpu.SMEM)] + [anywhere] * 5,
        out_specs=(local,) * 5,
        scratch_shapes=scratch(),
        compiler_params=pltpu.CompilerParams(
            collective_id=0, has_side_effects=True, vmem_limit_bytes=VMEM_LIMIT
        ),
    )(
        leaf_map, regions.reshape(B * 16, F), leaf_bond_weight[0], mid_weight[0, 0],
        upper_weight[0], head_cotangent.T,
    )
    kept = [pltpu.with_memory_space_constraint(array, pltpu.VMEM) for array in kept]
    outs = pl.pallas_call(
        gradients,
        out_shape=(
            jax.ShapeDtypeStruct((4, F, D), BF),
            jax.ShapeDtypeStruct((D, D), BF),
            jax.ShapeDtypeStruct((256, 2, D), BF),
        ),
        in_specs=[local] * 5,
        out_specs=(anywhere,) * 3,
        scratch_shapes=[
            pltpu.VMEM((4, F, D), BF), pltpu.VMEM((D, D), BF), pltpu.VMEM((256, 2, D), BF),
            pltpu.SemaphoreType.DMA((9,)),
        ],
        compiler_params=pltpu.CompilerParams(vmem_limit_bytes=32000000),
    )(*kept)
    return (outs[0][None], outs[1][None, None], outs[2][None])


def solution(mesh):
    placed = (
        P("rep", "sub", None),
        P("sub"),
        P(("sub", "rep"), None, None, None),
        P("sub", "rep", None, None),
        P("sub", None, None, None),
        P("rep", "sub"),
    )
    return jax.shard_map(
        on_device,
        mesh=mesh,
        in_specs=placed,
        out_specs=(
            P(("sub", "rep"), None, None, None),
            P("sub", "rep", None, None),
            P("sub", "rep", None, None),
        ),
        check_vma=False,
    )
```
